32 devices in a mesh: vocab: 8 (over y, x, core), blk: 4 (over z).
Axes of the slice: x: 2, y: 2, z: 4, core: 2. Of those that a mesh axis runs over, the one named last changes fastest.
Arguments:
- char_ids: int32 [16384, 50], P(('vocab', 'blk')), may hold values from 0 to 255, as said below
- char_table: bfloat16 [256, 16], replicated, may hold values from -5 to 5
- conv_weight: bfloat16 [112, 896], replicated, may hold values from -0.75 to 0.75
- proj_weight: bfloat16 [896, 1024], replicated, may hold values from -0.1875 to 0.1875
- gate_weight: bfloat16 [2, 1024, 1024], replicated, may hold values from -0.1875 to 0.1875
- trans_weight: bfloat16 [2, 1024, 1024], replicated, may hold values from -0.1875 to 0.1875
- gate_bias: float32 [2, 1024], replicated, may hold values from -4 to 4
- hidden: bfloat16 [2048, 1024], P(('vocab', 'blk')), may hold values from -48 to 48
- targets: int32 [2048], P(('vocab', 'blk')), may hold values from 0 to 16383
Outputs:
- row_loss: float32 [2048], P(('vocab', 'blk'))
- hidden_grad: bfloat16 [2048, 1024], P(('vocab', 'blk'))
The draws below stay inside these ranges and needn't reach their ends.
Inputs may be any that keep to these rules, and one draw needn't show every extreme that they name: `char_ids`: each word has 2 to 50 characters with ids 1 and up, followed by the padding id 0.
All inputs are finite; a program needn't handle non-finite values.
Results may differ from the reference program's by a relative error of at most 0.014.
The reference program's roundings to bfloat16 on the way count: a program that leaves them out, or rounds other values in their place, can miss the bound.
Values may be sent and summed in bfloat16 or wider, within the bound.
No kernel may reach another device: no remote copies, remote signals or barrier semaphores. Data moves between devices by JAX's collectives and lax.ppermute only.
A program may use at most 128 MiB of HBM per device.

```python
import math
import jax
import jax.numpy as jnp
import numpy as np
from jax import lax

D = 1024
CE = 16
FW = 128
CHARS = 256
LEN = 50
NW = 7
LAYERS = 2
VOCAB = 16384
ROWS = 2048


def draw_char_ids(key, part):
    key_len, key_val = jax.random.split(key)
    lengths = jax.random.randint(key_len, (VOCAB, 1), 2, LEN + 1)
    values = jax.random.randint(key_val, (VOCAB, LEN), 1, CHARS)
    position = jnp.arange(LEN)[None, :]
    return jnp.where(position < lengths, values, 0).astype(jnp.int32)


def draw_hidden(key, part):
    key_a = jax.random.fold_in(key, 0)
    return (jax.random.truncated_normal(key_a, -4.0, 4.0, (ROWS, D), jnp.float32) * 0.2).astype(jnp.bfloat16)


def set_ends(result, own_key, least, top_value):
    spot = [jax.random.randint(jax.random.fold_in(own_key, axis), (), 0, length) for axis, length in enumerate(result.shape)]
    main_axis = result.shape.index(max(result.shape))
    beside = spot[:main_axis] + [(spot[main_axis] + 1) % result.shape[main_axis]] + spot[main_axis + 1:]
    return result.at[tuple(spot)].set(least).at[tuple(beside)].set(top_value)


def rank_bounds(amount, skew):
    loads = [(1 << 20) // math.isqrt(grade ** skew) + 1 for grade in range(1, amount + 1)]
    deviation = 1 + sum(loads) // (1 << 30)
    return np.cumsum(np.array([max(1, weight // deviation) for weight in loads]))


def ranked(stream_key, dims, number_of, lean):
    table = rank_bounds(number_of, lean)
    ticket = jax.random.randint(jax.random.fold_in(stream_key, 1), dims, 0, int(table[number_of - 1]))
    grade = jnp.searchsorted(jnp.asarray(table, jnp.int32), ticket, side="right")
    return jax.random.permutation(jax.random.fold_in(stream_key, 2), number_of)[grade].astype(jnp.int32)


def bell_draw(rng, shape, width, reach, kind=jnp.bfloat16):
    return jnp.clip(width * jax.random.normal(rng, shape, jnp.float32), -reach, reach).astype(kind)


def setup_inputs(seed: int = 0) -> dict:
    splits = jax.random.split(jax.random.key(seed), 10)
    char_ids = draw_char_ids(jax.random.fold_in(splits[9], 71), 0)
    char_table = bell_draw(splits[1], (CHARS, CE), 1.0, 5.0)
    conv_weight = bell_draw(splits[2], (NW * CE, NW * FW), (4 * CE) ** -0.5, 0.75)
    proj_weight = bell_draw(splits[3], (NW * FW, D), (NW * FW) ** -0.5, 0.1875)
    gate_weight = bell_draw(splits[4], (LAYERS, D, D), D ** -0.5, 0.1875)
    trans_weight = bell_draw(splits[5], (LAYERS, D, D), D ** -0.5, 0.1875)
    gate_bias = bell_draw(splits[6], (LAYERS, D), 1.0, 4.0, jnp.float32)
    hidden = draw_hidden(jax.random.fold_in(splits[9], 71), 0)
    targets = set_ends(ranked(splits[8], (ROWS,), VOCAB, 2), jax.random.fold_in(splits[8], 3), 0, VOCAB - 1).astype(jnp.int32)
    return {"char_ids": char_ids, "char_table": char_table, "conv_weight": conv_weight, "proj_weight": proj_weight, "gate_weight": gate_weight, "trans_weight": trans_weight, "gate_bias": gate_bias, "hidden": hidden, "targets": targets}


def char_features(char_ids, char_table, conv_weight):
    num_words = char_ids.shape[0]
    length = char_ids.shape[1]
    symbols = char_table.shape[0]
    embed_dim = char_table.shape[1]
    widths = conv_weight.shape[0] // embed_dim
    filters = conv_weight.shape[1] // widths
    onehot = (char_ids[:, :, None] == jnp.arange(symbols, dtype=jnp.int32)[None, None, :]).astype(jnp.bfloat16)
    vectors = jnp.dot(onehot.reshape(num_words * length, symbols), char_table, preferred_element_type=jnp.float32)
    vectors = vectors.astype(jnp.bfloat16).reshape(num_words, length, embed_dim)
    padded = jnp.pad(vectors, ((0, 0), (0, widths - 1), (0, 0)))
    windows = jnp.concatenate([padded[:, shift_at:shift_at + length, :] for shift_at in range(widths)], axis=2)
    offset = jnp.arange(widths * embed_dim) // embed_dim
    kernel = jnp.arange(widths * filters) // filters + 1
    masked = jnp.where(offset[:, None] < kernel[None, :], conv_weight, jnp.zeros_like(conv_weight))
    conv_out = jnp.dot(windows.reshape(num_words * length, widths * embed_dim), masked, preferred_element_type=jnp.float32)
    conv_out = conv_out.reshape(num_words, length, widths * filters)
    position = jnp.arange(length)
    usable = position[:, None] <= length - kernel[None, :]
    pooled = jnp.max(jnp.where(usable[None, :, :], conv_out, -jnp.inf), axis=1)
    return jnp.tanh(pooled).astype(jnp.bfloat16)


def embed_words(char_ids, char_table, conv_weight, proj_weight, gate_weight, trans_weight, gate_bias):
    features = char_features(char_ids, char_table, conv_weight)
    current = jnp.dot(features, proj_weight, preferred_element_type=jnp.float32).astype(jnp.bfloat16)
    for layer_idx in range(gate_weight.shape[0]):
        opened = jax.nn.sigmoid(jnp.dot(current, gate_weight[layer_idx], preferred_element_type=jnp.float32) + gate_bias[layer_idx])
        carried = jax.nn.relu(jnp.dot(current, trans_weight[layer_idx], preferred_element_type=jnp.float32))
        current = (opened * carried + (1.0 - opened) * current.astype(jnp.float32)).astype(jnp.bfloat16)
    return current


def embed_all(char_ids, char_table, conv_weight, proj_weight, gate_weight, trans_weight, gate_bias):
    num_total = char_ids.shape[0]
    block_size = math.gcd(num_total, 128)
    grouped = char_ids.reshape(num_total // block_size, block_size, char_ids.shape[1])

    def one_block(piece_ids):
        return embed_words(piece_ids, char_table, conv_weight, proj_weight, gate_weight, trans_weight, gate_bias)

    return lax.map(one_block, grouped).reshape(num_total, proj_weight.shape[1])


def fold_panel(acc_state, row_block, row_spot, word_panel):
    run_max, run_total, weighted, target_vec = acc_state
    scores = jnp.dot(row_block, word_panel.T, preferred_element_type=jnp.float32)
    new_max = jnp.maximum(run_max, jnp.max(scores, axis=1))
    rescale = jnp.exp(run_max - new_max)
    soft_weights = jnp.exp(scores - new_max[:, None]).astype(jnp.bfloat16)
    run_total = run_total * rescale + jnp.sum(soft_weights.astype(jnp.float32), axis=1)
    weighted = weighted * rescale[:, None] + jnp.dot(soft_weights, word_panel, preferred_element_type=jnp.float32)
    count_words = word_panel.shape[0]
    inside = (row_spot >= 0) & (row_spot < count_words)
    picked = jnp.take(word_panel, jnp.clip(row_spot, 0, count_words - 1).astype(jnp.int32), axis=0).astype(jnp.float32)
    target_vec = target_vec + jnp.where(inside[:, None], picked, jnp.zeros_like(picked))
    return (new_max, run_total, weighted, target_vec)


def reference(char_ids, char_table, conv_weight, proj_weight, gate_weight, trans_weight, gate_bias, hidden, targets):
    num_total = char_ids.shape[0]
    block_size = math.gcd(num_total, 4096)
    grouped = char_ids.reshape(num_total // block_size, block_size, LEN)
    starts = (jnp.arange(num_total // block_size, dtype=jnp.int32) * block_size).astype(jnp.int32)
    row_count = hidden.shape[0]
    model_dim = hidden.shape[1]
    initial = (jnp.full((row_count,), -jnp.inf, jnp.float32), jnp.zeros((row_count,), jnp.float32),
               jnp.zeros((row_count, model_dim), jnp.float32), jnp.zeros((row_count, model_dim), jnp.float32))

    def scan_step(acc_state, inputs):
        piece_ids, piece_start = inputs
        word_panel = embed_all(piece_ids, char_table, conv_weight, proj_weight, gate_weight, trans_weight, gate_bias)
        row_spot = (targets - piece_start).astype(jnp.int32)
        return fold_panel(acc_state, hidden, row_spot, word_panel), None

    final_state, _ = lax.scan(scan_step, initial, (grouped, starts))
    run_max, run_total, weighted, target_vec = final_state
    target_score = jnp.sum(hidden.astype(jnp.float32) * target_vec, axis=1)
    row_loss = run_max + jnp.log(run_total) - target_score
    hidden_grad = (weighted / run_total[:, None] - target_vec).astype(jnp.bfloat16)
    return (row_loss, hidden_grad)
```

```python
import functools
import jax
import jax.numpy as jnp
from jax import lax
from jax.experimental import pallas as pl
from jax.experimental.pallas import tpu as pltpu
from jax.sharding import PartitionSpec as P

bf16=jnp.bfloat16; f32=jnp.float32
LANES=128; SPAN=8

def prep_toeplitz(conv_ref, toep, ce, widths, filters):
    depth = toep.shape[0]
    for k in range(widths):
        rows = (k + 1) * ce
        piece = conv_ref[0:rows, k * filters:(k + 1) * filters]
        for o in range(SPAN):
            cols = slice((k * SPAN + o) * filters, (k * SPAN + o + 1) * filters)
            if o:
                toep[0:o * ce, cols] = jnp.zeros((o * ce, filters), bf16)
            toep[o * ce:o * ce + rows, cols] = piece
            rest = depth - o * ce - rows
            if rest:
                toep[o * ce + rows:depth, cols] = jnp.zeros((rest, filters), bf16)

def lookup(ids_ref, tab_ref, vec, words, length, ce):
    per = LANES // ce
    for t in range(words // LANES):
        for g in range(vec.shape[1] // LANES):
            parts = []
            for q in range(per):
                p = g * per + q
                if p >= length:
                    parts.append(jnp.zeros((ce, LANES), f32)); continue
                idx = jnp.broadcast_to(ids_ref[p:p + 1, t * LANES:(t + 1) * LANES], (8, LANES))
                low = jnp.bitwise_and(idx, LANES - 1)
                top = idx >= LANES
                for h in range(ce // 8):
                    a = jnp.take_along_axis(tab_ref[h * 8:h * 8 + 8, 0:LANES], low, axis=1)
                    b = jnp.take_along_axis(tab_ref[h * 8:h * 8 + 8, LANES:2 * LANES], low, axis=1)
                    parts.append(jnp.where(top, b, a))
            block = jnp.concatenate(parts, axis=0)
            vec[t * LANES:(t + 1) * LANES, g * LANES:(g + 1) * LANES] = block.T.astype(bf16)

def conv_pool(vec, toep, acc, length, widths, filters):
    words = vec.shape[0]
    def tile(b, k, o, lhs):
        cols = slice((k * SPAN + o) * filters, (k * SPAN + o + 2) * filters)
        return jnp.dot(lhs, toep[:, cols], preferred_element_type=f32)
    acc[...] = jnp.full(acc.shape, -jnp.inf, f32)
    least = (length - widths + 1) // SPAN
    def body(b, _):
        lhs = vec[:, pl.ds(pl.multiple_of(b * LANES, LANES), 2 * LANES)]
        for k in range(widths):
            best = acc[:, k * filters:(k + 1) * filters]
            for o in range(0, SPAN, 2):
                r = tile(b, k, o, lhs)
                best = jnp.maximum(best, jnp.maximum(r[:, :filters], r[:, filters:]))
            acc[:, k * filters:(k + 1) * filters] = best
        return 0
    lax.fori_loop(0, least, body, 0)
    for b in range(least, -(-length // SPAN)):
        lhs = vec[:, b * LANES:(b + 2) * LANES]
        for k in range(widths):
            usable = min(SPAN, length - k - b * SPAN)
            if usable <= 0: continue
            best = acc[:, k * filters:(k + 1) * filters]
            for o in range(0, usable, 2):
                r = tile(b, k, o, lhs)
                best = jnp.maximum(best, r[:, :filters])
                if o + 1 < usable:
                    best = jnp.maximum(best, r[:, filters:])
            acc[:, k * filters:(k + 1) * filters] = best

def cnn_kernel(ids_ref, tab_ref, conv_ref, bias_ref, proj_hbm, gate_hbm, trans_hbm, *rest,
               widths, filters, ce, length, layers, nt, outs):
    out_refs, scratch = rest[:outs], rest[outs:]
    vec, toep, acc, feat, proj, gate, trans, state, last, sems = scratch
    copies = [pltpu.make_async_copy(s, d, sems.at[i]) for i, (s, d) in enumerate(
        ((proj_hbm, proj), (gate_hbm, gate), (trans_hbm, trans)))]
    for c in copies:
        c.start()
    words = ids_ref.shape[1]
    prep_toeplitz(conv_ref, toep, ce, widths, filters)
    lookup(ids_ref, tab_ref, vec, words, length, ce)
    conv_pool(vec, toep, acc, length, widths, filters)
    for c in copies:
        c.wait()
    feat[...] = jnp.tanh(acc[...]).astype(bf16)
    model = last.shape[1]
    for n in range(0, model, nt):
        state[:, n:n + nt] = jnp.dot(feat[...], proj[:, n:n + nt], preferred_element_type=f32).astype(bf16)
    for l in range(layers):
        for n in range(0, model, nt):
            cur = state[...]
            g = jnp.dot(cur, gate[l, :, n:n + nt], preferred_element_type=f32) + bias_ref[l:l + 1, n:n + nt]
            t = jnp.dot(cur, trans[l, :, n:n + nt], preferred_element_type=f32)
            opened = jax.nn.sigmoid(g)
            carried = jnp.maximum(t, 0.0)
            new = (opened * carried + (1.0 - opened) * state[:, n:n + nt].astype(f32)).astype(bf16)
            if l + 1 < layers:
                last[:, n:n + nt] = new
            else:
                at = 0
                for ref in out_refs:
                    ref[:, n:n + nt] = new[at:at + ref.shape[0], :]
                    at += ref.shape[0]
        if l + 1 < layers:
            state[...] = last[...]


ANY = pl.BlockSpec(memory_space=pl.ANY)
VM = pl.BlockSpec(memory_space=pltpu.VMEM)


def params(limit_mib=56):
    return pltpu.CompilerParams(vmem_limit_bytes=limit_mib << 20)


def embed(ids_t, sizes, tab_t, conv_weight, proj_weight, gate_weight, trans_weight, gate_bias, nt=256):
    length, words = ids_t.shape
    ce = tab_t.shape[0]
    widths = conv_weight.shape[0] // ce
    filters = conv_weight.shape[1] // widths
    layers, model, _ = gate_weight.shape
    flops = 2 * words * (length * 256 * widths * filters + widths * filters * model + 2 * layers * model * model)
    return pl.pallas_call(
        functools.partial(cnn_kernel, widths=widths, filters=filters, ce=ce, length=length, layers=layers, nt=nt,
                          outs=len(sizes)),
        out_shape=[jax.ShapeDtypeStruct((s, model), bf16) for s in sizes],
        in_specs=[VM, VM, VM, VM, ANY, ANY, ANY],
        out_specs=[VM] * len(sizes),
        scratch_shapes=[
            pltpu.VMEM((words, (-(-length // SPAN) + 1) * LANES), bf16),
            pltpu.VMEM((2 * LANES, widths * SPAN * filters), bf16),
            pltpu.VMEM((words, widths * filters), f32),
            pltpu.VMEM((words, widths * filters), bf16),
            pltpu.VMEM(proj_weight.shape, bf16),
            pltpu.VMEM(gate_weight.shape, bf16),
            pltpu.VMEM(trans_weight.shape, bf16),
            pltpu.VMEM((words, model), bf16),
            pltpu.VMEM((words, model), bf16),
            pltpu.SemaphoreType.DMA((3,)),
        ],
        compiler_params=params(),
        cost_estimate=pl.CostEstimate(flops=flops, bytes_accessed=12 << 20, transcendentals=words * 4096),
        name="embed",
    )(ids_t, tab_t, conv_weight, gate_bias, proj_weight, gate_weight, trans_weight)


def pick_kernel(spot_ref, ids_ref, out_ref):
    words = ids_ref.shape[1]
    rows = spot_ref.shape[1]
    at = lax.broadcasted_iota(jnp.int32, (words, rows), 0)
    hot = jnp.where(at == spot_ref[...], 1.0, 0.0).astype(bf16)
    out_ref[...] = jnp.dot(ids_ref[...], hot, preferred_element_type=f32).astype(bf16)


def pick(spot, ids):
    return pl.pallas_call(
        pick_kernel,
        out_shape=jax.ShapeDtypeStruct((ids.shape[0], spot.shape[1]), bf16),
        in_specs=[VM, VM], out_specs=VM, compiler_params=params(),
        cost_estimate=pl.CostEstimate(flops=2 * 256 * ids.shape[1] * spot.shape[1], bytes_accessed=1 << 20,
                                      transcendentals=0),
        name="pick",
    )(spot, ids)


def by_row(line, i):
    return jnp.broadcast_to(line[i:i + 1, :], (LANES, LANES)).T


def as_line(column):
    return jnp.broadcast_to(column, (LANES, LANES)).T[0:1, :]


def part_of_softmax(rows_ref, words, score, prob, out):
    at = 0
    top = None
    for ref in words:
        n = ref.shape[0]
        piece = lax.dot_general(rows_ref[...], ref[...], (((1,), (1,)), ((), ())), preferred_element_type=f32)
        score[:, at:at + n] = piece
        best = jnp.max(piece, axis=1, keepdims=True)
        top = best if top is None else jnp.maximum(top, best)
        at += n
    at = 0
    total = None
    for ref in words:
        n = ref.shape[0]
        w = jnp.exp(score[:, at:at + n] - top).astype(bf16)
        prob[:, at:at + n] = w
        s = jnp.sum(w.astype(f32), axis=1, keepdims=True)
        total = s if total is None else total + s
        at += n
    model = out.shape[1]
    for n in range(0, model, 256):
        at = 0
        res = None
        for ref in words:
            size = ref.shape[0]
            d = jnp.dot(prob[:, at:at + size], ref[:, n:n + 256], preferred_element_type=f32)
            res = d if res is None else res + d
            at += size
        out[:, n:n + 256] = res
    return top, total


def first_kernel(*refs, nh, nw):
    hid, words = refs[:nh], refs[nh:nh + nw]
    out, top_ref, total_ref, rows, score, prob = refs[nh + nw:]
    at = 0
    for h in hid:
        rows[at:at + h.shape[0], :] = h[...]
        at += h.shape[0]
    top, total = part_of_softmax(rows, words, score, prob, out)
    top_ref[...] = jnp.broadcast_to(top, top_ref.shape)
    total_ref[...] = jnp.broadcast_to(total, total_ref.shape)


def fold_cost(rows, words, model):
    return pl.CostEstimate(flops=4 * rows * words * model, bytes_accessed=2 * (rows + words) * model,
                           transcendentals=rows * words)


def first_fold(hid, words):
    model = hid[0].shape[1]
    rows = sum(h.shape[0] for h in hid)
    count = sum(w.shape[0] for w in words)
    return pl.pallas_call(
        functools.partial(first_kernel, nh=len(hid), nw=len(words)),
        out_shape=[jax.ShapeDtypeStruct((rows, model), f32), jax.ShapeDtypeStruct((rows, LANES), f32),
                   jax.ShapeDtypeStruct((rows, LANES), f32)],
        in_specs=[VM] * (len(hid) + len(words)), out_specs=[VM] * 3,
        scratch_shapes=[pltpu.VMEM((rows, model), bf16), pltpu.VMEM((rows, count), f32),
                        pltpu.VMEM((rows, count), bf16)],
        compiler_params=params(), cost_estimate=fold_cost(rows, count, model), name="first_fold",
    )(*hid, *words)


def second_kernel(*refs, nh, nw):
    hid, words = refs[:nh], refs[nh:nh + nw]
    old, top_ref, total_ref, a_keep, a_send, b_keep, b_send, lse, rows, score, prob, new = refs[nh + nw:]
    at = 0
    for h in hid:
        rows[at:at + h.shape[0], :] = h[...]
        at += h.shape[0]
    top2, total2 = part_of_softmax(rows, words, score, prob, new)
    top1, total1 = top_ref[:, 0:1], total_ref[:, 0:1]
    top = jnp.maximum(top1, top2)
    s1, s2 = jnp.exp(top1 - top), jnp.exp(top2 - top)
    total = s1 * total1 + s2 * total2
    s1, s2 = s1 / total, s2 / total
    whole = top + jnp.log(total)
    count, model = new.shape
    half, quarter = model // 2, count // 4
    for i in range(count // LANES):
        part = slice(i * LANES, (i + 1) * LANES)
        lse[i:i + 1, :] = as_line(whole[part, :])
    for q in range(4):
        part = slice(q * quarter, (q + 1) * quarter)
        mix = s1[part, :] * old[part, :] + s2[part, :] * new[part, :]
        mix = mix.astype(bf16)
        a = a_keep if q < 2 else a_send
        a[(q % 2) * quarter:(q % 2 + 1) * quarter, :] = mix[:, :half]
        b = b_keep if q % 2 == 0 else b_send
        b[(q // 2) * quarter:(q // 2 + 1) * quarter, :] = mix[:, half:]


def second_fold(hid, words, state):
    model = hid[0].shape[1]
    rows = sum(h.shape[0] for h in hid)
    count = sum(w.shape[0] for w in words)
    side = jax.ShapeDtypeStruct((rows // 2, model // 2), bf16)
    return pl.pallas_call(
        functools.partial(second_kernel, nh=len(hid), nw=len(words)),
        out_shape=[side] * 4 + [jax.ShapeDtypeStruct((rows // LANES, LANES), f32)],
        in_specs=[VM] * (len(hid) + len(words) + 3), out_specs=[VM] * 5,
        scratch_shapes=[pltpu.VMEM((rows, model), bf16), pltpu.VMEM((rows, count), f32),
                        pltpu.VMEM((rows, count), bf16), pltpu.VMEM((rows, model), f32)],
        compiler_params=params(), cost_estimate=fold_cost(rows, count, model), name="second_fold",
    )(*hid, *words, *state)


def join(one, two):
    top = jnp.maximum(one, two)
    s1, s2 = jnp.exp(one - top), jnp.exp(two - top)
    total = s1 + s2
    return s1 / total, s2 / total, top + jnp.log(total)


def mix_rows(mine, other, s1, s2):
    parts = []
    for n in range(0, mine.shape[1], LANES):
        parts.append(s1 * mine[:, n:n + LANES].astype(f32) + s2 * other[:, n:n + LANES].astype(f32))
    return jnp.concatenate(parts, axis=1)


def merge_one_kernel(a_keep, a_got, b_keep, b_got, lse, a_lse, b_lse,
                     a_keep2, a_send2, b_keep2, b_send2, a_line, b_line):
    lines = lse.shape[0]
    per = lines // 4
    for keep, got, got_lse, outs, line, mine_q, their_q in (
            (a_keep, a_got, a_lse, (a_keep2, a_send2), a_line, (0, 1), (2, 3)),
            (b_keep, b_got, b_lse, (b_keep2, b_send2), b_line, (0, 2), (1, 3))):
        for j in range(2):
            for i in range(per):
                mi, ti = mine_q[j] * per + i, their_q[j] * per + i
                w1, w2, _ = join(by_row(lse, mi), by_row(got_lse, ti))
                row = slice((j * per + i) * LANES, (j * per + i + 1) * LANES)
                outs[j][i * LANES:(i + 1) * LANES, :] = mix_rows(keep[row, :], got[row, :], w1, w2).astype(bf16)
                line[j * per + i:j * per + i + 1, :] = join(lse[mi:mi + 1, :], got_lse[ti:ti + 1, :])[2]


def merge_one(a_keep, a_got, b_keep, b_got, lse, a_lse, b_lse):
    rows, half = a_keep.shape
    side = jax.ShapeDtypeStruct((rows // 2, half), bf16)
    line = jax.ShapeDtypeStruct((lse.shape[0] // 2, LANES), f32)
    return pl.pallas_call(
        merge_one_kernel, out_shape=[side] * 4 + [line] * 2,
        in_specs=[VM] * 7, out_specs=[VM] * 6, compiler_params=params(),
        cost_estimate=pl.CostEstimate(flops=4 * rows * half, bytes_accessed=12 * rows * half, transcendentals=0),
        name="merge_one",
    )(a_keep, a_got, b_keep, b_got, lse, a_lse, b_lse)


def merge_two_kernel(a_keep, a_got, b_keep, b_got, a_line, b_line, a_lse, b_lse, keep2, send2, lines):
    per = a_line.shape[0] // 2
    rows, half = a_keep.shape
    for c, (keep, got, line, got_line) in enumerate(
            ((a_keep, a_got, a_line, a_lse), (b_keep, b_got, b_line, b_lse))):
        for i in range(per):
            w1, w2, _ = join(by_row(line, i), by_row(got_line, per + i))
            row = slice(i * LANES, (i + 1) * LANES)
            out = mix_rows(keep[row, :], got[row, :], w1, w2).astype(bf16)
            cols = slice(c * half, (c + 1) * half)
            for at in range(0, LANES, LANES // 2):
                to = i * LANES + at
                ref = keep2 if to < rows // 2 else send2
                to = to if to < rows // 2 else to - rows // 2
                ref[to:to + LANES // 2, cols] = out[at:at + LANES // 2, :]
            lines[c * per + i:c * per + i + 1, :] = join(line[i:i + 1, :], got_line[per + i:per + i + 1, :])[2]


def merge_two(a_keep, a_got, b_keep, b_got, a_line, b_line, a_lse, b_lse):
    rows, half = a_keep.shape
    side = jax.ShapeDtypeStruct((rows // 2, 2 * half), bf16)
    return pl.pallas_call(
        merge_two_kernel, out_shape=[side] * 2 + [jax.ShapeDtypeStruct(a_line.shape, f32)],
        in_specs=[VM] * 8, out_specs=[VM] * 3, compiler_params=params(),
        cost_estimate=pl.CostEstimate(flops=8 * rows * half, bytes_accessed=12 * rows * half, transcendentals=0),
        name="merge_two",
    )(a_keep, a_got, b_keep, b_got, a_line, b_line, a_lse, b_lse)


def finish_kernel(keep, got, lines, got_lines, hid, target, loss, grad):
    rows, model = keep.shape
    for c in range(2):
        mine = lines[c:c + 1, :]
        other = pltpu.roll(got_lines[c:c + 1, :], LANES // 2, axis=1)
        w1, w2, whole = join(by_row(mine, 0), by_row(other, 0))
        cols = slice(c * model // 2, (c + 1) * model // 2)
        out = mix_rows(keep[:, cols], got[:, cols], w1[:rows], w2[:rows])
        grad[:, cols] = (out - target[:, cols].astype(f32)).astype(bf16)
        if c == 0:
            lse = whole[:rows, 0:1]
    aim = jnp.sum(hid[...].astype(f32) * target[...].astype(f32), axis=1, keepdims=True)
    column = jnp.concatenate([lse - aim, jnp.zeros((LANES - rows, 1), f32)], axis=0)
    loss[...] = as_line(column)


def finish(keep, got, lines, got_lines, hid, target):
    rows, model = keep.shape
    return pl.pallas_call(
        finish_kernel,
        out_shape=[jax.ShapeDtypeStruct((1, LANES), f32), jax.ShapeDtypeStruct((rows, model), bf16)],
        in_specs=[VM] * 6, out_specs=[VM] * 2, compiler_params=params(),
        cost_estimate=pl.CostEstimate(flops=8 * rows * model, bytes_accessed=12 * rows * model, transcendentals=0),
        name="finish",
    )(keep, got, lines, got_lines, hid, target)


def halve_kernel(keep, got, lines, got_lines, keep2, send2, lines2):
    rows, model = keep.shape
    per = lines.shape[0] // 2
    near = per // 2
    for c in range(2):
        cols = slice(c * model // 2, (c + 1) * model // 2)
        for i in range(near):
            mine, other = c * per + i, c * per + near + i
            w1, w2, _ = join(by_row(lines, mine), by_row(got_lines, other))
            row = slice(i * LANES, (i + 1) * LANES)
            out = mix_rows(keep[row, cols], got[row, cols], w1, w2).astype(bf16)
            for at in range(0, LANES, LANES // 2):
                to = i * LANES + at
                ref = keep2 if to < rows // 2 else send2
                to = to if to < rows // 2 else to - rows // 2
                ref[to:to + LANES // 2, cols] = out[at:at + LANES // 2, :]
            lines2[c * near + i:c * near + i + 1, :] = join(
                lines[mine:mine + 1, :], got_lines[other:other + 1, :])[2]


def halve(keep, got, lines, got_lines):
    rows, model = keep.shape
    side = jax.ShapeDtypeStruct((rows // 2, model), bf16)
    return pl.pallas_call(
        halve_kernel, out_shape=[side] * 2 + [jax.ShapeDtypeStruct((lines.shape[0] // 2, LANES), f32)],
        in_specs=[VM] * 4, out_specs=[VM] * 3, compiler_params=params(), name="halve",
    )(keep, got, lines, got_lines)


def per_device(char_ids, char_table, conv_weight, proj_weight, gate_weight, trans_weight, gate_bias, hidden, targets,
               *, vocab, blk):
    devices = vocab * blk
    axes = ("vocab", "blk")

    def swap(x, bits):
        return lax.ppermute(x, axes, [(i, i ^ bits) for i in range(devices)])

    core, near = blk, 1
    bit_a, bit_b = 2 * blk, 4 * blk
    rest = [1 << i for i in range(1, blk.bit_length() - 1)] + [
        blk << i for i in range(3, vocab.bit_length() - 1)]
    me = lax.axis_index("vocab") * blk + lax.axis_index("blk")
    local, length = char_ids.shape
    mine = hidden.shape[0]

    rows, goal = hidden, targets.reshape(1, mine)
    for bit in rest:
        rows, goal = (jnp.concatenate([rows, swap(rows, bit)], axis=0),
                      jnp.concatenate([goal, swap(goal, bit)], axis=1))
    hid = [rows] + [swap(rows, b) for b in (bit_b, bit_a, bit_a | bit_b)]
    goal = jnp.concatenate([goal] + [swap(goal, b) for b in (bit_b, bit_a, bit_a | bit_b)], axis=1)

    ids_t = char_ids.T
    some = ids_t.astype(bf16)
    some = jnp.concatenate([some, swap(some, core)], axis=1)
    some = jnp.concatenate([some, swap(some, near)], axis=1)
    apart = (goal // local) ^ me
    slot = jnp.where(apart == 0, 0, jnp.where(apart == core, 1, jnp.where(
        apart == near, 2, jnp.where(apart == (core | near), 3, -1))))
    spot = jnp.where(slot >= 0, slot * local + goal % local, -1)
    chars = pick(spot, some)
    for bit in [bit_a, bit_b] + rest[::-1]:
        n = chars.shape[1] // 2
        chars = chars[:, :n] + swap(chars[:, n:], bit)
    aim_ids = chars.astype(jnp.int32)
    pad = -mine % LANES
    aim_ids = jnp.pad(aim_ids, ((0, 0), (0, pad)))

    tab_t = char_table.T.astype(f32)
    weights = (tab_t, conv_weight, proj_weight, gate_weight, trans_weight, gate_bias)
    half = local // 2
    (e0,) = embed(ids_t[:, :half], (half,), *weights)
    e1, aim = embed(jnp.concatenate([ids_t[:, half:], aim_ids], axis=1), (half, mine), *weights)
    c0, c1 = swap(e0, core), swap(e1, core)
    z0, z1 = swap(e0, near), swap(e1, near)
    d0, d1 = swap(z0, core), swap(z1, core)

    state = first_fold(hid, [e0, c0, e1, c1])
    a_keep, a_send, b_keep, b_send, lse = second_fold(hid, [z0, d0, z1, d1], state)
    a_keep, a_send, b_keep, b_send, a_line, b_line = merge_one(
        a_keep, swap(a_send, bit_a), b_keep, swap(b_send, bit_b), lse, swap(lse, bit_a), swap(lse, bit_b))
    keep, send, lines = merge_two(
        a_keep, swap(a_send, bit_b), b_keep, swap(b_send, bit_a), a_line, b_line,
        swap(a_line, bit_b), swap(b_line, bit_a))
    for bit in rest[:0:-1]:
        keep, send, lines = halve(keep, swap(send, bit), lines, swap(lines, bit))
    loss, grad = finish(keep, swap(send, rest[0]), lines, swap(lines, rest[0]), hidden, aim)
    return loss[0, :mine], grad


def solution(mesh):
    words = P(("vocab", "blk"))
    return jax.shard_map(
        functools.partial(per_device, vocab=mesh.shape["vocab"], blk=mesh.shape["blk"]),
        mesh=mesh,
        in_specs=(P(("vocab", "blk"), None), P(), P(), P(), P(), P(), P(), P(("vocab", "blk"), None), words),
        out_specs=(words, P(("vocab", "blk"), None)),
        check_vma=False,
    )
```

```python
import functools
import jax
import jax.numpy as jnp
from jax import lax
from jax.experimental import pallas as pl
from jax.experimental.pallas import tpu as pltpu
from jax.sharding import PartitionSpec as P

bf16=jnp.bfloat16; f32=jnp.float32
LANES = 128
SPAN = 8

def prep_toeplitz(conv_ref, toep, ce, widths, filters):
    depth = toep.shape[0]
    for k in range(widths):
        rows = (k + 1) * ce
        piece = conv_ref[0:rows, k * filters:(k + 1) * filters]
        for o in range(SPAN):
            cols = slice((k * SPAN + o) * filters, (k * SPAN + o + 1) * filters)
            if o:
                toep[0:o * ce, cols] = jnp.zeros((o * ce, filters), bf16)
            toep[o * ce:o * ce + rows, cols] = piece
            rest = depth - o * ce - rows
            if rest:
                toep[o * ce + rows:depth, cols] = jnp.zeros((rest, filters), bf16)

def lookup(ids_ref, start, words, tab_ref, vec, turn, length, ce):
    per = LANES // ce
    for at in range(0, words, LANES):
        count = min(LANES, words - at)
        turn[...] = jnp.zeros(turn.shape, f32)
        turn[0:count, 0:length] = ids_ref[start + at:start + at + count, 0:length].astype(f32)
        ids = turn[...].T.astype(jnp.int32)
        for g in range(vec.shape[1] // LANES):
            parts = []
            for q in range(per):
                p = g * per + q
                if p >= length:
                    parts.append(jnp.zeros((ce, LANES), f32))
                    continue
                idx = jnp.broadcast_to(ids[p:p + 1, :], (8, LANES))
                low = jnp.bitwise_and(idx, LANES - 1)
                top = idx >= LANES
                for h in range(ce // 8):
                    one = jnp.take_along_axis(tab_ref[h * 8:h * 8 + 8, 0:LANES], low, axis=1)
                    two = jnp.take_along_axis(tab_ref[h * 8:h * 8 + 8, LANES:2 * LANES], low, axis=1)
                    parts.append(jnp.where(top, two, one))
            block = jnp.concatenate(parts, axis=0)
            vec[at:at + count, g * LANES:(g + 1) * LANES] = block.T[0:count].astype(bf16)


def conv_pool(vec, toep, acc, length, widths, filters):
    words = vec.shape[0]
    def tile(b, k, o, lhs):
        cols = slice((k * SPAN + o) * filters, (k * SPAN + o + 2) * filters)
        return jnp.dot(lhs, toep[:, cols], preferred_element_type=f32)
    acc[...] = jnp.full(acc.shape, -jnp.inf, f32)
    least = (length - widths + 1) // SPAN
    def body(b, _):
        lhs = vec[:, pl.ds(pl.multiple_of(b * LANES, LANES), 2 * LANES)]
        for k in range(widths):
            best = acc[:, k * filters:(k + 1) * filters]
            for o in range(0, SPAN, 2):
                r = tile(b, k, o, lhs)
                best = jnp.maximum(best, jnp.maximum(r[:, :filters], r[:, filters:]))
            acc[:, k * filters:(k + 1) * filters] = best
        return 0
    lax.fori_loop(0, least, body, 0)
    for b in range(least, -(-length // SPAN)):
        lhs = vec[:, b * LANES:(b + 2) * LANES]
        for k in range(widths):
            usable = min(SPAN, length - k - b * SPAN)
            if usable <= 0: continue
            best = acc[:, k * filters:(k + 1) * filters]
            for o in range(0, usable, 2):
                r = tile(b, k, o, lhs)
                best = jnp.maximum(best, r[:, :filters])
                if o + 1 < usable:
                    best = jnp.maximum(best, r[:, filters:])
            acc[:, k * filters:(k + 1) * filters] = best

def cnn_kernel(ids_ref, tab_ref, conv_ref, bias_ref, proj_hbm, gate_hbm, trans_hbm, *rest,
               widths, filters, ce, length, layers, nt, start):
    out_ref, vec, toep, acc, feat, proj, gate, trans, state, last, turn, sems = rest
    copies = [pltpu.make_async_copy(s, d, sems.at[i]) for i, (s, d) in enumerate(
        ((proj_hbm, proj), (gate_hbm, gate), (trans_hbm, trans)))]
    for c in copies:
        c.start()
    words = out_ref.shape[0]
    prep_toeplitz(conv_ref, toep, ce, widths, filters)
    lookup(ids_ref, start, words, tab_ref, vec, turn, length, ce)
    conv_pool(vec, toep, acc, length, widths, filters)
    for c in copies:
        c.wait()
    feat[...] = jnp.tanh(acc[...]).astype(bf16)
    model = last.shape[1]
    for n in range(0, model, nt):
        state[:, n:n + nt] = jnp.dot(feat[...], proj[:, n:n + nt], preferred_element_type=f32).astype(bf16)
    for l in range(layers):
        for n in range(0, model, nt):
            cur = state[...]
            g = jnp.dot(cur, gate[l, :, n:n + nt], preferred_element_type=f32) + bias_ref[l:l + 1, n:n + nt]
            t = jnp.dot(cur, trans[l, :, n:n + nt], preferred_element_type=f32)
            opened = jax.nn.sigmoid(g)
            carried = jnp.maximum(t, 0.0)
            new = (opened * carried + (1.0 - opened) * state[:, n:n + nt].astype(f32)).astype(bf16)
            if l + 1 < layers:
                last[:, n:n + nt] = new
            else:
                out_ref[:, n:n + nt] = new
        if l + 1 < layers:
            state[...] = last[...]


ANY = pl.BlockSpec(memory_space=pl.ANY)
VM = pl.BlockSpec(memory_space=pltpu.VMEM)


def params(limit_mib=56):
    return pltpu.CompilerParams(vmem_limit_bytes=limit_mib << 20)


def embed(ids, length, start, words, tab_t, conv_weight, proj_weight, gate_weight, trans_weight, gate_bias, nt=256):
    ce = tab_t.shape[0]
    widths = conv_weight.shape[0] // ce
    filters = conv_weight.shape[1] // widths
    layers, model, _ = gate_weight.shape
    flops = 2 * words * (length * 256 * widths * filters + widths * filters * model + 2 * layers * model * model)
    return pl.pallas_call(
        functools.partial(cnn_kernel, widths=widths, filters=filters, ce=ce, length=length, layers=layers, nt=nt,
                          start=start),
        out_shape=jax.ShapeDtypeStruct((words, model), bf16),
        in_specs=[VM, VM, VM, VM, ANY, ANY, ANY],
        out_specs=VM,
        scratch_shapes=[
            pltpu.VMEM((words, (-(-length // SPAN) + 1) * LANES), bf16),
            pltpu.VMEM((2 * LANES, widths * SPAN * filters), bf16),
            pltpu.VMEM((words, widths * filters), f32),
            pltpu.VMEM((words, widths * filters), bf16),
            pltpu.VMEM(proj_weight.shape, bf16),
            pltpu.VMEM(gate_weight.shape, bf16),
            pltpu.VMEM(trans_weight.shape, bf16),
            pltpu.VMEM((words, model), bf16),
            pltpu.VMEM((words, model), bf16),
            pltpu.VMEM((LANES, LANES), f32),
            pltpu.SemaphoreType.DMA((3,)),
        ],
        compiler_params=params(),
        cost_estimate=pl.CostEstimate(flops=flops, bytes_accessed=12 << 20, transcendentals=words * 4096),
        name="embed",
    )(ids, tab_t, conv_weight, gate_bias, proj_weight, gate_weight, trans_weight)


def pick_kernel(me_ref, *refs, nh, order, local):
    hid, ids = refs[:nh], refs[nh:nh + len(order)]
    keep, send = refs[nh + len(order):]
    model = hid[0].shape[1] - LANES
    at = 0
    for h in hid:
        rows = h.shape[0]
        code = h[:, model:model + LANES].astype(f32).astype(jnp.int32)
        goal = code[:, 0:1] * 256 + code[:, 1:2]
        owner = lax.div(goal, local)
        apart = jnp.bitwise_xor(owner, me_ref[0])
        place = goal - owner * local
        lane = lax.broadcasted_iota(jnp.int32, (rows, local), 1)
        out = None
        for ref, bits in zip(ids, order):
            spot = jnp.where(apart == bits, place, -1)
            hot = jnp.where(lane == spot, 1.0, 0.0).astype(bf16)
            d = lax.dot_general(hot, ref[...], (((1,), (1,)), ((), ())), preferred_element_type=f32)
            out = d if out is None else out + d
        ref = keep if at < keep.shape[0] else send
        to = at if at < keep.shape[0] else at - keep.shape[0]
        ref[to:to + rows, 0:out.shape[1]] = out.astype(bf16)
        at += rows


def pick(me, hid, ids, order):
    rows = sum(h.shape[0] for h in hid)
    chars, local = ids[0].shape
    side = jax.ShapeDtypeStruct((rows // 2, chars), bf16)
    return pl.pallas_call(
        functools.partial(pick_kernel, nh=len(hid), order=order, local=local),
        out_shape=[side] * 2,
        in_specs=[pl.BlockSpec(memory_space=pltpu.SMEM)] + [VM] * (len(hid) + len(ids)), out_specs=[VM] * 2,
        compiler_params=params(),
        cost_estimate=pl.CostEstimate(flops=2 * 256 * rows * local * len(ids), bytes_accessed=2 << 20,
                                      transcendentals=0),
        name="pick",
    )(me, *hid, *ids)


def by_row(line, i):
    return jnp.broadcast_to(line[i:i + 1, :], (LANES, LANES)).T


def as_line(column):
    return jnp.broadcast_to(column, (LANES, LANES)).T[0:1, :]


def part_of_softmax(rows_ref, words, score, prob, out):
    at = 0
    top = None
    for ref in words:
        n = ref.shape[0]
        piece = lax.dot_general(rows_ref[...], ref[...], (((1,), (1,)), ((), ())), preferred_element_type=f32)
        score[:, at:at + n] = piece
        best = jnp.max(piece, axis=1, keepdims=True)
        top = best if top is None else jnp.maximum(top, best)
        at += n
    at = 0
    total = None
    for ref in words:
        n = ref.shape[0]
        w = jnp.exp(score[:, at:at + n] - top).astype(bf16)
        prob[:, at:at + n] = w
        s = jnp.sum(w.astype(f32), axis=1, keepdims=True)
        total = s if total is None else total + s
        at += n
    model = out.shape[1]
    for n in range(0, model, 256):
        at = 0
        res = None
        for ref in words:
            size = ref.shape[0]
            d = jnp.dot(prob[:, at:at + size], ref[:, n:n + 256], preferred_element_type=f32)
            res = d if res is None else res + d
            at += size
        out[:, n:n + 256] = res
    return top, total


def first_kernel(*refs, nh, nw):
    hid, words = refs[:nh], refs[nh:nh + nw]
    out, top_ref, total_ref, rows, score, prob = refs[nh + nw:]
    at = 0
    for h in hid:
        rows[at:at + h.shape[0], :] = h[:, 0:rows.shape[1]]
        at += h.shape[0]
    top, total = part_of_softmax(rows, words, score, prob, out)
    top_ref[...] = jnp.broadcast_to(top, top_ref.shape)
    total_ref[...] = jnp.broadcast_to(total, total_ref.shape)


def fold_cost(rows, words, model):
    return pl.CostEstimate(flops=4 * rows * words * model, bytes_accessed=2 * (rows + words) * model,
                           transcendentals=rows * words)


def first_fold(hid, words):
    model = words[0].shape[1]
    rows = sum(h.shape[0] for h in hid)
    count = sum(w.shape[0] for w in words)
    return pl.pallas_call(
        functools.partial(first_kernel, nh=len(hid), nw=len(words)),
        out_shape=[jax.ShapeDtypeStruct((rows, model), f32), jax.ShapeDtypeStruct((rows, LANES), f32),
                   jax.ShapeDtypeStruct((rows, LANES), f32)],
        in_specs=[VM] * (len(hid) + len(words)), out_specs=[VM] * 3,
        scratch_shapes=[pltpu.VMEM((rows, model), bf16), pltpu.VMEM((rows, count), f32),
                        pltpu.VMEM((rows, count), bf16)],
        compiler_params=params(), cost_estimate=fold_cost(rows, count, model), name="first_fold",
    )(*hid, *words)


def second_kernel(*refs, nh, nw):
    hid, words = refs[:nh], refs[nh:nh + nw]
    old, top_ref, total_ref, a_keep, a_send, b_keep, b_send, lse, rows, score, prob, new = refs[nh + nw:]
    at = 0
    for h in hid:
        rows[at:at + h.shape[0], :] = h[:, 0:rows.shape[1]]
        at += h.shape[0]
    top2, total2 = part_of_softmax(rows, words, score, prob, new)
    top1, total1 = top_ref[:, 0:1], total_ref[:, 0:1]
    top = jnp.maximum(top1, top2)
    s1, s2 = jnp.exp(top1 - top), jnp.exp(top2 - top)
    total = s1 * total1 + s2 * total2
    s1, s2 = s1 / total, s2 / total
    whole = top + jnp.log(total)
    count, model = new.shape
    half, quarter = model // 2, count // 4
    for i in range(count // LANES):
        part = slice(i * LANES, (i + 1) * LANES)
        lse[i:i + 1, :] = as_line(whole[part, :])
    for q in range(4):
        part = slice(q * quarter, (q + 1) * quarter)
        mix = s1[part, :] * old[part, :] + s2[part, :] * new[part, :]
        mix = mix.astype(bf16)
        a = a_keep if q < 2 else a_send
        a[(q % 2) * quarter:(q % 2 + 1) * quarter, :] = mix[:, :half]
        b = b_keep if q % 2 == 0 else b_send
        b[(q // 2) * quarter:(q // 2 + 1) * quarter, :] = mix[:, half:]


def second_fold(hid, words, state):
    model = words[0].shape[1]
    rows = sum(h.shape[0] for h in hid)
    count = sum(w.shape[0] for w in words)
    side = jax.ShapeDtypeStruct((rows // 2, model // 2), bf16)
    return pl.pallas_call(
        functools.partial(second_kernel, nh=len(hid), nw=len(words)),
        out_shape=[side] * 4 + [jax.ShapeDtypeStruct((rows // LANES, LANES), f32)],
        in_specs=[VM] * (len(hid) + len(words) + 3), out_specs=[VM] * 5,
        scratch_shapes=[pltpu.VMEM((rows, model), bf16), pltpu.VMEM((rows, count), f32),
                        pltpu.VMEM((rows, count), bf16), pltpu.VMEM((rows, model), f32)],
        compiler_params=params(), cost_estimate=fold_cost(rows, count, model), name="second_fold",
    )(*hid, *words, *state)


def join(one, two):
    top = jnp.maximum(one, two)
    s1, s2 = jnp.exp(one - top), jnp.exp(two - top)
    total = s1 + s2
    return s1 / total, s2 / total, top + jnp.log(total)


def mix_rows(mine, other, s1, s2):
    parts = []
    for n in range(0, mine.shape[1], LANES):
        parts.append(s1 * mine[:, n:n + LANES].astype(f32) + s2 * other[:, n:n + LANES].astype(f32))
    return jnp.concatenate(parts, axis=1)


def merge_one_kernel(a_keep, a_got, b_keep, b_got, lse, a_lse, b_lse,
                     a_keep2, a_send2, b_keep2, b_send2, a_line, b_line):
    lines = lse.shape[0]
    per = lines // 4
    for keep, got, got_lse, outs, line, mine_q, their_q in (
            (a_keep, a_got, a_lse, (a_keep2, a_send2), a_line, (0, 1), (2, 3)),
            (b_keep, b_got, b_lse, (b_keep2, b_send2), b_line, (0, 2), (1, 3))):
        for j in range(2):
            for i in range(per):
                mi, ti = mine_q[j] * per + i, their_q[j] * per + i
                w1, w2, _ = join(by_row(lse, mi), by_row(got_lse, ti))
                row = slice((j * per + i) * LANES, (j * per + i + 1) * LANES)
                outs[j][i * LANES:(i + 1) * LANES, :] = mix_rows(keep[row, :], got[row, :], w1, w2).astype(bf16)
                line[j * per + i:j * per + i + 1, :] = join(lse[mi:mi + 1, :], got_lse[ti:ti + 1, :])[2]


def merge_one(a_keep, a_got, b_keep, b_got, lse, a_lse, b_lse):
    rows, half = a_keep.shape
    side = jax.ShapeDtypeStruct((rows // 2, half), bf16)
    line = jax.ShapeDtypeStruct((lse.shape[0] // 2, LANES), f32)
    return pl.pallas_call(
        merge_one_kernel, out_shape=[side] * 4 + [line] * 2,
        in_specs=[VM] * 7, out_specs=[VM] * 6, compiler_params=params(),
        cost_estimate=pl.CostEstimate(flops=4 * rows * half, bytes_accessed=12 * rows * half, transcendentals=0),
        name="merge_one",
    )(a_keep, a_got, b_keep, b_got, lse, a_lse, b_lse)


def merge_two_kernel(a_keep, a_got, b_keep, b_got, a_line, b_line, a_lse, b_lse, keep2, send2, lines):
    per = a_line.shape[0] // 2
    rows, half = a_keep.shape
    for c, (keep, got, line, got_line) in enumerate(
            ((a_keep, a_got, a_line, a_lse), (b_keep, b_got, b_line, b_lse))):
        for i in range(per):
            w1, w2, _ = join(by_row(line, i), by_row(got_line, per + i))
            row = slice(i * LANES, (i + 1) * LANES)
            out = mix_rows(keep[row, :], got[row, :], w1, w2).astype(bf16)
            cols = slice(c * half, (c + 1) * half)
            for at in range(0, LANES, LANES // 2):
                to = i * LANES + at
                ref = keep2 if to < rows // 2 else send2
                to = to if to < rows // 2 else to - rows // 2
                ref[to:to + LANES // 2, cols] = out[at:at + LANES // 2, :]
            lines[c * per + i:c * per + i + 1, :] = join(line[i:i + 1, :], got_line[per + i:per + i + 1, :])[2]


def merge_two(a_keep, a_got, b_keep, b_got, a_line, b_line, a_lse, b_lse):
    rows, half = a_keep.shape
    side = jax.ShapeDtypeStruct((rows // 2, 2 * half), bf16)
    return pl.pallas_call(
        merge_two_kernel, out_shape=[side] * 2 + [jax.ShapeDtypeStruct(a_line.shape, f32)],
        in_specs=[VM] * 8, out_specs=[VM] * 3, compiler_params=params(),
        cost_estimate=pl.CostEstimate(flops=8 * rows * half, bytes_accessed=12 * rows * half, transcendentals=0),
        name="merge_two",
    )(a_keep, a_got, b_keep, b_got, a_line, b_line, a_lse, b_lse)


def finish_kernel(keep, got, lines, got_lines, hid, target, loss, grad):
    rows, model = keep.shape
    for c in range(2):
        mine = lines[c:c + 1, :]
        other = pltpu.roll(got_lines[c:c + 1, :], LANES // 2, axis=1)
        w1, w2, whole = join(by_row(mine, 0), by_row(other, 0))
        cols = slice(c * model // 2, (c + 1) * model // 2)
        out = mix_rows(keep[:, cols], got[:, cols], w1[:rows], w2[:rows])
        grad[:, cols] = (out - target[:, cols].astype(f32)).astype(bf16)
        if c == 0:
            lse = whole[:rows, 0:1]
    aim = jnp.sum(hid[...].astype(f32) * target[...].astype(f32), axis=1, keepdims=True)
    column = jnp.concatenate([lse - aim, jnp.zeros((LANES - rows, 1), f32)], axis=0)
    loss[...] = as_line(column)


def finish(keep, got, lines, got_lines, hid, target):
    rows, model = keep.shape
    return pl.pallas_call(
        finish_kernel,
        out_shape=[jax.ShapeDtypeStruct((1, LANES), f32), jax.ShapeDtypeStruct((rows, model), bf16)],
        in_specs=[VM] * 6, out_specs=[VM] * 2, compiler_params=params(),
        cost_estimate=pl.CostEstimate(flops=8 * rows * model, bytes_accessed=12 * rows * model, transcendentals=0),
        name="finish",
    )(keep, got, lines, got_lines, hid, target)


def halve_kernel(keep, got, lines, got_lines, keep2, send2, lines2):
    rows, model = keep.shape
    per = lines.shape[0] // 2
    near = per // 2
    for c in range(2):
        cols = slice(c * model // 2, (c + 1) * model // 2)
        for i in range(near):
            mine, other = c * per + i, c * per + near + i
            w1, w2, _ = join(by_row(lines, mine), by_row(got_lines, other))
            row = slice(i * LANES, (i + 1) * LANES)
            out = mix_rows(keep[row, cols], got[row, cols], w1, w2).astype(bf16)
            for at in range(0, LANES, LANES // 2):
                to = i * LANES + at
                ref = keep2 if to < rows // 2 else send2
                to = to if to < rows // 2 else to - rows // 2
                ref[to:to + LANES // 2, cols] = out[at:at + LANES // 2, :]
            lines2[c * near + i:c * near + i + 1, :] = join(
                lines[mine:mine + 1, :], got_lines[other:other + 1, :])[2]


def halve(keep, got, lines, got_lines):
    rows, model = keep.shape
    side = jax.ShapeDtypeStruct((rows // 2, model), bf16)
    return pl.pallas_call(
        halve_kernel, out_shape=[side] * 2 + [jax.ShapeDtypeStruct((lines.shape[0] // 2, LANES), f32)],
        in_specs=[VM] * 4, out_specs=[VM] * 3, compiler_params=params(), name="halve",
    )(keep, got, lines, got_lines)


def per_device(char_ids, char_table, conv_weight, proj_weight, gate_weight, trans_weight, gate_bias, hidden, targets,
               *, vocab, blk):
    devices = vocab * blk
    axes = ("vocab", "blk")

    def swap(x, bits):
        return lax.ppermute(x, axes, [(i, i ^ bits) for i in range(devices)])

    core, near = blk, 1
    bit_a, bit_b = 2 * blk, 4 * blk
    rest = [1 << i for i in range(1, blk.bit_length() - 1)] + [
        blk << i for i in range(3, vocab.bit_length() - 1)]
    me = lax.axis_index("vocab") * blk + lax.axis_index("blk")
    local, length = char_ids.shape
    mine = hidden.shape[0]

    goal = targets.reshape(mine, 1)
    code = jnp.concatenate([goal // 256, goal % 256], axis=1).astype(bf16)
    rows = jnp.concatenate([hidden, code, jnp.zeros((mine, LANES - 2), bf16)], axis=1)
    for bit in rest:
        rows = jnp.concatenate([rows, swap(rows, bit)], axis=0)

    ids_own = char_ids.T.astype(bf16)
    ids_core, ids_near = swap(ids_own, core), swap(ids_own, near)

    tab_t = char_table.T.astype(f32)
    weights = (tab_t, conv_weight, proj_weight, gate_weight, trans_weight, gate_bias)
    sizes = (192, 192, 128) if local == 512 else (local // 2, local // 4, local // 4)
    pieces, start, ids = [], 0, char_ids
    hid = None
    for i, size in enumerate(sizes):
        pieces.append(embed(ids, length, start, size, *weights))
        start += size
        if i == 0:
            rows, ids_core, ids_near, ids, _ = lax.optimization_barrier((rows, ids_core, ids_near, ids, pieces[0]))
            hid = [rows] + [swap(rows, b) for b in (bit_b, bit_a, bit_a | bit_b)]
            ids_far = swap(ids_near, core)
        elif i == 1:
            *hid, ids_far, ids = lax.optimization_barrier((*hid, ids_far, ids))
    cores = [swap(e, core) for e in pieces]
    nears = [swap(e, near) for e in pieces]
    fars = [swap(e, core) for e in nears]

    late = 1 if 4 * hid[0].shape[0] <= local else len(nears)
    state = first_fold(hid, pieces + cores + nears[:-late] + fars[:-late])
    me = me.astype(jnp.int32).reshape(1)
    chars, away = pick(me, hid, [ids_own, ids_core, ids_near, ids_far], (0, core, near, core | near))
    chars = chars + swap(away, bit_a)
    for bit in [bit_b] + rest[::-1]:
        n = chars.shape[0] // 2
        chars = chars[:n] + swap(chars[n:], bit)
    aim = embed(chars, length, 0, mine, *weights)

    a_keep, a_send, b_keep, b_send, lse = second_fold(hid, nears[-late:] + fars[-late:], state)
    a_keep, a_send, b_keep, b_send, a_line, b_line = merge_one(
        a_keep, swap(a_send, bit_a), b_keep, swap(b_send, bit_b), lse, swap(lse, bit_a), swap(lse, bit_b))
    keep, send, lines = merge_two(
        a_keep, swap(a_send, bit_b), b_keep, swap(b_send, bit_a), a_line, b_line,
        swap(a_line, bit_b), swap(b_line, bit_a))
    for bit in rest[:0:-1]:
        keep, send, lines = halve(keep, swap(send, bit), lines, swap(lines, bit))
    loss, grad = finish(keep, swap(send, rest[0]), lines, swap(lines, rest[0]), hidden, aim)
    return loss[0, :mine], grad


def solution(mesh):
    words = P(("vocab", "blk"))
    return jax.shard_map(
        functools.partial(per_device, vocab=mesh.shape["vocab"], blk=mesh.shape["blk"]),
        mesh=mesh,
        in_specs=(P(("vocab", "blk"), None), P(), P(), P(), P(), P(), P(), P(("vocab", "blk"), None), words),
        out_specs=(words, P(("vocab", "blk"), None)),
        check_vma=False,
    )
```

```python
import functools
import jax
import jax.numpy as jnp
from jax import lax
from jax.experimental import pallas as pl
from jax.experimental.pallas import tpu as pltpu
from jax.sharding import PartitionSpec as P

bf16=jnp.bfloat16; f32=jnp.float32
LANES = 128
SPAN = 8

def prep_toeplitz(conv_ref, toep, ce, widths, filters):
    depth = toep.shape[0]
    for k in range(widths):
        rows = (k + 1) * ce
        piece = conv_ref[0:rows, k * filters:(k + 1) * filters]
        for o in range(SPAN):
            cols = slice((k * SPAN + o) * filters, (k * SPAN + o + 1) * filters)
            if o:
                toep[0:o * ce, cols] = jnp.zeros((o * ce, filters), bf16)
            toep[o * ce:o * ce + rows, cols] = piece
            rest = depth - o * ce - rows
            if rest:
                toep[o * ce + rows:depth, cols] = jnp.zeros((rest, filters), bf16)

def lookup(ids_ref, start, words, tab_ref, vec, turn, length, ce):
    per = LANES // ce
    for at in range(0, words, LANES):
        count = min(LANES, words - at)
        turn[...] = jnp.zeros(turn.shape, f32)
        turn[0:count, 0:length] = ids_ref[start + at:start + at + count, 0:length].astype(f32)
        ids = turn[...].T.astype(jnp.int32)
        for g in range(vec.shape[1] // LANES):
            parts = []
            for q in range(per):
                p = g * per + q
                if p >= length:
                    parts.append(jnp.zeros((ce, LANES), f32))
                    continue
                idx = jnp.broadcast_to(ids[p:p + 1, :], (8, LANES))
                low = jnp.bitwise_and(idx, LANES - 1)
                top = idx >= LANES
                for h in range(ce // 8):
                    one = jnp.take_along_axis(tab_ref[h * 8:h * 8 + 8, 0:LANES], low, axis=1)
                    two = jnp.take_along_axis(tab_ref[h * 8:h * 8 + 8, LANES:2 * LANES], low, axis=1)
                    parts.append(jnp.where(top, two, one))
            block = jnp.concatenate(parts, axis=0)
            vec[at:at + count, g * LANES:(g + 1) * LANES] = block.T[0:count].astype(bf16)


def conv_pool(vec, toep, acc, length, widths, filters):
    words = vec.shape[0]
    def tile(b, k, o, lhs):
        cols = slice((k * SPAN + o) * filters, (k * SPAN + o + 2) * filters)
        return jnp.dot(lhs, toep[:, cols], preferred_element_type=f32)
    acc[...] = jnp.full(acc.shape, -jnp.inf, f32)
    least = (length - widths + 1) // SPAN
    def body(b, _):
        lhs = vec[:, pl.ds(pl.multiple_of(b * LANES, LANES), 2 * LANES)]
        for k in range(widths):
            best = acc[:, k * filters:(k + 1) * filters]
            for o in range(0, SPAN, 2):
                r = tile(b, k, o, lhs)
                best = jnp.maximum(best, jnp.maximum(r[:, :filters], r[:, filters:]))
            acc[:, k * filters:(k + 1) * filters] = best
        return 0
    lax.fori_loop(0, least, body, 0)
    for b in range(least, -(-length // SPAN)):
        lhs = vec[:, b * LANES:(b + 2) * LANES]
        for k in range(widths):
            usable = min(SPAN, length - k - b * SPAN)
            if usable <= 0: continue
            best = acc[:, k * filters:(k + 1) * filters]
            for o in range(0, usable, 2):
                r = tile(b, k, o, lhs)
                best = jnp.maximum(best, r[:, :filters])
                if o + 1 < usable:
                    best = jnp.maximum(best, r[:, filters:])
            acc[:, k * filters:(k + 1) * filters] = best

def cnn_kernel(ids_ref, tab_ref, conv_ref, bias_ref, proj_hbm, gate_hbm, trans_hbm, *rest,
               widths, filters, ce, length, layers, nt, start):
    out_ref, vec, toep, acc, feat, proj, gate, trans, state, last, turn, sems = rest
    copies = [pltpu.make_async_copy(s, d, sems.at[i]) for i, (s, d) in enumerate(
        ((proj_hbm, proj), (gate_hbm, gate), (trans_hbm, trans)))]
    for c in copies:
        c.start()
    words = out_ref.shape[0]
    prep_toeplitz(conv_ref, toep, ce, widths, filters)
    lookup(ids_ref, start, words, tab_ref, vec, turn, length, ce)
    conv_pool(vec, toep, acc, length, widths, filters)
    for c in copies:
        c.wait()
    feat[...] = jnp.tanh(acc[...]).astype(bf16)
    model = last.shape[1]
    for n in range(0, model, nt):
        state[:, n:n + nt] = jnp.dot(feat[...], proj[:, n:n + nt], preferred_element_type=f32).astype(bf16)
    for l in range(layers):
        for n in range(0, model, nt):
            cur = state[...]
            g = jnp.dot(cur, gate[l, :, n:n + nt], preferred_element_type=f32) + bias_ref[l:l + 1, n:n + nt]
            t = jnp.dot(cur, trans[l, :, n:n + nt], preferred_element_type=f32)
            opened = jax.nn.sigmoid(g)
            carried = jnp.maximum(t, 0.0)
            new = (opened * carried + (1.0 - opened) * state[:, n:n + nt].astype(f32)).astype(bf16)
            if l + 1 < layers:
                last[:, n:n + nt] = new
            else:
                out_ref[:, n:n + nt] = new
        if l + 1 < layers:
            state[...] = last[...]


ANY = pl.BlockSpec(memory_space=pl.ANY)
VM = pl.BlockSpec(memory_space=pltpu.VMEM)


def params(limit_mib=56):
    return pltpu.CompilerParams(vmem_limit_bytes=limit_mib << 20)


def embed(ids, length, start, words, tab_t, conv_weight, proj_weight, gate_weight, trans_weight, gate_bias, nt=256):
    ce = tab_t.shape[0]
    widths = conv_weight.shape[0] // ce
    filters = conv_weight.shape[1] // widths
    layers, model, _ = gate_weight.shape
    flops = 2 * words * (length * 256 * widths * filters + widths * filters * model + 2 * layers * model * model)
    return pl.pallas_call(
        functools.partial(cnn_kernel, widths=widths, filters=filters, ce=ce, length=length, layers=layers, nt=nt,
                          start=start),
        out_shape=jax.ShapeDtypeStruct((words, model), bf16),
        in_specs=[VM, VM, VM, VM, ANY, ANY, ANY],
        out_specs=VM,
        scratch_shapes=[
            pltpu.VMEM((words, (-(-length // SPAN) + 1) * LANES), bf16),
            pltpu.VMEM((2 * LANES, widths * SPAN * filters), bf16),
            pltpu.VMEM((words, widths * filters), f32),
            pltpu.VMEM((words, widths * filters), bf16),
            pltpu.VMEM(proj_weight.shape, bf16),
            pltpu.VMEM(gate_weight.shape, bf16),
            pltpu.VMEM(trans_weight.shape, bf16),
            pltpu.VMEM((words, model), bf16),
            pltpu.VMEM((words, model), bf16),
            pltpu.VMEM((LANES, LANES), f32),
            pltpu.SemaphoreType.DMA((3,)),
        ],
        compiler_params=params(),
        cost_estimate=pl.CostEstimate(flops=flops, bytes_accessed=12 << 20, transcendentals=words * 4096),
        name="embed",
    )(ids, tab_t, conv_weight, gate_bias, proj_weight, gate_weight, trans_weight)


def as_line(column):
    return jnp.broadcast_to(column, (LANES, LANES)).T[0:1, :]


def to_lines(column, out, at):
    for i in range(column.shape[0] // LANES):
        out[at + i:at + i + 1, :] = as_line(column[i * LANES:(i + 1) * LANES, :])


def aims(me_ref, hid, local):
    model = hid[0].shape[1] - LANES
    apart, place = [], []
    for h in hid:
        code = h[:, model:model + LANES].astype(f32).astype(jnp.int32)
        goal = code[:, 0:1] * 256 + code[:, 1:2]
        owner = lax.div(goal, local)
        apart.append(jnp.bitwise_xor(owner, me_ref[0]))
        place.append(goal - owner * local)
    return jnp.concatenate(apart, axis=0), jnp.concatenate(place, axis=0)


def spots(apart, place, meta):
    bits, start = meta
    return jnp.where(apart == bits, place - start, -1)


def scores_of(rows, words, metas, apart, place, score, prob):
    at, top, aim = 0, None, None
    for ref, meta in zip(words, metas):
        n = ref.shape[0]
        piece = lax.dot_general(rows[...], ref[...], (((1,), (1,)), ((), ())), preferred_element_type=f32)
        score[:, at:at + n] = piece
        lane = lax.broadcasted_iota(jnp.int32, piece.shape, 1)
        hit = jnp.sum(jnp.where(lane == spots(apart, place, meta), piece, 0.0), axis=1, keepdims=True)
        best = jnp.max(piece, axis=1, keepdims=True)
        top = best if top is None else jnp.maximum(top, best)
        aim = hit if aim is None else aim + hit
        at += n
    at, total = 0, None
    for ref in words:
        n = ref.shape[0]
        w = jnp.exp(score[:, at:at + n] - top).astype(bf16)
        prob[:, at:at + n] = w
        part = jnp.sum(w.astype(f32), axis=1, keepdims=True)
        total = part if total is None else total + part
        at += n
    return top, total, aim


def sums_of(words, metas, apart, place, prob, hot, out, target, before=None):
    at = 0
    for ref, meta in zip(words, metas):
        n = ref.shape[0]
        lane = lax.broadcasted_iota(jnp.int32, (prob.shape[0], n), 1)
        hot[:, at:at + n] = jnp.where(lane == spots(apart, place, meta), 1.0, 0.0).astype(bf16)
        at += n
    model = out.shape[1]
    for n in range(0, model, 256):
        at, res, aim = 0, None, None
        for ref in words:
            size = ref.shape[0]
            block = ref[:, n:n + 256]
            one = jnp.dot(prob[:, at:at + size], block, preferred_element_type=f32)
            two = jnp.dot(hot[:, at:at + size], block, preferred_element_type=f32)
            res = one if res is None else res + one
            aim = two if aim is None else aim + two
            at += size
        out[:, n:n + 256] = res
        if before is not None:
            aim = aim + before[:, n:n + 256].astype(f32)
        target[:, n:n + 256] = aim.astype(bf16)


def load_rows(hid, rows):
    at = 0
    for h in hid:
        rows[at:at + h.shape[0], :] = h[:, 0:rows.shape[1]]
        at += h.shape[0]


def first_kernel(me_ref, *refs, nh, metas, local):
    hid, words = refs[:nh], refs[nh:nh + len(metas)]
    out, target, stats, rows, score, prob, hot = refs[nh + len(metas):]
    load_rows(hid, rows)
    apart, place = aims(me_ref, hid, local)
    top, total, aim = scores_of(rows, words, metas, apart, place, score, prob)
    stats[:, 0:LANES] = jnp.broadcast_to(top, (top.shape[0], LANES))
    stats[:, LANES:2 * LANES] = jnp.broadcast_to(total, (top.shape[0], LANES))
    stats[:, 2 * LANES:3 * LANES] = jnp.broadcast_to(aim, (top.shape[0], LANES))
    sums_of(words, metas, apart, place, prob, hot, out, target)


def cost(flops, size, trans=0):
    return pl.CostEstimate(flops=flops, bytes_accessed=size, transcendentals=trans)


SM = pl.BlockSpec(memory_space=pltpu.SMEM)


def first_fold(me, hid, words, metas, local):
    model = words[0].shape[1]
    rows = sum(h.shape[0] for h in hid)
    count = sum(w.shape[0] for w in words)
    return pl.pallas_call(
        functools.partial(first_kernel, nh=len(hid), metas=metas, local=local),
        out_shape=[jax.ShapeDtypeStruct((rows, model), f32), jax.ShapeDtypeStruct((rows, model), bf16),
                   jax.ShapeDtypeStruct((rows, 3 * LANES), f32)],
        in_specs=[SM] + [VM] * (len(hid) + len(words)), out_specs=[VM] * 3,
        scratch_shapes=[pltpu.VMEM((rows, model), bf16), pltpu.VMEM((rows, count), f32),
                        pltpu.VMEM((rows, count), bf16), pltpu.VMEM((rows, count), bf16)],
        compiler_params=params(), cost_estimate=cost(6 * rows * count * model, 2 * (rows + count) * model),
        name="first_fold",
    )(me, *hid, *words)


def score_kernel(me_ref, *refs, nh, metas, local):
    hid, words = refs[:nh], refs[nh:nh + len(metas)]
    stats, prob, tops, lines, rows, score = refs[nh + len(metas):]
    load_rows(hid, rows)
    apart, place = aims(me_ref, hid, local)
    top2, total2, aim2 = scores_of(rows, words, metas, apart, place, score, prob)
    top1, total1 = stats[:, 0:1], stats[:, LANES:LANES + 1]
    top = jnp.maximum(top1, top2)
    total = jnp.exp(top1 - top) * total1 + jnp.exp(top2 - top) * total2
    tops[...] = jnp.broadcast_to(top2, tops.shape)
    to_lines(top + jnp.log(total), lines, 0)
    to_lines(stats[:, 2 * LANES:2 * LANES + 1] + aim2, lines, lines.shape[0] // 2)


def last_scores(me, hid, words, metas, local, stats):
    model = words[0].shape[1]
    rows = sum(h.shape[0] for h in hid)
    count = sum(w.shape[0] for w in words)
    return pl.pallas_call(
        functools.partial(score_kernel, nh=len(hid), metas=metas, local=local),
        out_shape=[jax.ShapeDtypeStruct((rows, count), bf16), jax.ShapeDtypeStruct((rows, LANES), f32),
                   jax.ShapeDtypeStruct((2 * rows // LANES, LANES), f32)],
        in_specs=[SM] + [VM] * (len(hid) + len(words) + 1), out_specs=[VM] * 3,
        scratch_shapes=[pltpu.VMEM((rows, model), bf16), pltpu.VMEM((rows, count), f32)],
        compiler_params=params(), cost_estimate=cost(2 * rows * count * model, 2 * (rows + count) * model),
        name="last_scores",
    )(me, *hid, *words, stats)


def sum_kernel(me_ref, *refs, nh, metas, local):
    hid, words = refs[:nh], refs[nh:nh + len(metas)]
    prob, before, out, target, hot = refs[nh + len(metas):]
    apart, place = aims(me_ref, hid, local)
    sums_of(words, metas, apart, place, prob, hot, out, target, before)


def last_sums(me, hid, words, metas, local, prob, before):
    rows, model = before.shape
    count = prob.shape[1]
    return pl.pallas_call(
        functools.partial(sum_kernel, nh=len(hid), metas=metas, local=local),
        out_shape=[jax.ShapeDtypeStruct((rows, model), f32), jax.ShapeDtypeStruct((rows, model), bf16)],
        in_specs=[SM] + [VM] * (len(hid) + len(words) + 2), out_specs=[VM] * 2,
        scratch_shapes=[pltpu.VMEM((rows, count), bf16)],
        compiler_params=params(), cost_estimate=cost(4 * rows * count * model, 2 * (rows + count) * model),
        name="last_sums",
    )(me, *hid, *words, prob, before)


def combine_kernel(*refs, flips):
    nl = len(flips)
    lines = refs[:nl]

    def value(j, i, kind):
        over, halves = flips[j]
        v = lines[j][kind * per + (i ^ over):kind * per + (i ^ over) + 1, :]
        return pltpu.roll(v, LANES // 2, axis=1) if halves else v

    one, two, target, stats, tops, a_keep, a_send, b_keep, b_send, loss = refs[nl:]
    per = lines[0].shape[0] // 2
    count, model = one.shape
    half, quarter = model // 2, count // 4
    for i in range(per):
        each = [value(j, i, 0) for j in range(nl)]
        top = each[0]
        for v in each[1:]:
            top = jnp.maximum(top, v)
        total = sum(jnp.exp(v - top) for v in each)
        aim = sum(value(j, i, 1) for j in range(nl))
        whole = top + jnp.log(total)
        if i == 0:
            loss[...] = whole - aim
        whole = jnp.broadcast_to(whole, (LANES, LANES)).T
        part = slice(i * LANES, (i + 1) * LANES)
        c1 = jnp.exp(stats[part, 0:LANES] - whole)
        c2 = jnp.exp(tops[part, :] - whole)
        q = i * LANES // quarter
        at = i * LANES - q * quarter
        a, b = (a_keep, a_send)[q // 2], (b_keep, b_send)[q % 2]
        a_at, b_at = (q % 2) * quarter + at, (q // 2) * quarter + at
        for n in range(0, model, LANES):
            cols = slice(n, n + LANES)
            mix = (c1 * one[part, cols] + c2 * two[part, cols] - target[part, cols].astype(f32)).astype(bf16)
            if n < half:
                a[a_at:a_at + LANES, cols] = mix
            else:
                b[b_at:b_at + LANES, n - half:n - half + LANES] = mix


def combine(lines, flips, one, two, target, stats, tops):
    rows, model = one.shape
    side = jax.ShapeDtypeStruct((rows // 2, model // 2), bf16)
    return pl.pallas_call(
        functools.partial(combine_kernel, flips=flips),
        out_shape=[side] * 4 + [jax.ShapeDtypeStruct((1, LANES), f32)],
        in_specs=[VM] * (len(lines) + 5), out_specs=[VM] * 5,
        compiler_params=params(), cost_estimate=cost(8 * rows * model, 12 * rows * model), name="combine",
    )(*lines, one, two, target, stats, tops)


def plus(a, b):
    return (a.astype(f32) + b.astype(f32)).astype(bf16)


def add_kernel(*refs):
    n = len(refs) // 4
    for i in range(n):
        keep, got = refs[2 * i:2 * i + 2]
        first, second = refs[2 * n + 2 * i:2 * n + 2 * i + 2]
        rows = first.shape[0]
        first[...] = plus(keep[0:rows, :], got[0:rows, :])
        second[...] = plus(keep[rows:2 * rows, :], got[rows:2 * rows, :])


def add_halves(*pairs):
    outs = [jax.ShapeDtypeStruct((p.shape[0] // 2, p.shape[1]), bf16) for p in pairs]
    return pl.pallas_call(
        add_kernel, out_shape=outs, in_specs=[VM] * len(pairs), out_specs=[VM] * len(pairs),
        compiler_params=params(), cost_estimate=cost(pairs[0].size, 8 * pairs[0].size), name="add_halves",
    )(*pairs)


def add_across_kernel(a_keep, a_got, b_keep, b_got, first, second):
    rows, half = first.shape[0], a_keep.shape[1]
    for c, (keep, got) in enumerate(((a_keep, a_got), (b_keep, b_got))):
        cols = slice(c * half, (c + 1) * half)
        first[:, cols] = plus(keep[0:rows, :], got[0:rows, :])
        second[:, cols] = plus(keep[rows:2 * rows, :], got[rows:2 * rows, :])


def add_across(a_keep, a_got, b_keep, b_got):
    rows, half = a_keep.shape
    return pl.pallas_call(
        add_across_kernel, out_shape=[jax.ShapeDtypeStruct((rows // 2, 2 * half), bf16)] * 2,
        in_specs=[VM] * 4, out_specs=[VM] * 2,
        compiler_params=params(), cost_estimate=cost(2 * rows * half, 12 * rows * half), name="add_across",
    )(a_keep, a_got, b_keep, b_got)


def per_device(char_ids, char_table, conv_weight, proj_weight, gate_weight, trans_weight, gate_bias, hidden, targets,
               *, vocab, blk):
    devices = vocab * blk
    axes = ("vocab", "blk")

    def swap(x, bits):
        return lax.ppermute(x, axes, [(i, i ^ bits) for i in range(devices)])

    core, near = blk, 1
    bit_a, bit_b = 2 * blk, 4 * blk
    rest = [1 << i for i in range(1, blk.bit_length() - 1)] + [
        blk << i for i in range(3, vocab.bit_length() - 1)]
    me = lax.axis_index("vocab") * blk + lax.axis_index("blk")
    local, length = char_ids.shape
    mine = hidden.shape[0]

    goal = targets.reshape(mine, 1)
    code = jnp.concatenate([goal // 256, goal % 256], axis=1).astype(bf16)
    rows = jnp.concatenate([hidden, code, jnp.zeros((mine, LANES - 2), bf16)], axis=1)
    for bit in rest:
        rows = jnp.concatenate([rows, swap(rows, bit)], axis=0)

    tab_t = char_table.T.astype(f32)
    weights = (tab_t, conv_weight, proj_weight, gate_weight, trans_weight, gate_bias)
    sizes = (local // 2, local // 2)
    pieces, marks, start = [], [], 0
    for i, size in enumerate(sizes):
        pieces.append(embed(char_ids, length, start, size, *weights))
        marks.append(start)
        start += size
    hid = [rows] + [swap(rows, b) for b in (bit_b, bit_a, bit_a | bit_b)]
    cores = [swap(e, core) for e in pieces]
    nears = [swap(e, near) for e in pieces]
    fars = [swap(e, core) for e in nears]

    me = me.astype(jnp.int32).reshape(1)
    meta = [tuple((bits, m) for m in marks) for bits in (0, core, near, core | near)]
    late = 1 if 4 * hid[0].shape[0] <= local else len(nears)
    one, target, stats = first_fold(
        me, hid, pieces + cores + nears[:-late] + fars[:-late],
        meta[0] + meta[1] + meta[2][:-late] + meta[3][:-late], local)
    words, metas = nears[-late:] + fars[-late:], meta[2][-late:] + meta[3][-late:]
    prob, tops, line = last_scores(me, hid, words, metas, local, stats)
    bits = [bit_a, bit_b] + rest
    others = [sum(b for j, b in enumerate(bits) if k >> j & 1) for k in range(1, 1 << len(bits))]
    order = rest + [bit_b, bit_a]
    flips = tuple((sum(1 << (j - 1) for j, b in enumerate(order) if j and o & b), bool(o & rest[0])) for o in others)
    lines = [swap(line, o) for o in others]
    two, target = last_sums(me, hid, words, metas, local, prob, target)
    a_keep, a_send, b_keep, b_send, loss = combine([line] + lines, ((0, False),) + flips, one, two, target, stats, tops)
    a_keep, a_send, b_keep, b_send = add_halves(a_keep, swap(a_send, bit_a), b_keep, swap(b_send, bit_b))
    keep, send = add_across(a_keep, swap(a_send, bit_b), b_keep, swap(b_send, bit_a))
    for bit in rest[:0:-1]:
        keep, send = add_halves(keep, swap(send, bit))
    grad = plus(keep, swap(send, rest[0]))
    return loss[0, :mine], grad


def solution(mesh):
    words = P(("vocab", "blk"))
    return jax.shard_map(
        functools.partial(per_device, vocab=mesh.shape["vocab"], blk=mesh.shape["blk"]),
        mesh=mesh,
        in_specs=(P(("vocab", "blk"), None), P(), P(), P(), P(), P(), P(), P(("vocab", "blk"), None), words),
        out_specs=(words, P(("vocab", "blk"), None)),
        check_vma=False,
    )
```

```python
import functools
import jax
import jax.numpy as jnp
from jax import lax
from jax.experimental import pallas as pl
from jax.experimental.pallas import tpu as pltpu
from jax.sharding import PartitionSpec as P

bf16=jnp.bfloat16; f32=jnp.float32
LANES = 128
SPAN = 8


def prep_toeplitz(conv_ref, toep, ce, widths, filters):
    depth = toep.shape[0]
    for k in range(widths):
        rows = (k + 1) * ce
        piece = conv_ref[0:rows, k * filters:(k + 1) * filters]
        for o in range(SPAN):
            cols = slice((k * SPAN + o) * filters, (k * SPAN + o + 1) * filters)
            if o:
                toep[0:o * ce, cols] = jnp.zeros((o * ce, filters), bf16)
            toep[o * ce:o * ce + rows, cols] = piece
            rest = depth - o * ce - rows
            if rest:
                toep[o * ce + rows:depth, cols] = jnp.zeros((rest, filters), bf16)

def lookup(ids_ref, start, words, tab_ref, vec, length, ce):
    per = LANES // ce
    low_tab = tab_ref[:, 0:LANES].astype(f32)
    top_tab = tab_ref[:, LANES:2 * LANES].astype(f32)
    for at in range(0, words, LANES):
        for g in range(vec.shape[1] // LANES):
            parts = []
            for q in range(per):
                p = g * per + q
                if p >= length:
                    parts.append(jnp.zeros((ce, LANES), f32))
                    continue
                idx = jnp.broadcast_to(ids_ref[p:p + 1, start + at:start + at + LANES], (8, LANES))
                low = jnp.bitwise_and(idx, LANES - 1)
                top = idx >= LANES
                for h in range(0, ce, 8):
                    one = jnp.take_along_axis(low_tab[h:h + 8], low, axis=1)
                    two = jnp.take_along_axis(top_tab[h:h + 8], low, axis=1)
                    parts.append(jnp.where(top, two, one))
            block = jnp.concatenate(parts, axis=0)
            vec[at:at + LANES, g * LANES:(g + 1) * LANES] = block.T.astype(bf16)


def conv_pool(vec, toep, acc, length, widths, filters):
    words = vec.shape[0]
    def tile(b, k, o, lhs):
        cols = slice((k * SPAN + o) * filters, (k * SPAN + o + 2) * filters)
        return jnp.dot(lhs, toep[:, cols], preferred_element_type=f32)
    acc[...] = jnp.full(acc.shape, -jnp.inf, f32)
    least = (length - widths + 1) // SPAN
    def body(b, _):
        lhs = vec[:, pl.ds(pl.multiple_of(b * LANES, LANES), 2 * LANES)]
        for k in range(widths):
            best = acc[:, k * filters:(k + 1) * filters]
            for o in range(0, SPAN, 2):
                r = tile(b, k, o, lhs)
                best = jnp.maximum(best, jnp.maximum(r[:, :filters], r[:, filters:]))
            acc[:, k * filters:(k + 1) * filters] = best
        return 0
    lax.fori_loop(0, least, body, 0)
    for b in range(least, -(-length // SPAN)):
        lhs = vec[:, b * LANES:(b + 2) * LANES]
        for k in range(widths):
            usable = min(SPAN, length - k - b * SPAN)
            if usable <= 0: continue
            best = acc[:, k * filters:(k + 1) * filters]
            for o in range(0, usable, 2):
                r = tile(b, k, o, lhs)
                best = jnp.maximum(best, r[:, :filters])
                if o + 1 < usable:
                    best = jnp.maximum(best, r[:, filters:])
            acc[:, k * filters:(k + 1) * filters] = best

def cnn_kernel(ids_ref, tab_ref, conv_ref, bias_ref, proj_hbm, gate_hbm, trans_hbm, *rest,
               widths, filters, ce, length, layers, nt, start):
    out_ref, vec, toep, acc, feat, proj, gate, trans, state, last, sems = rest
    copies = [pltpu.make_async_copy(s, d, sems.at[i]) for i, (s, d) in enumerate(
        ((proj_hbm, proj), (gate_hbm, gate), (trans_hbm, trans)))]
    for c in copies:
        c.start()
    words = out_ref.shape[0]
    prep_toeplitz(conv_ref, toep, ce, widths, filters)
    lookup(ids_ref, start, words, tab_ref, vec, length, ce)
    conv_pool(vec, toep, acc, length, widths, filters)
    for c in copies:
        c.wait()
    feat[...] = jnp.tanh(acc[...]).astype(bf16)
    model = last.shape[1]
    for n in range(0, model, nt):
        state[:, n:n + nt] = jnp.dot(feat[...], proj[:, n:n + nt], preferred_element_type=f32).astype(bf16)
    for l in range(layers):
        for n in range(0, model, nt):
            cur = state[...]
            g = jnp.dot(cur, gate[l, :, n:n + nt], preferred_element_type=f32) + bias_ref[l:l + 1, n:n + nt]
            t = jnp.dot(cur, trans[l, :, n:n + nt], preferred_element_type=f32)
            opened = jax.nn.sigmoid(g)
            carried = jnp.maximum(t, 0.0)
            new = (opened * carried + (1.0 - opened) * state[:, n:n + nt].astype(f32)).astype(bf16)
            if l + 1 < layers:
                last[:, n:n + nt] = new
            else:
                out_ref[:, n:n + nt] = new
        if l + 1 < layers:
            state[...] = last[...]


ANY = pl.BlockSpec(memory_space=pl.ANY)
VM = pl.BlockSpec(memory_space=pltpu.VMEM)


def params(limit_mib=56):
    return pltpu.CompilerParams(vmem_limit_bytes=limit_mib << 20)


def embed(ids, length, start, words, tab_t, conv_weight, proj_weight, gate_weight, trans_weight, gate_bias, nt=256):
    ce = tab_t.shape[0]
    widths = conv_weight.shape[0] // ce
    filters = conv_weight.shape[1] // widths
    layers, model, _ = gate_weight.shape
    flops = 2 * words * (length * 256 * widths * filters + widths * filters * model + 2 * layers * model * model)
    return pl.pallas_call(
        functools.partial(cnn_kernel, widths=widths, filters=filters, ce=ce, length=length, layers=layers, nt=nt,
                          start=start),
        out_shape=jax.ShapeDtypeStruct((words, model), bf16),
        in_specs=[VM, VM, VM, VM, ANY, ANY, ANY],
        out_specs=VM,
        scratch_shapes=[
            pltpu.VMEM((words, (-(-length // SPAN) + 1) * LANES), bf16),
            pltpu.VMEM((2 * LANES, widths * SPAN * filters), bf16),
            pltpu.VMEM((words, widths * filters), f32),
            pltpu.VMEM((words, widths * filters), bf16),
            pltpu.VMEM(proj_weight.shape, bf16),
            pltpu.VMEM(gate_weight.shape, bf16),
            pltpu.VMEM(trans_weight.shape, bf16),
            pltpu.VMEM((words, model), bf16),
            pltpu.VMEM((words, model), bf16),
            pltpu.SemaphoreType.DMA((3,)),
        ],
        compiler_params=params(),
        cost_estimate=pl.CostEstimate(flops=flops, bytes_accessed=12 << 20, transcendentals=words * 4096),
        name="embed",
    )(ids, tab_t, conv_weight, gate_bias, proj_weight, gate_weight, trans_weight)


def as_line(column):
    return jnp.broadcast_to(column, (LANES, LANES)).T[0:1, :]


def to_lines(column, out, at):
    for i in range(column.shape[0] // LANES):
        out[at + i:at + i + 1, :] = as_line(column[i * LANES:(i + 1) * LANES, :])


def aims(me_ref, hid, local):
    model = hid[0].shape[1] - LANES
    apart, place = [], []
    for h in hid:
        code = h[:, model:model + LANES].astype(f32).astype(jnp.int32)
        goal = code[:, 0:1] * 256 + code[:, 1:2]
        owner = lax.div(goal, local)
        apart.append(jnp.bitwise_xor(owner, me_ref[0]))
        place.append(goal - owner * local)
    return jnp.concatenate(apart, axis=0), jnp.concatenate(place, axis=0)


def spots(apart, place, meta):
    bits, start = meta
    return jnp.where(apart == bits, place - start, -1)


def scores_of(rows, words, score, prob):
    at, top = 0, None
    for ref in words:
        n = ref.shape[0]
        piece = lax.dot_general(rows[...], ref[...], (((1,), (1,)), ((), ())), preferred_element_type=f32)
        score[:, at:at + n] = piece
        best = jnp.max(piece, axis=1, keepdims=True)
        top = best if top is None else jnp.maximum(top, best)
        at += n
    at, total = 0, None
    for ref in words:
        n = ref.shape[0]
        w = jnp.exp(score[:, at:at + n] - top).astype(bf16)
        prob[:, at:at + n] = w
        part = jnp.sum(w.astype(f32), axis=1, keepdims=True)
        total = part if total is None else total + part
        at += n
    return top, total


def hot_words(words, metas, apart, place, hot):
    at = 0
    for ref, meta in zip(words, metas):
        n = ref.shape[0]
        lane = lax.broadcasted_iota(jnp.int32, (hot.shape[0], n), 1)
        hot[:, at:at + n] = jnp.where(lane == spots(apart, place, meta), 1.0, 0.0).astype(bf16)
        at += n


def product(left, words, n, size):
    at, res = 0, None
    for ref in words:
        count = ref.shape[0]
        d = jnp.dot(left[:, at:at + count], ref[:, n:n + size], preferred_element_type=f32)
        res = d if res is None else res + d
        at += count
    return res


def load_rows(hid, rows):
    at = 0
    for h in hid:
        rows[at:at + h.shape[0], :] = h[:, 0:rows.shape[1]]
        at += h.shape[0]


def first_kernel(me_ref, *refs, nh, metas, local):
    hid, words = refs[:nh], refs[nh:nh + len(metas)]
    out, target, stats, rows, score, prob, hot = refs[nh + len(metas):]
    load_rows(hid, rows)
    top, total = scores_of(rows, words, score, prob)
    stats[:, 0:LANES] = jnp.broadcast_to(top, (top.shape[0], LANES))
    stats[:, LANES:2 * LANES] = jnp.broadcast_to(total, (top.shape[0], LANES))
    hot_words(words, metas, *aims(me_ref, hid, local), hot)
    for n in range(0, out.shape[1], 256):
        out[:, n:n + 256] = product(prob, words, n, 256)
        target[:, n:n + 256] = product(hot, words, n, 256).astype(bf16)


def cost(flops, size, trans=0):
    return pl.CostEstimate(flops=flops, bytes_accessed=size, transcendentals=trans)


SM = pl.BlockSpec(memory_space=pltpu.SMEM)


def first_fold(me, hid, words, metas, local):
    model = words[0].shape[1]
    rows = sum(h.shape[0] for h in hid)
    count = sum(w.shape[0] for w in words)
    return pl.pallas_call(
        functools.partial(first_kernel, nh=len(hid), metas=metas, local=local),
        out_shape=[jax.ShapeDtypeStruct((rows, model), f32), jax.ShapeDtypeStruct((rows, model), bf16),
                   jax.ShapeDtypeStruct((rows, 2 * LANES), f32)],
        in_specs=[SM] + [VM] * (len(hid) + len(words)), out_specs=[VM] * 3,
        scratch_shapes=[pltpu.VMEM((rows, model), bf16), pltpu.VMEM((rows, count), f32),
                        pltpu.VMEM((rows, count), bf16), pltpu.VMEM((rows, count), bf16)],
        compiler_params=params(), cost_estimate=cost(6 * rows * count * model, 2 * (rows + count) * model),
        name="first_fold",
    )(me, *hid, *words)


def last_kernel(me_ref, *refs, nh, metas, group, local):
    hid, words = refs[:nh], refs[nh:nh + len(metas)]
    own, one, before, stats, value, target, facts, lines, rows, score, prob, hot = refs[nh + len(metas):]
    load_rows(hid, rows)
    count, model = one.shape
    apart, place = aims(me_ref, hid, local)
    top2, total2 = scores_of(rows, words, score, prob)
    hot_words(words, metas, apart, place, hot)
    top1, total1 = stats[:, 0:1], stats[:, LANES:LANES + 1]
    top = jnp.maximum(top1, top2)
    s1, s2 = jnp.exp(top1 - top), jnp.exp(top2 - top)
    total = s1 * total1 + s2 * total2
    s1, s2 = s1 / total, s2 / total
    whole = top + jnp.log(total)
    centre = jnp.sum(own[0:LANES, :].astype(f32), axis=0, keepdims=True) * (1.0 / LANES)
    aim = None
    for n in range(0, model, 256):
        cols = slice(n, n + 256)
        mix = s1 * one[:, cols] + s2 * product(prob, words, n, 256)
        value[:, cols] = (mix - centre[:, cols]).astype(bf16)
        goal = product(hot, words, n, 256) + before[:, cols].astype(f32)
        target[:, cols] = goal.astype(bf16)
        part = jnp.sum(goal * rows[:, cols].astype(f32), axis=1, keepdims=True)
        aim = part if aim is None else aim + part
    inside = sum(jnp.where(apart == bits, 1.0, 0.0) for bits in group)
    facts[:, 0:LANES] = jnp.broadcast_to(whole, (count, LANES))
    facts[:, LANES:2 * LANES] = jnp.broadcast_to(inside, (count, LANES))
    per = count // LANES
    to_lines(whole, lines, 0)
    to_lines(aim, lines, per)
    for n in range(model // LANES):
        lines[2 * per + n:2 * per + n + 1, :] = centre[:, n * LANES:(n + 1) * LANES]


def last_fold(me, hid, words, metas, group, local, own, one, before, stats):
    rows, model = one.shape
    count = sum(w.shape[0] for w in words)
    return pl.pallas_call(
        functools.partial(last_kernel, nh=len(hid), metas=metas, group=group, local=local),
        out_shape=[jax.ShapeDtypeStruct((rows, model), bf16)] * 2 + [
            jax.ShapeDtypeStruct((rows, 2 * LANES), f32),
            jax.ShapeDtypeStruct((2 * rows // LANES + model // LANES, LANES), f32)],
        in_specs=[SM] + [VM] * (len(hid) + len(words) + 4), out_specs=[VM] * 4,
        scratch_shapes=[pltpu.VMEM((rows, model), bf16), pltpu.VMEM((rows, count), f32),
                        pltpu.VMEM((rows, count), bf16), pltpu.VMEM((rows, count), bf16)],
        compiler_params=params(), cost_estimate=cost(6 * rows * count * model, 2 * (rows + count) * model),
        name="last_fold",
    )(me, *hid, *words, own, one, before, stats)


def combine_kernel(*refs, flips):
    nl = len(flips)
    lines = refs[:nl]
    value, target, facts, a_keep, a_send, b_keep, b_send, loss = refs[nl:]
    count, model = value.shape
    per = count // LANES
    half, quarter = model // 2, count // 4

    def line(j, i, kind):
        over, halves = flips[j]
        v = lines[j][kind * per + (i ^ over):kind * per + (i ^ over) + 1, :]
        return pltpu.roll(v, LANES // 2, axis=1) if halves else v

    mus, shifts = [], []
    for n in range(model // LANES):
        row = slice(2 * per + n, 2 * per + n + 1)
        mu = sum(ref[row, :] for ref in lines) * (1.0 / nl)
        mus.append(jnp.broadcast_to(mu, (LANES, LANES)))
        shifts.append(jnp.broadcast_to(lines[0][row, :] - mu, (LANES, LANES)))
    for i in range(per):
        each = [line(j, i, 0) for j in range(nl)]
        top = functools.reduce(jnp.maximum, each)
        whole = top + jnp.log(sum(jnp.exp(v - top) for v in each))
        if i == 0:
            loss[...] = whole - sum(line(j, i, 1) for j in range(nl))
        whole = jnp.broadcast_to(whole, (LANES, LANES)).T
        part = slice(i * LANES, (i + 1) * LANES)
        weight = jnp.exp(facts[part, 0:LANES] - whole)
        inside = facts[part, LANES:2 * LANES]
        q = i * LANES // quarter
        at = i * LANES - q * quarter
        a, b = (a_keep, a_send)[q // 2], (b_keep, b_send)[q % 2]
        a_at, b_at = (q % 2) * quarter + at, (q // 2) * quarter + at
        for n in range(model // LANES):
            cols = slice(n * LANES, (n + 1) * LANES)
            mix = weight * (value[part, cols].astype(f32) + shifts[n])
            mix = (mix - (target[part, cols].astype(f32) - inside * mus[n])).astype(bf16)
            if n * LANES < half:
                a[a_at:a_at + LANES, cols] = mix
            else:
                b[b_at:b_at + LANES, n * LANES - half:(n + 1) * LANES - half] = mix


def combine(lines, flips, value, target, facts):
    rows, model = value.shape
    side = jax.ShapeDtypeStruct((rows // 2, model // 2), bf16)
    return pl.pallas_call(
        functools.partial(combine_kernel, flips=flips),
        out_shape=[side] * 4 + [jax.ShapeDtypeStruct((1, LANES), f32)],
        in_specs=[VM] * (len(lines) + 3), out_specs=[VM] * 5,
        compiler_params=params(), cost_estimate=cost(8 * rows * model, 8 * rows * model), name="combine",
    )(*lines, value, target, facts)


def plus(a, b):
    return (a.astype(f32) + b.astype(f32)).astype(bf16)


def add_kernel(*refs):
    n = len(refs) // 4
    for i in range(n):
        keep, got = refs[2 * i:2 * i + 2]
        first, second = refs[2 * n + 2 * i:2 * n + 2 * i + 2]
        rows = first.shape[0]
        first[...] = plus(keep[0:rows, :], got[0:rows, :])
        second[...] = plus(keep[rows:2 * rows, :], got[rows:2 * rows, :])


def add_halves(*pairs):
    outs = [jax.ShapeDtypeStruct((p.shape[0] // 2, p.shape[1]), bf16) for p in pairs]
    return pl.pallas_call(
        add_kernel, out_shape=outs, in_specs=[VM] * len(pairs), out_specs=[VM] * len(pairs),
        compiler_params=params(), cost_estimate=cost(pairs[0].size, 8 * pairs[0].size), name="add_halves",
    )(*pairs)


def add_across_kernel(a_keep, a_got, b_keep, b_got, first, second):
    rows, half = first.shape[0], a_keep.shape[1]
    for c, (keep, got) in enumerate(((a_keep, a_got), (b_keep, b_got))):
        cols = slice(c * half, (c + 1) * half)
        first[:, cols] = plus(keep[0:rows, :], got[0:rows, :])
        second[:, cols] = plus(keep[rows:2 * rows, :], got[rows:2 * rows, :])


def add_across(a_keep, a_got, b_keep, b_got):
    rows, half = a_keep.shape
    return pl.pallas_call(
        add_across_kernel, out_shape=[jax.ShapeDtypeStruct((rows // 2, 2 * half), bf16)] * 2,
        in_specs=[VM] * 4, out_specs=[VM] * 2,
        compiler_params=params(), cost_estimate=cost(2 * rows * half, 12 * rows * half), name="add_across",
    )(a_keep, a_got, b_keep, b_got)


def per_device(char_ids, char_table, conv_weight, proj_weight, gate_weight, trans_weight, gate_bias, hidden, targets,
               *, vocab, blk):
    devices = vocab * blk
    axes = ("vocab", "blk")

    def swap(x, bits):
        return lax.ppermute(x, axes, [(i, i ^ bits) for i in range(devices)])

    core, near = blk, 1
    bit_a, bit_b = 2 * blk, 4 * blk
    rest = [1 << i for i in range(1, blk.bit_length() - 1)] + [
        blk << i for i in range(3, vocab.bit_length() - 1)]
    me = lax.axis_index("vocab") * blk + lax.axis_index("blk")
    local, length = char_ids.shape
    mine = hidden.shape[0]

    rows, goal = hidden, targets.reshape(1, mine)
    for bit in rest:
        rows = jnp.concatenate([rows, swap(rows, bit)], axis=0)
        goal = jnp.concatenate([goal, swap(goal, bit)], axis=1)
    goal = goal.reshape(-1, 1)
    code = jnp.concatenate([goal // 256, goal % 256], axis=1).astype(bf16)
    rows = jnp.concatenate([rows, jnp.pad(code, ((0, 0), (0, LANES - 2)))], axis=1)

    weights = (char_table.T, conv_weight, proj_weight, gate_weight, trans_weight, gate_bias)
    size = local // 2
    marks = (0, size)
    ids = char_ids.T
    e0 = embed(ids, length, 0, size, *weights)
    hid = [rows] + [swap(rows, b) for b in (bit_b, bit_a, bit_a | bit_b)]
    e1 = embed(ids, length, size, size, *weights)
    held, *hid = lax.optimization_barrier((e1, *hid))
    pieces = [e0, held]
    cores = [swap(e, core) for e in pieces]
    nears = [swap(e, near) for e in pieces]
    fars = [swap(e, core) for e in nears]

    me = me.astype(jnp.int32).reshape(1)
    meta = [tuple((bits, m) for m in marks) for bits in (0, core, near, core | near)]
    late = 1 if 4 * hid[0].shape[0] <= local else len(nears)
    one, target, stats = first_fold(
        me, hid, pieces + cores + nears[:-late] + fars[:-late],
        meta[0] + meta[1] + meta[2][:-late] + meta[3][:-late], local)
    words, metas = nears[-late:] + fars[-late:], meta[2][-late:] + meta[3][-late:]
    value, target, facts, line = last_fold(
        me, hid, words, metas, (0, core, near, core | near), local, e0, one, target, stats)
    bits = [bit_a, bit_b] + rest
    others = [sum(b for j, b in enumerate(bits) if k >> j & 1) for k in range(1, 1 << len(bits))]
    order = rest + [bit_b, bit_a]
    flips = tuple((sum(1 << (j - 1) for j, b in enumerate(order) if j and o & b), bool(o & rest[0])) for o in others)
    lines = [swap(line, o) for o in others]
    a_keep, a_send, b_keep, b_send, loss = combine([line] + lines, ((0, False),) + flips, value, target, facts)
    a_keep, a_send, b_keep, b_send = add_halves(a_keep, swap(a_send, bit_a), b_keep, swap(b_send, bit_b))
    keep, send = add_across(a_keep, swap(a_send, bit_b), b_keep, swap(b_send, bit_a))
    for bit in rest[:0:-1]:
        keep, send = add_halves(keep, swap(send, bit))
    grad = plus(keep, swap(send, rest[0]))
    return loss[0, :mine], grad


def solution(mesh):
    words = P(("vocab", "blk"))
    return jax.shard_map(
        functools.partial(per_device, vocab=mesh.shape["vocab"], blk=mesh.shape["blk"]),
        mesh=mesh,
        in_specs=(P(("vocab", "blk"), None), P(), P(), P(), P(), P(), P(), P(("vocab", "blk"), None), words),
        out_specs=(words, P(("vocab", "blk"), None)),
        check_vma=False,
    )
```

```python
import functools
import jax
import jax.numpy as jnp
from jax import lax
from jax.experimental import pallas as pl
from jax.experimental.pallas import tpu as pltpu
from jax.sharding import PartitionSpec as P

bf16=jnp.bfloat16; f32=jnp.float32
LANES = 128
SPAN = 8


def prep_toeplitz(conv_ref, toep, ce, widths, filters):
    depth = toep.shape[0]
    for k in range(widths):
        rows = (k + 1) * ce
        piece = conv_ref[0:rows, k * filters:(k + 1) * filters]
        for o in range(SPAN):
            cols = slice((k * SPAN + o) * filters, (k * SPAN + o + 1) * filters)
            if o:
                toep[0:o * ce, cols] = jnp.zeros((o * ce, filters), bf16)
            toep[o * ce:o * ce + rows, cols] = piece
            rest = depth - o * ce - rows
            if rest:
                toep[o * ce + rows:depth, cols] = jnp.zeros((rest, filters), bf16)

def lookup(ids_ref, start, words, tab_ref, vec, length, ce):
    per = LANES // ce
    low_tab = tab_ref[:, 0:LANES].astype(f32)
    top_tab = tab_ref[:, LANES:2 * LANES].astype(f32)
    first = start // LANES * LANES
    for tile in range(first, start + words, LANES):
        low_word, high_word = max(tile, start), min(tile + LANES, start + words)
        for g in range(vec.shape[1] // LANES):
            parts = []
            for q in range(per):
                p = g * per + q
                if p >= length:
                    parts.append(jnp.zeros((ce, LANES), f32))
                    continue
                idx = jnp.broadcast_to(ids_ref[p:p + 1, tile:tile + LANES], (8, LANES))
                low = jnp.bitwise_and(idx, LANES - 1)
                top = idx >= LANES
                for h in range(0, ce, 8):
                    one = jnp.take_along_axis(low_tab[h:h + 8], low, axis=1)
                    two = jnp.take_along_axis(top_tab[h:h + 8], low, axis=1)
                    parts.append(jnp.where(top, two, one))
            block = jnp.concatenate(parts, axis=0).T.astype(bf16)
            vec[low_word - start:high_word - start, g * LANES:(g + 1) * LANES] = block[low_word - tile:high_word - tile]


def conv_pool(vec, toep, acc, length, widths, filters):
    words = vec.shape[0]
    def tile(b, k, o, lhs):
        cols = slice((k * SPAN + o) * filters, (k * SPAN + o + 2) * filters)
        return jnp.dot(lhs, toep[:, cols], preferred_element_type=f32)
    acc[...] = jnp.full(acc.shape, -jnp.inf, f32)
    least = (length - widths + 1) // SPAN
    def body(b, _):
        lhs = vec[:, pl.ds(pl.multiple_of(b * LANES, LANES), 2 * LANES)]
        for k in range(widths):
            best = acc[:, k * filters:(k + 1) * filters]
            for o in range(0, SPAN, 2):
                r = tile(b, k, o, lhs)
                best = jnp.maximum(best, jnp.maximum(r[:, :filters], r[:, filters:]))
            acc[:, k * filters:(k + 1) * filters] = best
        return 0
    lax.fori_loop(0, least, body, 0)
    for b in range(least, -(-length // SPAN)):
        lhs = vec[:, b * LANES:(b + 2) * LANES]
        for k in range(widths):
            usable = min(SPAN, length - k - b * SPAN)
            if usable <= 0: continue
            best = acc[:, k * filters:(k + 1) * filters]
            for o in range(0, usable, 2):
                r = tile(b, k, o, lhs)
                best = jnp.maximum(best, r[:, :filters])
                if o + 1 < usable:
                    best = jnp.maximum(best, r[:, filters:])
            acc[:, k * filters:(k + 1) * filters] = best

def cnn_kernel(ids_ref, tab_ref, conv_ref, bias_ref, proj_hbm, gate_hbm, trans_hbm, *rest,
               widths, filters, ce, length, layers, nt, start):
    out_ref, vec, toep, acc, feat, proj, gate, trans, state, last, sems = rest
    copies = [pltpu.make_async_copy(s, d, sems.at[i]) for i, (s, d) in enumerate(
        ((proj_hbm, proj), (gate_hbm, gate), (trans_hbm, trans)))]
    for c in copies:
        c.start()
    words = out_ref.shape[0]
    prep_toeplitz(conv_ref, toep, ce, widths, filters)
    lookup(ids_ref, start, words, tab_ref, vec, length, ce)
    conv_pool(vec, toep, acc, length, widths, filters)
    for c in copies:
        c.wait()
    feat[...] = jnp.tanh(acc[...]).astype(bf16)
    model = last.shape[1]
    for n in range(0, model, nt):
        state[:, n:n + nt] = jnp.dot(feat[...], proj[:, n:n + nt], preferred_element_type=f32).astype(bf16)
    for l in range(layers):
        for n in range(0, model, nt):
            cur = state[...]
            g = jnp.dot(cur, gate[l, :, n:n + nt], preferred_element_type=f32) + bias_ref[l:l + 1, n:n + nt]
            t = jnp.dot(cur, trans[l, :, n:n + nt], preferred_element_type=f32)
            opened = jax.nn.sigmoid(g)
            carried = jnp.maximum(t, 0.0)
            new = (opened * carried + (1.0 - opened) * state[:, n:n + nt].astype(f32)).astype(bf16)
            if l + 1 < layers:
                last[:, n:n + nt] = new
            else:
                out_ref[:, n:n + nt] = new
        if l + 1 < layers:
            state[...] = last[...]


ANY = pl.BlockSpec(memory_space=pl.ANY)
VM = pl.BlockSpec(memory_space=pltpu.VMEM)


def params(limit_mib=56):
    return pltpu.CompilerParams(vmem_limit_bytes=limit_mib << 20)


def embed(ids, length, start, words, tab_t, conv_weight, proj_weight, gate_weight, trans_weight, gate_bias, nt=256):
    ce = tab_t.shape[0]
    widths = conv_weight.shape[0] // ce
    filters = conv_weight.shape[1] // widths
    layers, model, _ = gate_weight.shape
    flops = 2 * words * (length * 256 * widths * filters + widths * filters * model + 2 * layers * model * model)
    return pl.pallas_call(
        functools.partial(cnn_kernel, widths=widths, filters=filters, ce=ce, length=length, layers=layers, nt=nt,
                          start=start),
        out_shape=jax.ShapeDtypeStruct((words, model), bf16),
        in_specs=[VM, VM, VM, VM, ANY, ANY, ANY],
        out_specs=VM,
        scratch_shapes=[
            pltpu.VMEM((words, (-(-length // SPAN) + 1) * LANES), bf16),
            pltpu.VMEM((2 * LANES, widths * SPAN * filters), bf16),
            pltpu.VMEM((words, widths * filters), f32),
            pltpu.VMEM((words, widths * filters), bf16),
            pltpu.VMEM(proj_weight.shape, bf16),
            pltpu.VMEM(gate_weight.shape, bf16),
            pltpu.VMEM(trans_weight.shape, bf16),
            pltpu.VMEM((words, model), bf16),
            pltpu.VMEM((words, model), bf16),
            pltpu.SemaphoreType.DMA((3,)),
        ],
        compiler_params=params(),
        cost_estimate=pl.CostEstimate(flops=flops, bytes_accessed=12 << 20, transcendentals=words * 4096),
        name="embed",
    )(ids, tab_t, conv_weight, gate_bias, proj_weight, gate_weight, trans_weight)


def as_line(column):
    return jnp.broadcast_to(column, (LANES, LANES)).T[0:1, :]


def to_lines(column, out, at):
    for i in range(column.shape[0] // LANES):
        out[at + i:at + i + 1, :] = as_line(column[i * LANES:(i + 1) * LANES, :])


def aims(me_ref, hid, local):
    model = hid[0].shape[1] - LANES
    apart, place = [], []
    for h in hid:
        code = h[:, model:model + LANES].astype(f32).astype(jnp.int32)
        goal = code[:, 0:1] * 256 + code[:, 1:2]
        owner = lax.div(goal, local)
        apart.append(jnp.bitwise_xor(owner, me_ref[0]))
        place.append(goal - owner * local)
    return jnp.concatenate(apart, axis=0), jnp.concatenate(place, axis=0)


def spots(apart, place, meta):
    bits, start = meta
    return jnp.where(apart == bits, place - start, -1)


def scores_of(rows, words, score, prob):
    at, top = 0, None
    for ref in words:
        n = ref.shape[0]
        piece = lax.dot_general(rows[...], ref[...], (((1,), (1,)), ((), ())), preferred_element_type=f32)
        score[:, at:at + n] = piece
        best = jnp.max(piece, axis=1, keepdims=True)
        top = best if top is None else jnp.maximum(top, best)
        at += n
    at, total = 0, None
    for ref in words:
        n = ref.shape[0]
        w = jnp.exp(score[:, at:at + n] - top).astype(bf16)
        prob[:, at:at + n] = w
        part = jnp.sum(w.astype(f32), axis=1, keepdims=True)
        total = part if total is None else total + part
        at += n
    return top, total


def hot_words(words, metas, apart, place, hot):
    at = 0
    for ref, meta in zip(words, metas):
        n = ref.shape[0]
        lane = lax.broadcasted_iota(jnp.int32, (hot.shape[0], n), 1)
        hot[:, at:at + n] = jnp.where(lane == spots(apart, place, meta), 1.0, 0.0).astype(bf16)
        at += n


def product(left, words, n, size):
    at, res = 0, None
    for ref in words:
        count = ref.shape[0]
        d = jnp.dot(left[:, at:at + count], ref[:, n:n + size], preferred_element_type=f32)
        res = d if res is None else res + d
        at += count
    return res


def load_rows(hid, rows):
    at = 0
    for h in hid:
        rows[at:at + h.shape[0], :] = h[:, 0:rows.shape[1]]
        at += h.shape[0]


def first_kernel(me_ref, *refs, nh, metas, local):
    hid, words = refs[:nh], refs[nh:nh + len(metas)]
    out, target, stats, rows, score, prob, hot = refs[nh + len(metas):]
    load_rows(hid, rows)
    top, total = scores_of(rows, words, score, prob)
    stats[:, 0:LANES] = jnp.broadcast_to(top, (top.shape[0], LANES))
    stats[:, LANES:2 * LANES] = jnp.broadcast_to(total, (top.shape[0], LANES))
    hot_words(words, metas, *aims(me_ref, hid, local), hot)
    for n in range(0, out.shape[1], 256):
        out[:, n:n + 256] = product(prob, words, n, 256)
        target[:, n:n + 256] = product(hot, words, n, 256).astype(bf16)


def cost(flops, size, trans=0):
    return pl.CostEstimate(flops=flops, bytes_accessed=size, transcendentals=trans)


SM = pl.BlockSpec(memory_space=pltpu.SMEM)


def first_fold(me, hid, words, metas, local):
    model = words[0].shape[1]
    rows = sum(h.shape[0] for h in hid)
    count = sum(w.shape[0] for w in words)
    return pl.pallas_call(
        functools.partial(first_kernel, nh=len(hid), metas=metas, local=local),
        out_shape=[jax.ShapeDtypeStruct((rows, model), f32), jax.ShapeDtypeStruct((rows, model), bf16),
                   jax.ShapeDtypeStruct((rows, 2 * LANES), f32)],
        in_specs=[SM] + [VM] * (len(hid) + len(words)), out_specs=[VM] * 3,
        scratch_shapes=[pltpu.VMEM((rows, model), bf16), pltpu.VMEM((rows, count), f32),
                        pltpu.VMEM((rows, count), bf16), pltpu.VMEM((rows, count), bf16)],
        compiler_params=params(), cost_estimate=cost(6 * rows * count * model, 2 * (rows + count) * model),
        name="first_fold",
    )(me, *hid, *words)


def last_kernel(me_ref, *refs, nh, metas, group, local):
    hid, words = refs[:nh], refs[nh:nh + len(metas)]
    own, one, before, stats, value, target, facts, lines, rows, score, prob, hot = refs[nh + len(metas):]
    load_rows(hid, rows)
    count, model = one.shape
    apart, place = aims(me_ref, hid, local)
    top2, total2 = scores_of(rows, words, score, prob)
    hot_words(words, metas, apart, place, hot)
    top1, total1 = stats[:, 0:1], stats[:, LANES:LANES + 1]
    top = jnp.maximum(top1, top2)
    s1, s2 = jnp.exp(top1 - top), jnp.exp(top2 - top)
    total = s1 * total1 + s2 * total2
    s1, s2 = s1 / total, s2 / total
    whole = top + jnp.log(total)
    centre = jnp.sum(own[0:LANES, :].astype(f32), axis=0, keepdims=True) * (1.0 / LANES)
    aim = None
    for n in range(0, model, 256):
        cols = slice(n, n + 256)
        mix = s1 * one[:, cols] + s2 * product(prob, words, n, 256)
        value[:, cols] = (mix - centre[:, cols]).astype(bf16)
        goal = product(hot, words, n, 256) + before[:, cols].astype(f32)
        target[:, cols] = goal.astype(bf16)
        part = jnp.sum(goal * rows[:, cols].astype(f32), axis=1, keepdims=True)
        aim = part if aim is None else aim + part
    inside = sum(jnp.where(apart == bits, 1.0, 0.0) for bits in group)
    facts[:, 0:LANES] = jnp.broadcast_to(whole, (count, LANES))
    facts[:, LANES:2 * LANES] = jnp.broadcast_to(inside, (count, LANES))
    per = count // LANES
    to_lines(whole, lines, 0)
    to_lines(aim, lines, per)
    for n in range(model // LANES):
        lines[2 * per + n:2 * per + n + 1, :] = centre[:, n * LANES:(n + 1) * LANES]


def last_fold(me, hid, words, metas, group, local, own, one, before, stats):
    rows, model = one.shape
    count = sum(w.shape[0] for w in words)
    return pl.pallas_call(
        functools.partial(last_kernel, nh=len(hid), metas=metas, group=group, local=local),
        out_shape=[jax.ShapeDtypeStruct((rows, model), bf16)] * 2 + [
            jax.ShapeDtypeStruct((rows, 2 * LANES), f32),
            jax.ShapeDtypeStruct((2 * rows // LANES + model // LANES, LANES), f32)],
        in_specs=[SM] + [VM] * (len(hid) + len(words) + 4), out_specs=[VM] * 4,
        scratch_shapes=[pltpu.VMEM((rows, model), bf16), pltpu.VMEM((rows, count), f32),
                        pltpu.VMEM((rows, count), bf16), pltpu.VMEM((rows, count), bf16)],
        compiler_params=params(), cost_estimate=cost(6 * rows * count * model, 2 * (rows + count) * model),
        name="last_fold",
    )(me, *hid, *words, own, one, before, stats)


def combine_kernel(*refs, flips):
    nl = len(flips)
    lines = refs[:nl]
    value, target, facts = refs[nl:nl + 3]
    parts, loss = refs[nl + 3:nl + 7], refs[nl + 7]
    count, model = value.shape
    per = count // LANES
    quarter = count // 4

    def line(j, i, kind):
        over, halves = flips[j]
        v = lines[j][kind * per + (i ^ over):kind * per + (i ^ over) + 1, :]
        return pltpu.roll(v, LANES // 2, axis=1) if halves else v

    mus, shifts = [], []
    for n in range(model // LANES):
        row = slice(2 * per + n, 2 * per + n + 1)
        mu = sum(ref[row, :] for ref in lines) * (1.0 / nl)
        mus.append(jnp.broadcast_to(mu, (LANES, LANES)))
        shifts.append(jnp.broadcast_to(lines[0][row, :] - mu, (LANES, LANES)))
    for i in range(per):
        each = [line(j, i, 0) for j in range(nl)]
        top = functools.reduce(jnp.maximum, each)
        whole = top + jnp.log(sum(jnp.exp(v - top) for v in each))
        if i == 0:
            loss[...] = whole - sum(line(j, i, 1) for j in range(nl))
        whole = jnp.broadcast_to(whole, (LANES, LANES)).T
        part = slice(i * LANES, (i + 1) * LANES)
        weight = jnp.exp(facts[part, 0:LANES] - whole)
        inside = facts[part, LANES:2 * LANES]
        q = i * LANES // quarter
        at = i * LANES - q * quarter
        for n in range(model // LANES):
            cols = slice(n * LANES, (n + 1) * LANES)
            mix = weight * (value[part, cols].astype(f32) + shifts[n])
            mix = (mix - (target[part, cols].astype(f32) - inside * mus[n])).astype(bf16)
            parts[q][at:at + LANES, cols] = mix


def combine(lines, flips, value, target, facts):
    rows, model = value.shape
    side = jax.ShapeDtypeStruct((rows // 4, model), bf16)
    return pl.pallas_call(
        functools.partial(combine_kernel, flips=flips),
        out_shape=[side] * 4 + [jax.ShapeDtypeStruct((1, LANES), f32)],
        in_specs=[VM] * (len(lines) + 3), out_specs=[VM] * 5,
        compiler_params=params(), cost_estimate=cost(8 * rows * model, 8 * rows * model), name="combine",
    )(*lines, value, target, facts)


def plus(a, b):
    return (a.astype(f32) + b.astype(f32)).astype(bf16)


def add_kernel(*refs):
    n = len(refs) // 4
    for i in range(n):
        keep, got = refs[2 * i:2 * i + 2]
        first, second = refs[2 * n + 2 * i:2 * n + 2 * i + 2]
        rows = first.shape[0]
        first[...] = plus(keep[0:rows, :], got[0:rows, :])
        second[...] = plus(keep[rows:2 * rows, :], got[rows:2 * rows, :])


def add_halves(*pairs):
    outs = [jax.ShapeDtypeStruct((p.shape[0] // 2, p.shape[1]), bf16) for p in pairs]
    return pl.pallas_call(
        add_kernel, out_shape=outs, in_specs=[VM] * len(pairs), out_specs=[VM] * len(pairs),
        compiler_params=params(), cost_estimate=cost(pairs[0].size, 8 * pairs[0].size), name="add_halves",
    )(*pairs)


def add_four_kernel(*refs):
    parts, halves = refs[:4], refs[4:]
    rows = halves[0].shape[0]
    for i, out in enumerate(halves):
        part = slice(i * rows, (i + 1) * rows)
        out[...] = sum(ref[part, :].astype(f32) for ref in parts).astype(bf16)


def add_four(*parts):
    rows, model = parts[0].shape
    return pl.pallas_call(
        add_four_kernel, out_shape=[jax.ShapeDtypeStruct((rows // 2, model), bf16)] * 2,
        in_specs=[VM] * 4, out_specs=[VM] * 2,
        compiler_params=params(), cost_estimate=cost(4 * rows * model, 10 * rows * model), name="add_four",
    )(*parts)


def per_device(char_ids, char_table, conv_weight, proj_weight, gate_weight, trans_weight, gate_bias, hidden, targets,
               *, vocab, blk):
    devices = vocab * blk
    axes = ("vocab", "blk")

    def swap(x, bits):
        return lax.ppermute(x, axes, [(i, i ^ bits) for i in range(devices)])

    core, near = blk, 1
    bit_a, bit_b = 2 * blk, 4 * blk
    rest = [1 << i for i in range(1, blk.bit_length() - 1)] + [
        blk << i for i in range(3, vocab.bit_length() - 1)]
    me = lax.axis_index("vocab") * blk + lax.axis_index("blk")
    local, length = char_ids.shape
    mine = hidden.shape[0]

    rows, goal = hidden, targets.reshape(1, mine)
    for bit in rest:
        rows = jnp.concatenate([rows, swap(rows, bit)], axis=0)
        goal = jnp.concatenate([goal, swap(goal, bit)], axis=1)
    weights = (char_table.T, conv_weight, proj_weight, gate_weight, trans_weight, gate_bias)
    many = 4 * (mine << len(rest)) > local
    size = local // 2 if many else local * 5 // 8 // 64 * 64
    marks = (0, size)
    ids = char_ids.T
    e0 = embed(ids, length, 0, size, *weights)
    e0, rows, goal = lax.optimization_barrier((e0, rows, goal))
    goal = goal.reshape(-1, 1)
    code = jnp.concatenate([goal // 256, goal % 256], axis=1).astype(bf16)
    rows = jnp.concatenate([rows, jnp.pad(code, ((0, 0), (0, LANES - 2)))], axis=1)
    hid = [rows] + [swap(rows, b) for b in (bit_b, bit_a, bit_a | bit_b)]
    e1 = embed(ids, length, size, local - size, *weights)
    held, *hid = lax.optimization_barrier((e1, *hid))
    pieces = [e0, held]
    cores = [swap(e, core) for e in pieces]
    nears = [swap(e, near) for e in pieces]
    held, nears[0] = lax.optimization_barrier((held, nears[0]))
    far = swap(nears[0], core)

    me = me.astype(jnp.int32).reshape(1)
    meta = [tuple((bits, m) for m in marks) for bits in (0, core, near, core | near)]
    early = [(nears[0], meta[2][0]), (far, meta[3][0])]
    late = []
    if many:
        early, late = [], early
    words = pieces + cores + [w for w, _ in early]
    one, target, stats = first_fold(me, hid, words, meta[0] + meta[1] + tuple(m for _, m in early), local)
    held, stats = lax.optimization_barrier((nears[1], stats))
    late += [(held, meta[2][1]), (swap(held, core), meta[3][1])]
    words, metas = [w for w, _ in late], tuple(m for _, m in late)
    value, target, facts, line = last_fold(
        me, hid, words, metas, (0, core, near, core | near), local, e0, one, target, stats)
    bits = [bit_a, bit_b] + rest
    others = [sum(b for j, b in enumerate(bits) if k >> j & 1) for k in range(1, 1 << len(bits))]
    order = rest + [bit_b, bit_a]
    flips = tuple((sum(1 << (j - 1) for j, b in enumerate(order) if j and o & b), bool(o & rest[0])) for o in others)
    lines = [swap(line, o) for o in others]
    *parts, loss = combine([line] + lines, ((0, False),) + flips, value, target, facts)
    far_part = swap(parts[3], bit_a | bit_b)
    keep, send = add_four(parts[0], swap(parts[1], bit_b), swap(parts[2], bit_a), far_part)
    for bit in rest[:0:-1]:
        keep, send = add_halves(keep, swap(send, bit))
    grad = plus(keep, swap(send, rest[0]))
    return loss[0, :mine], grad


def solution(mesh):
    words = P(("vocab", "blk"))
    return jax.shard_map(
        functools.partial(per_device, vocab=mesh.shape["vocab"], blk=mesh.shape["blk"]),
        mesh=mesh,
        in_specs=(P(("vocab", "blk"), None), P(), P(), P(), P(), P(), P(), P(("vocab", "blk"), None), words),
        out_specs=(words, P(("vocab", "blk"), None)),
        check_vma=False,
    )
```

```python
import functools
import jax
import jax.numpy as jnp
from jax import lax
from jax.experimental import pallas as pl
from jax.experimental.pallas import tpu as pltpu
from jax.sharding import PartitionSpec as P

bf16=jnp.bfloat16; f32=jnp.float32
LANES = 128
SPAN = 8


def prep_toeplitz(conv_ref, toep, ce, widths, filters):
    depth = toep.shape[0]
    for k in range(widths):
        rows = (k + 1) * ce
        piece = conv_ref[0:rows, k * filters:(k + 1) * filters]
        for o in range(SPAN):
            cols = slice((k * SPAN + o) * filters, (k * SPAN + o + 1) * filters)
            if o:
                toep[0:o * ce, cols] = jnp.zeros((o * ce, filters), bf16)
            toep[o * ce:o * ce + rows, cols] = piece
            rest = depth - o * ce - rows
            if rest:
                toep[o * ce + rows:depth, cols] = jnp.zeros((rest, filters), bf16)

def lookup(ids_ref, start, words, tab_ref, vec, length, ce):
    per = LANES // ce
    low_tab = tab_ref[:, 0:LANES].astype(f32)
    top_tab = tab_ref[:, LANES:2 * LANES].astype(f32)
    first = start // LANES * LANES
    for tile in range(first, start + words, LANES):
        low_word, high_word = max(tile, start), min(tile + LANES, start + words)
        for g in range(vec.shape[1] // LANES):
            parts = []
            for q in range(per):
                p = g * per + q
                if p >= length:
                    parts.append(jnp.zeros((ce, LANES), f32))
                    continue
                idx = jnp.broadcast_to(ids_ref[p:p + 1, tile:tile + LANES], (8, LANES))
                low = jnp.bitwise_and(idx, LANES - 1)
                top = idx >= LANES
                for h in range(0, ce, 8):
                    one = jnp.take_along_axis(low_tab[h:h + 8], low, axis=1)
                    two = jnp.take_along_axis(top_tab[h:h + 8], low, axis=1)
                    parts.append(jnp.where(top, two, one))
            block = jnp.concatenate(parts, axis=0).T.astype(bf16)
            vec[low_word - start:high_word - start, g * LANES:(g + 1) * LANES] = block[low_word - tile:high_word - tile]


def conv_pool(vec, toep, acc, length, widths, filters):
    words = vec.shape[0]
    def tile(b, k, o, lhs):
        cols = slice((k * SPAN + o) * filters, (k * SPAN + o + 2) * filters)
        return jnp.dot(lhs, toep[:, cols], preferred_element_type=f32)
    acc[...] = jnp.full(acc.shape, -jnp.inf, f32)
    least = (length - widths + 1) // SPAN
    def body(b, _):
        lhs = vec[:, pl.ds(pl.multiple_of(b * LANES, LANES), 2 * LANES)]
        for k in range(widths):
            best = acc[:, k * filters:(k + 1) * filters]
            for o in range(0, SPAN, 2):
                r = tile(b, k, o, lhs)
                best = jnp.maximum(best, jnp.maximum(r[:, :filters], r[:, filters:]))
            acc[:, k * filters:(k + 1) * filters] = best
        return 0
    lax.fori_loop(0, least, body, 0)
    for b in range(least, -(-length // SPAN)):
        lhs = vec[:, b * LANES:(b + 2) * LANES]
        for k in range(widths):
            usable = min(SPAN, length - k - b * SPAN)
            if usable <= 0: continue
            best = acc[:, k * filters:(k + 1) * filters]
            for o in range(0, usable, 2):
                r = tile(b, k, o, lhs)
                best = jnp.maximum(best, r[:, :filters])
                if o + 1 < usable:
                    best = jnp.maximum(best, r[:, filters:])
            acc[:, k * filters:(k + 1) * filters] = best

def cnn_kernel(ids_ref, tab_ref, conv_ref, bias_ref, proj_hbm, gate_hbm, trans_hbm, *rest,
               widths, filters, ce, length, layers, nt, start):
    out_ref, vec, toep, acc, feat, proj, gate, trans, state, last, sems = rest
    copies = [pltpu.make_async_copy(s, d, sems.at[i]) for i, (s, d) in enumerate(
        ((proj_hbm, proj), (gate_hbm, gate), (trans_hbm, trans)))]
    for c in copies:
        c.start()
    words = out_ref.shape[0]
    prep_toeplitz(conv_ref, toep, ce, widths, filters)
    lookup(ids_ref, start, words, tab_ref, vec, length, ce)
    conv_pool(vec, toep, acc, length, widths, filters)
    for c in copies:
        c.wait()
    feat[...] = jnp.tanh(acc[...]).astype(bf16)
    model = last.shape[1]
    for n in range(0, model, nt):
        state[:, n:n + nt] = jnp.dot(feat[...], proj[:, n:n + nt], preferred_element_type=f32).astype(bf16)
    for l in range(layers):
        for n in range(0, model, nt):
            cur = state[...]
            g = jnp.dot(cur, gate[l, :, n:n + nt], preferred_element_type=f32) + bias_ref[l:l + 1, n:n + nt]
            t = jnp.dot(cur, trans[l, :, n:n + nt], preferred_element_type=f32)
            opened = jax.nn.sigmoid(g)
            carried = jnp.maximum(t, 0.0)
            new = (opened * carried + (1.0 - opened) * state[:, n:n + nt].astype(f32)).astype(bf16)
            if l + 1 < layers:
                last[:, n:n + nt] = new
            else:
                out_ref[:, n:n + nt] = new
        if l + 1 < layers:
            state[...] = last[...]


ANY = pl.BlockSpec(memory_space=pl.ANY)
VM = pl.BlockSpec(memory_space=pltpu.VMEM)


def params(limit_mib=56):
    return pltpu.CompilerParams(vmem_limit_bytes=limit_mib << 20)


def embed(ids, length, start, words, tab_t, conv_weight, proj_weight, gate_weight, trans_weight, gate_bias, nt=256):
    ce = tab_t.shape[0]
    widths = conv_weight.shape[0] // ce
    filters = conv_weight.shape[1] // widths
    layers, model, _ = gate_weight.shape
    flops = 2 * words * (length * 256 * widths * filters + widths * filters * model + 2 * layers * model * model)
    return pl.pallas_call(
        functools.partial(cnn_kernel, widths=widths, filters=filters, ce=ce, length=length, layers=layers, nt=nt,
                          start=start),
        out_shape=jax.ShapeDtypeStruct((words, model), bf16),
        in_specs=[VM, VM, VM, VM, ANY, ANY, ANY],
        out_specs=VM,
        scratch_shapes=[
            pltpu.VMEM((words, (-(-length // SPAN) + 1) * LANES), bf16),
            pltpu.VMEM((2 * LANES, widths * SPAN * filters), bf16),
            pltpu.VMEM((words, widths * filters), f32),
            pltpu.VMEM((words, widths * filters), bf16),
            pltpu.VMEM(proj_weight.shape, bf16),
            pltpu.VMEM(gate_weight.shape, bf16),
            pltpu.VMEM(trans_weight.shape, bf16),
            pltpu.VMEM((words, model), bf16),
            pltpu.VMEM((words, model), bf16),
            pltpu.SemaphoreType.DMA((3,)),
        ],
        compiler_params=params(),
        cost_estimate=pl.CostEstimate(flops=flops, bytes_accessed=12 << 20, transcendentals=words * 4096),
        name="embed",
    )(ids, tab_t, conv_weight, gate_bias, proj_weight, gate_weight, trans_weight)


def as_line(column):
    return jnp.broadcast_to(column, (LANES, LANES)).T[0:1, :]


def to_lines(column, out, at):
    for i in range(column.shape[0] // LANES):
        out[at + i:at + i + 1, :] = as_line(column[i * LANES:(i + 1) * LANES, :])


def aims(me_ref, hid, local):
    model = hid[0].shape[1] - LANES
    apart, place = [], []
    for h in hid:
        code = h[:, model:model + LANES].astype(f32).astype(jnp.int32)
        goal = code[:, 0:1] * 256 + code[:, 1:2]
        owner = lax.div(goal, local)
        apart.append(jnp.bitwise_xor(owner, me_ref[0]))
        place.append(goal - owner * local)
    return jnp.concatenate(apart, axis=0), jnp.concatenate(place, axis=0)


def spots(apart, place, meta):
    bits, start = meta
    return jnp.where(apart == bits, place - start, -1)


def scores_of(rows, words, metas, apart, place, score, prob, hot):
    at, top, aim = 0, None, None
    for ref, meta in zip(words, metas):
        n = ref.shape[0]
        piece = lax.dot_general(rows[...], ref[...], (((1,), (1,)), ((), ())), preferred_element_type=f32)
        score[:, at:at + n] = piece
        hit = lax.broadcasted_iota(jnp.int32, piece.shape, 1) == spots(apart, place, meta)
        hot[:, at:at + n] = jnp.where(hit, 1.0, 0.0).astype(bf16)
        part = jnp.sum(jnp.where(hit, piece, 0.0), axis=1, keepdims=True)
        best = jnp.max(piece, axis=1, keepdims=True)
        top = best if top is None else jnp.maximum(top, best)
        aim = part if aim is None else aim + part
        at += n
    at, total = 0, None
    for ref in words:
        n = ref.shape[0]
        w = jnp.exp(score[:, at:at + n] - top).astype(bf16)
        prob[:, at:at + n] = w
        part = jnp.sum(w.astype(f32), axis=1, keepdims=True)
        total = part if total is None else total + part
        at += n
    return top, total, aim


def product(left, words, n, size):
    at, res = 0, None
    for ref in words:
        count = ref.shape[0]
        d = jnp.dot(left[:, at:at + count], ref[:, n:n + size], preferred_element_type=f32)
        res = d if res is None else res + d
        at += count
    return res


def load_rows(hid, rows):
    at = 0
    for h in hid:
        rows[at:at + h.shape[0], :] = h[:, 0:rows.shape[1]]
        at += h.shape[0]


def first_kernel(me_ref, *refs, nh, metas, local):
    hid, words = refs[:nh], refs[nh:nh + len(metas)]
    out, target, stats, rows, score, prob, hot = refs[nh + len(metas):]
    load_rows(hid, rows)
    each = scores_of(rows, words, metas, *aims(me_ref, hid, local), score, prob, hot)
    for i, column in enumerate(each):
        stats[:, i * LANES:(i + 1) * LANES] = jnp.broadcast_to(column, (column.shape[0], LANES))
    for n in range(0, out.shape[1], 256):
        out[:, n:n + 256] = product(prob, words, n, 256)
        target[:, n:n + 256] = product(hot, words, n, 256).astype(bf16)


def cost(flops, size, trans=0):
    return pl.CostEstimate(flops=flops, bytes_accessed=size, transcendentals=trans)


SM = pl.BlockSpec(memory_space=pltpu.SMEM)


def first_fold(me, hid, words, metas, local):
    model = words[0].shape[1]
    rows = sum(h.shape[0] for h in hid)
    count = sum(w.shape[0] for w in words)
    return pl.pallas_call(
        functools.partial(first_kernel, nh=len(hid), metas=metas, local=local),
        out_shape=[jax.ShapeDtypeStruct((rows, model), f32), jax.ShapeDtypeStruct((rows, model), bf16),
                   jax.ShapeDtypeStruct((rows, 3 * LANES), f32)],
        in_specs=[SM] + [VM] * (len(hid) + len(words)), out_specs=[VM] * 3,
        scratch_shapes=[pltpu.VMEM((rows, model), bf16), pltpu.VMEM((rows, count), f32),
                        pltpu.VMEM((rows, count), bf16), pltpu.VMEM((rows, count), bf16)],
        compiler_params=params(), cost_estimate=cost(6 * rows * count * model, 2 * (rows + count) * model),
        name="first_fold",
    )(me, *hid, *words)


def last_kernel(me_ref, *refs, nh, metas, group, local):
    hid, words = refs[:nh], refs[nh:nh + len(metas)]
    own, stats, prob, hot, facts, lines, rows, score = refs[nh + len(metas):]
    load_rows(hid, rows)
    count, model = rows.shape
    apart, place = aims(me_ref, hid, local)
    top2, total2, aim2 = scores_of(rows, words, metas, apart, place, score, prob, hot)
    top1, total1, aim1 = (stats[:, i * LANES:i * LANES + 1] for i in range(3))
    top = jnp.maximum(top1, top2)
    total = jnp.exp(top1 - top) * total1 + jnp.exp(top2 - top) * total2
    inside = sum(jnp.where(apart == bits, 1.0, 0.0) for bits in group)
    facts[:, 0:LANES] = jnp.broadcast_to(top2, (count, LANES))
    facts[:, LANES:2 * LANES] = jnp.broadcast_to(inside, (count, LANES))
    per = count // LANES
    to_lines(top + jnp.log(total), lines, 0)
    to_lines(aim1 + aim2, lines, per)
    centre = jnp.sum(own[0:LANES, :].astype(f32), axis=0, keepdims=True) * (1.0 / LANES)
    for n in range(model // LANES):
        lines[2 * per + n:2 * per + n + 1, :] = centre[:, n * LANES:(n + 1) * LANES]


def last_scores(me, hid, words, metas, group, local, own, stats):
    model = own.shape[1]
    rows = stats.shape[0]
    count = sum(w.shape[0] for w in words)
    return pl.pallas_call(
        functools.partial(last_kernel, nh=len(hid), metas=metas, group=group, local=local),
        out_shape=[jax.ShapeDtypeStruct((rows, count), bf16)] * 2 + [
            jax.ShapeDtypeStruct((rows, 2 * LANES), f32),
            jax.ShapeDtypeStruct((2 * rows // LANES + model // LANES, LANES), f32)],
        in_specs=[SM] + [VM] * (len(hid) + len(words) + 2), out_specs=[VM] * 4,
        scratch_shapes=[pltpu.VMEM((rows, model), bf16), pltpu.VMEM((rows, count), f32)],
        compiler_params=params(), cost_estimate=cost(2 * rows * count * model, 2 * (rows + count) * model),
        name="last_scores",
    )(me, *hid, *words, own, stats)


def close_kernel(*refs, flips, nw):
    nl = len(flips)
    lines, words = refs[:nl], refs[nl:nl + nw]
    prob, hot, one, before, stats, facts = refs[nl + nw:nl + nw + 6]
    parts, loss = refs[nl + nw + 6:nl + nw + 10], refs[nl + nw + 10]
    count, model = one.shape
    per = count // LANES
    quarter = count // 4

    def line(j, i, kind):
        over, halves = flips[j]
        v = lines[j][kind * per + (i ^ over):kind * per + (i ^ over) + 1, :]
        return pltpu.roll(v, LANES // 2, axis=1) if halves else v

    scales = []
    for i in range(per):
        each = [line(j, i, 0) for j in range(nl)]
        top = functools.reduce(jnp.maximum, each)
        whole = top + jnp.log(sum(jnp.exp(v - top) for v in each))
        if i == 0:
            loss[...] = whole - sum(line(j, i, 1) for j in range(nl))
        weight = jnp.broadcast_to(jnp.exp(each[0] - whole), (LANES, LANES)).T
        whole = jnp.broadcast_to(whole, (LANES, LANES)).T
        part = slice(i * LANES, (i + 1) * LANES)
        scales.append((jnp.exp(stats[part, 0:LANES] - whole)[:, 0:1], jnp.exp(facts[part, 0:LANES] - whole)[:, 0:1],
                       (facts[part, LANES:2 * LANES] - weight)[:, 0:1]))
    c1, c2, c3 = (jnp.concatenate(c, axis=0) for c in zip(*scales))
    for n in range(0, model, 256):
        cols = slice(n, n + 256)
        mu = jnp.concatenate([
            sum(ref[2 * per + m // LANES:2 * per + m // LANES + 1, :] for ref in lines) * (1.0 / nl)
            for m in range(n, n + 256, LANES)], axis=1)
        goal = product(hot, words, n, 256) + before[:, cols].astype(f32)
        mix = (c1 * one[:, cols] + c2 * product(prob, words, n, 256) + (c3 * mu - goal)).astype(bf16)
        for q in range(4):
            parts[q][:, cols] = mix[q * quarter:(q + 1) * quarter]


def close(lines, flips, words, prob, hot, one, before, stats, facts):
    rows, model = one.shape
    side = jax.ShapeDtypeStruct((rows // 4, model), bf16)
    return pl.pallas_call(
        functools.partial(close_kernel, flips=flips, nw=len(words)),
        out_shape=[side] * 4 + [jax.ShapeDtypeStruct((1, LANES), f32)],
        in_specs=[VM] * (len(lines) + len(words) + 6), out_specs=[VM] * 5, compiler_params=params(),
        cost_estimate=cost(4 * rows * prob.shape[1] * model, 8 * rows * model), name="close",
    )(*lines, *words, prob, hot, one, before, stats, facts)


def plus(a, b):
    return (a.astype(f32) + b.astype(f32)).astype(bf16)


def add_kernel(*refs):
    n = len(refs) // 4
    for i in range(n):
        keep, got = refs[2 * i:2 * i + 2]
        first, second = refs[2 * n + 2 * i:2 * n + 2 * i + 2]
        rows = first.shape[0]
        first[...] = plus(keep[0:rows, :], got[0:rows, :])
        second[...] = plus(keep[rows:2 * rows, :], got[rows:2 * rows, :])


def add_halves(*pairs):
    outs = [jax.ShapeDtypeStruct((p.shape[0] // 2, p.shape[1]), bf16) for p in pairs]
    return pl.pallas_call(
        add_kernel, out_shape=outs, in_specs=[VM] * len(pairs), out_specs=[VM] * len(pairs),
        compiler_params=params(), cost_estimate=cost(pairs[0].size, 8 * pairs[0].size), name="add_halves",
    )(*pairs)


def add_four_kernel(*refs):
    parts, halves = refs[:4], refs[4:]
    rows = halves[0].shape[0]
    for i, out in enumerate(halves):
        part = slice(i * rows, (i + 1) * rows)
        out[...] = sum(ref[part, :].astype(f32) for ref in parts).astype(bf16)


def add_four(*parts):
    rows, model = parts[0].shape
    return pl.pallas_call(
        add_four_kernel, out_shape=[jax.ShapeDtypeStruct((rows // 2, model), bf16)] * 2,
        in_specs=[VM] * 4, out_specs=[VM] * 2,
        compiler_params=params(), cost_estimate=cost(4 * rows * model, 10 * rows * model), name="add_four",
    )(*parts)


def per_device(char_ids, char_table, conv_weight, proj_weight, gate_weight, trans_weight, gate_bias, hidden, targets,
               *, vocab, blk):
    devices = vocab * blk
    axes = ("vocab", "blk")

    def swap(x, bits):
        return lax.ppermute(x, axes, [(i, i ^ bits) for i in range(devices)])

    core, near = blk, 1
    bit_a, bit_b = 2 * blk, 4 * blk
    rest = [1 << i for i in range(1, blk.bit_length() - 1)] + [
        blk << i for i in range(3, vocab.bit_length() - 1)]
    me = lax.axis_index("vocab") * blk + lax.axis_index("blk")
    local, length = char_ids.shape
    mine = hidden.shape[0]

    rows, goal = hidden, targets.reshape(1, mine)
    for bit in rest:
        rows = jnp.concatenate([rows, swap(rows, bit)], axis=0)
        goal = jnp.concatenate([goal, swap(goal, bit)], axis=1)
    weights = (char_table.T, conv_weight, proj_weight, gate_weight, trans_weight, gate_bias)
    many = 4 * (mine << len(rest)) > local
    size = local // 2
    marks = (0, size)
    ids = char_ids.T
    e0 = embed(ids, length, 0, size, *weights)
    e0, rows, goal = lax.optimization_barrier((e0, rows, goal))
    goal = goal.reshape(-1, 1)
    code = jnp.concatenate([goal // 256, goal % 256], axis=1).astype(bf16)
    rows = jnp.concatenate([rows, jnp.pad(code, ((0, 0), (0, LANES - 2)))], axis=1)
    hid = [rows] + [swap(rows, b) for b in (bit_b, bit_a, bit_a | bit_b)]
    e1 = embed(ids, length, size, local - size, *weights)
    held, *hid = lax.optimization_barrier((e1, *hid))
    pieces = [e0, held]
    cores = [swap(e, core) for e in pieces]
    nears = [swap(e, near) for e in pieces]
    held, nears[0] = lax.optimization_barrier((held, nears[0]))
    far = swap(nears[0], core)

    me = me.astype(jnp.int32).reshape(1)
    meta = [tuple((bits, m) for m in marks) for bits in (0, core, near, core | near)]
    early = [(nears[0], meta[2][0]), (far, meta[3][0])]
    late = []
    if many:
        early, late = [], early
    words = pieces + cores + [w for w, _ in early]
    one, target, stats = first_fold(me, hid, words, meta[0] + meta[1] + tuple(m for _, m in early), local)
    held, stats = lax.optimization_barrier((nears[1], stats))
    late += [(held, meta[2][1]), (swap(held, core), meta[3][1])]
    words, metas = [w for w, _ in late], tuple(m for _, m in late)
    prob, hot, facts, line = last_scores(
        me, hid, words, metas, (0, core, near, core | near), local, e0, stats)
    bits = [bit_a, bit_b] + rest
    others = [sum(b for j, b in enumerate(bits) if k >> j & 1) for k in range(1, 1 << len(bits))]
    order = rest + [bit_b, bit_a]
    flips = tuple((sum(1 << (j - 1) for j, b in enumerate(order) if j and o & b), bool(o & rest[0])) for o in others)
    lines = [swap(line, o) for o in others]
    *parts, loss = close([line] + lines, ((0, False),) + flips, words, prob, hot, one, target, stats, facts)
    far_part = swap(parts[3], bit_a | bit_b)
    keep, send = add_four(parts[0], swap(parts[1], bit_b), swap(parts[2], bit_a), far_part)
    for bit in rest[:0:-1]:
        keep, send = add_halves(keep, swap(send, bit))
    grad = plus(keep, swap(send, rest[0]))
    return loss[0, :mine], grad


def solution(mesh):
    words = P(("vocab", "blk"))
    return jax.shard_map(
        functools.partial(per_device, vocab=mesh.shape["vocab"], blk=mesh.shape["blk"]),
        mesh=mesh,
        in_specs=(P(("vocab", "blk"), None), P(), P(), P(), P(), P(), P(), P(("vocab", "blk"), None), words),
        out_specs=(words, P(("vocab", "blk"), None)),
        check_vma=False,
    )
```

```python
import functools
import jax
import jax.numpy as jnp
from jax import lax
from jax.experimental import pallas as pl
from jax.experimental.pallas import tpu as pltpu
from jax.sharding import PartitionSpec as P

bf16=jnp.bfloat16; f32=jnp.float32
LANES = 128
SPAN = 8


def prep_toeplitz(conv_ref, toep, ce, widths, filters):
    depth = toep.shape[0]
    for k in range(widths):
        rows = (k + 1) * ce
        piece = conv_ref[0:rows, k * filters:(k + 1) * filters]
        for o in range(SPAN):
            cols = slice((k * SPAN + o) * filters, (k * SPAN + o + 1) * filters)
            if o:
                toep[0:o * ce, cols] = jnp.zeros((o * ce, filters), bf16)
            toep[o * ce:o * ce + rows, cols] = piece
            rest = depth - o * ce - rows
            if rest:
                toep[o * ce + rows:depth, cols] = jnp.zeros((rest, filters), bf16)

def lookup(ids_ref, start, words, tab_ref, vec, length, ce):
    per = LANES // ce
    low_tab = tab_ref[:, 0:LANES].astype(f32)
    top_tab = tab_ref[:, LANES:2 * LANES].astype(f32)
    first = start // LANES * LANES
    for tile in range(first, start + words, LANES):
        low_word, high_word = max(tile, start), min(tile + LANES, start + words)
        for g in range(vec.shape[1] // LANES):
            parts = []
            for q in range(per):
                p = g * per + q
                if p >= length:
                    parts.append(jnp.zeros((ce, LANES), f32))
                    continue
                idx = jnp.broadcast_to(ids_ref[p:p + 1, tile:tile + LANES], (8, LANES))
                low = jnp.bitwise_and(idx, LANES - 1)
                top = idx >= LANES
                for h in range(0, ce, 8):
                    one = jnp.take_along_axis(low_tab[h:h + 8], low, axis=1)
                    two = jnp.take_along_axis(top_tab[h:h + 8], low, axis=1)
                    parts.append(jnp.where(top, two, one))
            block = jnp.concatenate(parts, axis=0).T.astype(bf16)
            vec[low_word - start:high_word - start, g * LANES:(g + 1) * LANES] = block[low_word - tile:high_word - tile]


def conv_pool(vec, toep, acc, length, widths, filters):
    def tile(k, o, lhs):
        cols = slice((k * SPAN + o) * filters, (k * SPAN + o + 2) * filters)
        return jnp.dot(lhs, toep[:, cols], preferred_element_type=f32)
    acc[...] = jnp.full(acc.shape, -jnp.inf, f32)
    for b in range(-(-length // SPAN)):
        lhs = vec[:, b * LANES:(b + 2) * LANES]
        for k in range(widths):
            usable = min(SPAN, length - k - b * SPAN)
            if usable <= 0:
                continue
            best = acc[:, k * filters:(k + 1) * filters]
            for o in range(0, usable, 2):
                r = tile(k, o, lhs)
                best = jnp.maximum(best, r[:, :filters])
                if o + 1 < usable:
                    best = jnp.maximum(best, r[:, filters:])
            acc[:, k * filters:(k + 1) * filters] = best


def cnn_kernel(ids_ref, tab_ref, conv_ref, bias_ref, proj_hbm, gate_hbm, trans_hbm, *rest,
               widths, filters, ce, length, layers, nt, start):
    out_ref, vec, toep, acc, feat, proj, gate, trans, state, last, sems = rest
    copies = [pltpu.make_async_copy(s, d, sems.at[i]) for i, (s, d) in enumerate(
        ((proj_hbm, proj), (gate_hbm, gate), (trans_hbm, trans)))]
    for c in copies:
        c.start()
    words = out_ref.shape[0]
    prep_toeplitz(conv_ref, toep, ce, widths, filters)
    lookup(ids_ref, start, words, tab_ref, vec, length, ce)
    conv_pool(vec, toep, acc, length, widths, filters)
    for c in copies:
        c.wait()
    feat[...] = jnp.tanh(acc[...]).astype(bf16)
    model = last.shape[1]
    for n in range(0, model, nt):
        state[:, n:n + nt] = jnp.dot(feat[...], proj[:, n:n + nt], preferred_element_type=f32).astype(bf16)
    for l in range(layers):
        for n in range(0, model, nt):
            cur = state[...]
            g = jnp.dot(cur, gate[l, :, n:n + nt], preferred_element_type=f32) + bias_ref[l:l + 1, n:n + nt]
            t = jnp.dot(cur, trans[l, :, n:n + nt], preferred_element_type=f32)
            opened = jax.nn.sigmoid(g)
            carried = jnp.maximum(t, 0.0)
            new = (opened * carried + (1.0 - opened) * state[:, n:n + nt].astype(f32)).astype(bf16)
            if l + 1 < layers:
                last[:, n:n + nt] = new
            else:
                out_ref[:, n:n + nt] = new
        if l + 1 < layers:
            state[...] = last[...]


ANY = pl.BlockSpec(memory_space=pl.ANY)
VM = pl.BlockSpec(memory_space=pltpu.VMEM)


def params(limit_mib=56):
    return pltpu.CompilerParams(vmem_limit_bytes=limit_mib << 20)


def embed(ids, length, start, words, tab_t, conv_weight, proj_weight, gate_weight, trans_weight, gate_bias, nt=256):
    ce = tab_t.shape[0]
    widths = conv_weight.shape[0] // ce
    filters = conv_weight.shape[1] // widths
    layers, model, _ = gate_weight.shape
    flops = 2 * words * (length * 256 * widths * filters + widths * filters * model + 2 * layers * model * model)
    return pl.pallas_call(
        functools.partial(cnn_kernel, widths=widths, filters=filters, ce=ce, length=length, layers=layers, nt=nt,
                          start=start),
        out_shape=jax.ShapeDtypeStruct((words, model), bf16),
        in_specs=[VM, VM, VM, VM, ANY, ANY, ANY],
        out_specs=VM,
        scratch_shapes=[
            pltpu.VMEM((words, (-(-length // SPAN) + 1) * LANES), bf16),
            pltpu.VMEM((2 * LANES, widths * SPAN * filters), bf16),
            pltpu.VMEM((words, widths * filters), f32),
            pltpu.VMEM((words, widths * filters), bf16),
            pltpu.VMEM(proj_weight.shape, bf16),
            pltpu.VMEM(gate_weight.shape, bf16),
            pltpu.VMEM(trans_weight.shape, bf16),
            pltpu.VMEM((words, model), bf16),
            pltpu.VMEM((words, model), bf16),
            pltpu.SemaphoreType.DMA((3,)),
        ],
        compiler_params=params(),
        cost_estimate=pl.CostEstimate(flops=flops, bytes_accessed=12 << 20, transcendentals=words * 4096),
        name="embed",
    )(ids, tab_t, conv_weight, gate_bias, proj_weight, gate_weight, trans_weight)


def as_line(column):
    return jnp.broadcast_to(column, (LANES, LANES)).T[0:1, :]


def to_lines(column, out, at):
    for i in range(column.shape[0] // LANES):
        out[at + i:at + i + 1, :] = as_line(column[i * LANES:(i + 1) * LANES, :])


def aims(me_ref, hid, local):
    model = hid[0].shape[1] - LANES
    apart, place = [], []
    for h in hid:
        code = h[:, model:model + LANES].astype(f32).astype(jnp.int32)
        goal = code[:, 0:1] * 256 + code[:, 1:2]
        owner = lax.div(goal, local)
        apart.append(jnp.bitwise_xor(owner, me_ref[0]))
        place.append(goal - owner * local)
    return jnp.concatenate(apart, axis=0), jnp.concatenate(place, axis=0)


def spots(apart, place, meta):
    bits, start = meta
    return jnp.where(apart == bits, place - start, -1)


def scores_of(rows, words, metas, apart, place, score, prob, hot):
    at, top, aim = 0, None, None
    for ref, meta in zip(words, metas):
        n = ref.shape[0]
        piece = lax.dot_general(rows[...], ref[...], (((1,), (1,)), ((), ())), preferred_element_type=f32)
        score[:, at:at + n] = piece
        hit = lax.broadcasted_iota(jnp.int32, piece.shape, 1) == spots(apart, place, meta)
        hot[:, at:at + n] = jnp.where(hit, 1.0, 0.0).astype(bf16)
        part = jnp.sum(jnp.where(hit, piece, 0.0), axis=1, keepdims=True)
        best = jnp.max(piece, axis=1, keepdims=True)
        top = best if top is None else jnp.maximum(top, best)
        aim = part if aim is None else aim + part
        at += n
    at, total = 0, None
    for ref in words:
        n = ref.shape[0]
        w = jnp.exp(score[:, at:at + n] - top).astype(bf16)
        prob[:, at:at + n] = w
        part = jnp.sum(w.astype(f32), axis=1, keepdims=True)
        total = part if total is None else total + part
        at += n
    return top, total, aim


def product(left, words, n, size):
    at, res = 0, None
    for ref in words:
        count = ref.shape[0]
        d = jnp.dot(left[:, at:at + count], ref[:, n:n + size], preferred_element_type=f32)
        res = d if res is None else res + d
        at += count
    return res


def load_rows(hid, rows):
    at = 0
    for h in hid:
        rows[at:at + h.shape[0], :] = h[:, 0:rows.shape[1]]
        at += h.shape[0]


def first_kernel(me_ref, *refs, nh, metas, local):
    hid, words = refs[:nh], refs[nh:nh + len(metas)]
    out, target, stats, rows, score, prob, hot = refs[nh + len(metas):]
    load_rows(hid, rows)
    each = scores_of(rows, words, metas, *aims(me_ref, hid, local), score, prob, hot)
    for i, column in enumerate(each):
        stats[:, i * LANES:(i + 1) * LANES] = jnp.broadcast_to(column, (column.shape[0], LANES))
    for n in range(0, out.shape[1], 256):
        out[:, n:n + 256] = product(prob, words, n, 256)
        target[:, n:n + 256] = product(hot, words, n, 256).astype(bf16)


def cost(flops, size, trans=0):
    return pl.CostEstimate(flops=flops, bytes_accessed=size, transcendentals=trans)


SM = pl.BlockSpec(memory_space=pltpu.SMEM)


def first_fold(me, hid, words, metas, local):
    model = words[0].shape[1]
    rows = sum(h.shape[0] for h in hid)
    count = sum(w.shape[0] for w in words)
    return pl.pallas_call(
        functools.partial(first_kernel, nh=len(hid), metas=metas, local=local),
        out_shape=[jax.ShapeDtypeStruct((rows, model), f32), jax.ShapeDtypeStruct((rows, model), bf16),
                   jax.ShapeDtypeStruct((rows, 3 * LANES), f32)],
        in_specs=[SM] + [VM] * (len(hid) + len(words)), out_specs=[VM] * 3,
        scratch_shapes=[pltpu.VMEM((rows, model), bf16), pltpu.VMEM((rows, count), f32),
                        pltpu.VMEM((rows, count), bf16), pltpu.VMEM((rows, count), bf16)],
        compiler_params=params(), cost_estimate=cost(6 * rows * count * model, 2 * (rows + count) * model),
        name="first_fold",
    )(me, *hid, *words)


def last_kernel(me_ref, *refs, nh, metas, group, local):
    hid, words = refs[:nh], refs[nh:nh + len(metas)]
    own, stats, prob, hot, facts, lines, rows, score = refs[nh + len(metas):]
    load_rows(hid, rows)
    count, model = rows.shape
    apart, place = aims(me_ref, hid, local)
    top2, total2, aim2 = scores_of(rows, words, metas, apart, place, score, prob, hot)
    top1, total1, aim1 = (stats[:, i * LANES:i * LANES + 1] for i in range(3))
    top = jnp.maximum(top1, top2)
    total = jnp.exp(top1 - top) * total1 + jnp.exp(top2 - top) * total2
    inside = sum(jnp.where(apart == bits, 1.0, 0.0) for bits in group)
    facts[:, 0:LANES] = jnp.broadcast_to(top2, (count, LANES))
    facts[:, LANES:2 * LANES] = jnp.broadcast_to(inside, (count, LANES))
    per = count // LANES
    to_lines(top + jnp.log(total), lines, 0)
    to_lines(aim1 + aim2, lines, per)
    centre = jnp.sum(own[0:LANES, :].astype(f32), axis=0, keepdims=True) * (1.0 / LANES)
    for n in range(model // LANES):
        lines[2 * per + n:2 * per + n + 1, :] = centre[:, n * LANES:(n + 1) * LANES]


def last_scores(me, hid, words, metas, group, local, own, stats):
    model = own.shape[1]
    rows = stats.shape[0]
    count = sum(w.shape[0] for w in words)
    return pl.pallas_call(
        functools.partial(last_kernel, nh=len(hid), metas=metas, group=group, local=local),
        out_shape=[jax.ShapeDtypeStruct((rows, count), bf16)] * 2 + [
            jax.ShapeDtypeStruct((rows, 2 * LANES), f32),
            jax.ShapeDtypeStruct((2 * rows // LANES + model // LANES, LANES), f32)],
        in_specs=[SM] + [VM] * (len(hid) + len(words) + 2), out_specs=[VM] * 4,
        scratch_shapes=[pltpu.VMEM((rows, model), bf16), pltpu.VMEM((rows, count), f32)],
        compiler_params=params(), cost_estimate=cost(2 * rows * count * model, 2 * (rows + count) * model),
        name="last_scores",
    )(me, *hid, *words, own, stats)


def close_kernel(*refs, flips, nw):
    nl = len(flips)
    lines, words, rest = refs[:4], refs[4:4 + nw], refs[4 + nw:]
    prob, hot, one, before, stats, facts = rest[:6]
    parts, loss = rest[6:10], rest[10]
    size = lines[0].shape[0] * 4 // nl
    count, model = one.shape
    per = count // LANES
    quarter = count // 4

    def line(j, i, kind):
        over, halves = flips[j]
        at = j % (nl // 4) * size + kind * per + (i ^ over)
        v = lines[j // (nl // 4)][at:at + 1, :]
        return pltpu.roll(v, LANES // 2, axis=1) if halves else v

    scales = []
    for i in range(per):
        each = [line(j, i, 0) for j in range(nl)]
        top = functools.reduce(jnp.maximum, each)
        whole = top + jnp.log(sum(jnp.exp(v - top) for v in each))
        if i == 0:
            loss[...] = whole - sum(line(j, i, 1) for j in range(nl))
        weight = jnp.broadcast_to(jnp.exp(each[0] - whole), (LANES, LANES)).T
        whole = jnp.broadcast_to(whole, (LANES, LANES)).T
        part = slice(i * LANES, (i + 1) * LANES)
        scales.append((jnp.exp(stats[part, 0:LANES] - whole)[:, 0:1], jnp.exp(facts[part, 0:LANES] - whole)[:, 0:1],
                       (facts[part, LANES:2 * LANES] - weight)[:, 0:1]))
    c1, c2, c3 = (jnp.concatenate(c, axis=0) for c in zip(*scales))
    for n in range(0, model, 256):
        cols = slice(n, n + 256)
        mu = jnp.concatenate([
            sum(ref[at + 2 * per + m // LANES:at + 2 * per + m // LANES + 1, :]
                for ref in lines for at in range(0, ref.shape[0], size)) * (1.0 / nl)
            for m in range(n, n + 256, LANES)], axis=1)
        goal = product(hot, words, n, 256) + before[:, cols].astype(f32)
        mix = (c1 * one[:, cols] + c2 * product(prob, words, n, 256) + (c3 * mu - goal)).astype(bf16)
        for q in range(4):
            parts[q][:, cols] = mix[q * quarter:(q + 1) * quarter]


def close(lines, flips, words, prob, hot, one, before, stats, facts):
    rows, model = one.shape
    side = jax.ShapeDtypeStruct((rows // 4, model), bf16)
    return pl.pallas_call(
        functools.partial(close_kernel, flips=flips, nw=len(words)),
        out_shape=[side] * 4 + [jax.ShapeDtypeStruct((1, LANES), f32)],
        in_specs=[VM] * (len(lines) + len(words) + 6), out_specs=[VM] * 5, compiler_params=params(),
        cost_estimate=cost(4 * rows * prob.shape[1] * model, 8 * rows * model), name="close",
    )(*lines, *words, prob, hot, one, before, stats, facts)


def plus(a, b):
    return (a.astype(f32) + b.astype(f32)).astype(bf16)


def add_kernel(*refs):
    n = len(refs) // 4
    for i in range(n):
        keep, got = refs[2 * i:2 * i + 2]
        first, second = refs[2 * n + 2 * i:2 * n + 2 * i + 2]
        rows = first.shape[0]
        first[...] = plus(keep[0:rows, :], got[0:rows, :])
        second[...] = plus(keep[rows:2 * rows, :], got[rows:2 * rows, :])


def add_halves(*pairs):
    outs = [jax.ShapeDtypeStruct((p.shape[0] // 2, p.shape[1]), bf16) for p in pairs]
    return pl.pallas_call(
        add_kernel, out_shape=outs, in_specs=[VM] * len(pairs), out_specs=[VM] * len(pairs),
        compiler_params=params(), cost_estimate=cost(pairs[0].size, 8 * pairs[0].size), name="add_halves",
    )(*pairs)


def add_four_kernel(*refs):
    parts, halves = refs[:4], refs[4:]
    rows = halves[0].shape[0]
    for i, out in enumerate(halves):
        part = slice(i * rows, (i + 1) * rows)
        out[...] = sum(ref[part, :].astype(f32) for ref in parts).astype(bf16)


def add_four(*parts):
    rows, model = parts[0].shape
    return pl.pallas_call(
        add_four_kernel, out_shape=[jax.ShapeDtypeStruct((rows // 2, model), bf16)] * 2,
        in_specs=[VM] * 4, out_specs=[VM] * 2,
        compiler_params=params(), cost_estimate=cost(4 * rows * model, 10 * rows * model), name="add_four",
    )(*parts)


def per_device(char_ids, char_table, conv_weight, proj_weight, gate_weight, trans_weight, gate_bias, hidden, targets,
               *, vocab, blk):
    devices = vocab * blk
    axes = ("vocab", "blk")

    def swap(x, bits):
        return lax.ppermute(x, axes, [(i, i ^ bits) for i in range(devices)])

    core, near = blk, 1
    bit_a, bit_b = 2 * blk, 4 * blk
    rest = [1 << i for i in range(1, blk.bit_length() - 1)] + [
        blk << i for i in range(3, vocab.bit_length() - 1)]
    me = lax.axis_index("vocab") * blk + lax.axis_index("blk")
    local, length = char_ids.shape
    mine = hidden.shape[0]

    rows, goal = hidden, targets.reshape(1, mine)
    for bit in rest:
        rows = jnp.concatenate([rows, swap(rows, bit)], axis=0)
        goal = jnp.concatenate([goal, swap(goal, bit)], axis=1)
    weights = (char_table.T, conv_weight, proj_weight, gate_weight, trans_weight, gate_bias)
    many = 4 * (mine << len(rest)) > local
    size = local // 2
    marks = (0, size)
    ids = char_ids.T
    e0 = embed(ids, length, 0, size, *weights)
    e0, rows, goal = lax.optimization_barrier((e0, rows, goal))
    goal = goal.reshape(-1, 1)
    code = jnp.concatenate([goal // 256, goal % 256], axis=1).astype(bf16)
    rows = jnp.concatenate([rows, jnp.pad(code, ((0, 0), (0, LANES - 2)))], axis=1)
    hid = [rows] + [swap(rows, b) for b in (bit_b, bit_a, bit_a | bit_b)]
    e1 = embed(ids, length, size, local - size, *weights)
    held, *hid = lax.optimization_barrier((e1, *hid))
    pieces = [e0, held]
    cores = [swap(e, core) for e in pieces]
    nears = [swap(e, near) for e in pieces]
    held, nears[0] = lax.optimization_barrier((held, nears[0]))
    far = swap(nears[0], core)

    me = me.astype(jnp.int32).reshape(1)
    meta = [tuple((bits, m) for m in marks) for bits in (0, core, near, core | near)]
    early = [(nears[0], meta[2][0]), (far, meta[3][0])]
    late = []
    if many:
        early, late = [], early
    words = pieces + cores + [w for w, _ in early]
    one, target, stats = first_fold(me, hid, words, meta[0] + meta[1] + tuple(m for _, m in early), local)
    held, stats = lax.optimization_barrier((nears[1], stats))
    late += [(held, meta[2][1]), (swap(held, core), meta[3][1])]
    words, metas = [w for w, _ in late], tuple(m for _, m in late)
    prob, hot, facts, line = last_scores(
        me, hid, words, metas, (0, core, near, core | near), local, e0, stats)
    lines, others = line, [0]
    for bit in rest:
        lines = jnp.concatenate([lines, swap(lines, bit)], axis=0)
        others += [o | bit for o in others]
    plane = (bit_b, bit_a, bit_a | bit_b)
    lines = [lines] + [swap(lines, o) for o in plane]
    others = [o | p for p in (0,) + plane for o in others]
    order = rest + [bit_b, bit_a]
    flips = tuple((sum(1 << (j - 1) for j, b in enumerate(order) if j and o & b), bool(o & rest[0])) for o in others)
    *parts, loss = close(lines, flips, words, prob, hot, one, target, stats, facts)
    far_part = swap(parts[3], bit_a | bit_b)
    keep, send = add_four(parts[0], swap(parts[1], bit_b), swap(parts[2], bit_a), far_part)
    for bit in rest[:0:-1]:
        keep, send = add_halves(keep, swap(send, bit))
    grad = plus(keep, swap(send, rest[0]))
    return loss[0, :mine], grad


def solution(mesh):
    words = P(("vocab", "blk"))
    return jax.shard_map(
        functools.partial(per_device, vocab=mesh.shape["vocab"], blk=mesh.shape["blk"]),
        mesh=mesh,
        in_specs=(P(("vocab", "blk"), None), P(), P(), P(), P(), P(), P(), P(("vocab", "blk"), None), words),
        out_specs=(words, P(("vocab", "blk"), None)),
        check_vma=False,
    )
```

```python
import functools
import jax
import jax.numpy as jnp
from jax import lax
from jax.experimental import pallas as pl
from jax.experimental.pallas import tpu as pltpu
from jax.sharding import PartitionSpec as P

bf16=jnp.bfloat16; f32=jnp.float32
LANES = 128
SPAN = 8


def prep_toeplitz(conv_ref, toep, ce, k, filters):
    depth = toep.shape[0]
    rows = (k + 1) * ce
    piece = conv_ref[0:rows, k * filters:(k + 1) * filters]
    for o in range(SPAN):
        cols = slice((k * SPAN + o) * filters, (k * SPAN + o + 1) * filters)
        if o:
            toep[0:o * ce, cols] = jnp.zeros((o * ce, filters), bf16)
        toep[o * ce:o * ce + rows, cols] = piece
        rest = depth - o * ce - rows
        if rest:
            toep[o * ce + rows:depth, cols] = jnp.zeros((rest, filters), bf16)


def lookup(ids_ref, start, words, tab_ref, vec, length, ce, g):
    per = LANES // ce
    low_tab = tab_ref[:, 0:LANES].astype(f32)
    top_tab = tab_ref[:, LANES:2 * LANES].astype(f32)
    first = start // LANES * LANES
    for tile in range(first, start + words, LANES):
        low_word, high_word = max(tile, start), min(tile + LANES, start + words)
        parts = []
        for p in range(g * per, (g + 1) * per):
            if p >= length:
                parts.append(jnp.zeros((ce, LANES), f32))
                continue
            idx = jnp.broadcast_to(ids_ref[p:p + 1, tile:tile + LANES], (8, LANES))
            low = jnp.bitwise_and(idx, LANES - 1)
            top = idx >= LANES
            for h in range(0, ce, 8):
                one = jnp.take_along_axis(low_tab[h:h + 8], low, axis=1)
                two = jnp.take_along_axis(top_tab[h:h + 8], low, axis=1)
                parts.append(jnp.where(top, two, one))
        block = jnp.concatenate(parts, axis=0).T.astype(bf16)
        vec[low_word - start:high_word - start, g * LANES:(g + 1) * LANES] = block[low_word - tile:high_word - tile]


def conv_pool(vec, toep, acc, length, widths, filters, look, build):
    def tile(k, o, lhs):
        cols = slice((k * SPAN + o) * filters, (k * SPAN + o + 2) * filters)
        return jnp.dot(lhs, toep[:, cols], preferred_element_type=f32)
    acc[...] = jnp.full(acc.shape, -jnp.inf, f32)
    look(0)
    for b in range(-(-length // SPAN)):
        look(b + 1)
        lhs = vec[:, b * LANES:(b + 2) * LANES]
        for k in range(widths):
            usable = min(SPAN, length - k - b * SPAN)
            if usable <= 0:
                continue
            if b == 0:
                build(k)
            best = acc[:, k * filters:(k + 1) * filters]
            for o in range(0, usable, 2):
                r = tile(k, o, lhs)
                best = jnp.maximum(best, r[:, :filters])
                if o + 1 < usable:
                    best = jnp.maximum(best, r[:, filters:])
            acc[:, k * filters:(k + 1) * filters] = best


def cnn_kernel(ids_ref, tab_ref, conv_ref, bias_ref, proj_hbm, gate_hbm, trans_hbm, *rest,
               widths, filters, ce, length, layers, nt, start):
    out_ref, vec, toep, acc, feat, proj, gate, trans, state, last, sems = rest
    copies = [pltpu.make_async_copy(s, d, sems.at[i]) for i, (s, d) in enumerate(
        ((proj_hbm, proj), (gate_hbm, gate), (trans_hbm, trans)))]
    for c in copies:
        c.start()
    words = out_ref.shape[0]
    conv_pool(
        vec, toep, acc, length, widths, filters,
        lambda g: lookup(ids_ref, start, words, tab_ref, vec, length, ce, g),
        lambda k: prep_toeplitz(conv_ref, toep, ce, k, filters))
    for c in copies:
        c.wait()
    feat[...] = jnp.tanh(acc[...]).astype(bf16)
    model = last.shape[1]
    for n in range(0, model, nt):
        state[:, n:n + nt] = jnp.dot(feat[...], proj[:, n:n + nt], preferred_element_type=f32).astype(bf16)
    for l in range(layers):
        for n in range(0, model, nt):
            cur = state[...]
            g = jnp.dot(cur, gate[l, :, n:n + nt], preferred_element_type=f32) + bias_ref[l:l + 1, n:n + nt]
            t = jnp.dot(cur, trans[l, :, n:n + nt], preferred_element_type=f32)
            opened = jax.nn.sigmoid(g)
            carried = jnp.maximum(t, 0.0)
            new = (opened * carried + (1.0 - opened) * state[:, n:n + nt].astype(f32)).astype(bf16)
            if l + 1 < layers:
                last[:, n:n + nt] = new
            else:
                out_ref[:, n:n + nt] = new
        if l + 1 < layers:
            state[...] = last[...]


ANY = pl.BlockSpec(memory_space=pl.ANY)
VM = pl.BlockSpec(memory_space=pltpu.VMEM)


def params(limit_mib=56):
    return pltpu.CompilerParams(vmem_limit_bytes=limit_mib << 20)


def embed(ids, length, start, words, tab_t, conv_weight, proj_weight, gate_weight, trans_weight, gate_bias, nt=256):
    ce = tab_t.shape[0]
    widths = conv_weight.shape[0] // ce
    filters = conv_weight.shape[1] // widths
    layers, model, _ = gate_weight.shape
    flops = 2 * words * (length * 256 * widths * filters + widths * filters * model + 2 * layers * model * model)
    return pl.pallas_call(
        functools.partial(cnn_kernel, widths=widths, filters=filters, ce=ce, length=length, layers=layers, nt=nt,
                          start=start),
        out_shape=jax.ShapeDtypeStruct((words, model), bf16),
        in_specs=[VM, VM, VM, VM, ANY, ANY, ANY],
        out_specs=VM,
        scratch_shapes=[
            pltpu.VMEM((words, (-(-length // SPAN) + 1) * LANES), bf16),
            pltpu.VMEM((2 * LANES, widths * SPAN * filters), bf16),
            pltpu.VMEM((words, widths * filters), f32),
            pltpu.VMEM((words, widths * filters), bf16),
            pltpu.VMEM(proj_weight.shape, bf16),
            pltpu.VMEM(gate_weight.shape, bf16),
            pltpu.VMEM(trans_weight.shape, bf16),
            pltpu.VMEM((words, model), bf16),
            pltpu.VMEM((words, model), bf16),
            pltpu.SemaphoreType.DMA((3,)),
        ],
        compiler_params=params(),
        cost_estimate=pl.CostEstimate(flops=flops, bytes_accessed=12 << 20, transcendentals=words * 4096),
        name="embed",
    )(ids, tab_t, conv_weight, gate_bias, proj_weight, gate_weight, trans_weight)


def as_line(column):
    return jnp.broadcast_to(column, (LANES, LANES)).T[0:1, :]


def to_lines(column, out, at):
    for i in range(column.shape[0] // LANES):
        out[at + i:at + i + 1, :] = as_line(column[i * LANES:(i + 1) * LANES, :])


def aims(me_ref, hid, local):
    model = hid[0].shape[1] - LANES
    apart, place = [], []
    for h in hid:
        code = h[:, model:model + LANES].astype(f32).astype(jnp.int32)
        goal = code[:, 0:1] * 256 + code[:, 1:2]
        owner = lax.div(goal, local)
        apart.append(jnp.bitwise_xor(owner, me_ref[0]))
        place.append(goal - owner * local)
    return jnp.concatenate(apart, axis=0), jnp.concatenate(place, axis=0)


def spots(apart, place, meta):
    bits, start = meta
    return jnp.where(apart == bits, place - start, -1)


def scores_of(rows, words, metas, apart, place, score, prob, hot):
    at, top, aim = 0, None, None
    for ref, meta in zip(words, metas):
        n = ref.shape[0]
        piece = lax.dot_general(rows[...], ref[...], (((1,), (1,)), ((), ())), preferred_element_type=f32)
        score[:, at:at + n] = piece
        hit = lax.broadcasted_iota(jnp.int32, piece.shape, 1) == spots(apart, place, meta)
        hot[:, at:at + n] = jnp.where(hit, 1.0, 0.0).astype(bf16)
        part = jnp.sum(jnp.where(hit, piece, 0.0), axis=1, keepdims=True)
        best = jnp.max(piece, axis=1, keepdims=True)
        top = best if top is None else jnp.maximum(top, best)
        aim = part if aim is None else aim + part
        at += n
    at, total = 0, None
    for ref in words:
        n = ref.shape[0]
        w = jnp.exp(score[:, at:at + n] - top).astype(bf16)
        prob[:, at:at + n] = w
        part = jnp.sum(w.astype(f32), axis=1, keepdims=True)
        total = part if total is None else total + part
        at += n
    return top, total, aim


def product(left, words, n, size):
    at, res = 0, None
    for ref in words:
        count = ref.shape[0]
        d = jnp.dot(left[:, at:at + count], ref[:, n:n + size], preferred_element_type=f32)
        res = d if res is None else res + d
        at += count
    return res


def pack(columns, out):
    lane = lax.broadcasted_iota(jnp.int32, out.shape, 1)
    res = jnp.zeros(out.shape, f32)
    for i, column in enumerate(columns):
        res = jnp.where(lane == i, column, res)
    out[...] = res


def load_rows(hid, rows):
    at = 0
    for h in hid:
        rows[at:at + h.shape[0], :] = h[:, 0:rows.shape[1]]
        at += h.shape[0]


def first_kernel(me_ref, *refs, nh, metas, local):
    hid, words = refs[:nh], refs[nh:nh + len(metas)]
    out, target, stats, rows, score, prob, hot = refs[nh + len(metas):]
    load_rows(hid, rows)
    each = scores_of(rows, words, metas, *aims(me_ref, hid, local), score, prob, hot)
    pack(each, stats)
    for n in range(0, out.shape[1], 256):
        out[:, n:n + 256] = product(prob, words, n, 256)
        target[:, n:n + 256] = product(hot, words, n, 256).astype(bf16)


def cost(flops, size, trans=0):
    return pl.CostEstimate(flops=flops, bytes_accessed=size, transcendentals=trans)


SM = pl.BlockSpec(memory_space=pltpu.SMEM)


def first_fold(me, hid, words, metas, local):
    model = words[0].shape[1]
    rows = sum(h.shape[0] for h in hid)
    count = sum(w.shape[0] for w in words)
    return pl.pallas_call(
        functools.partial(first_kernel, nh=len(hid), metas=metas, local=local),
        out_shape=[jax.ShapeDtypeStruct((rows, model), f32), jax.ShapeDtypeStruct((rows, model), bf16),
                   jax.ShapeDtypeStruct((rows, LANES), f32)],
        in_specs=[SM] + [VM] * (len(hid) + len(words)), out_specs=[VM] * 3,
        scratch_shapes=[pltpu.VMEM((rows, model), bf16), pltpu.VMEM((rows, count), f32),
                        pltpu.VMEM((rows, count), bf16), pltpu.VMEM((rows, count), bf16)],
        compiler_params=params(), cost_estimate=cost(6 * rows * count * model, 2 * (rows + count) * model),
        name="first_fold",
    )(me, *hid, *words)


def last_kernel(me_ref, *refs, nh, metas, group, local):
    hid, words = refs[:nh], refs[nh:nh + len(metas)]
    stats, prob, hot, facts, lines, rows, score = refs[nh + len(metas):]
    load_rows(hid, rows)
    count, model = rows.shape
    apart, place = aims(me_ref, hid, local)
    top2, total2, aim2 = scores_of(rows, words, metas, apart, place, score, prob, hot)
    top1, total1, aim1 = (stats[:, i:i + 1] for i in range(3))
    top = jnp.maximum(top1, top2)
    total = jnp.exp(top1 - top) * total1 + jnp.exp(top2 - top) * total2
    inside = sum(jnp.where(apart == bits, 1.0, 0.0) for bits in group)
    pack((top2, inside), facts)
    per = count // LANES
    to_lines(top + jnp.log(total), lines, 0)
    to_lines(aim1 + aim2, lines, per)
    centre = jnp.sum(words[0][0:LANES, :].astype(f32), axis=0, keepdims=True) * (1.0 / LANES)
    for n in range(model // LANES):
        lines[2 * per + n:2 * per + n + 1, :] = centre[:, n * LANES:(n + 1) * LANES]


def last_scores(me, hid, words, metas, group, local, stats):
    model = words[0].shape[1]
    rows = stats.shape[0]
    count = sum(w.shape[0] for w in words)
    return pl.pallas_call(
        functools.partial(last_kernel, nh=len(hid), metas=metas, group=group, local=local),
        out_shape=[jax.ShapeDtypeStruct((rows, count), bf16)] * 2 + [
            jax.ShapeDtypeStruct((rows, LANES), f32),
            jax.ShapeDtypeStruct((2 * rows // LANES + model // LANES, LANES), f32)],
        in_specs=[SM] + [VM] * (len(hid) + len(words) + 1), out_specs=[VM] * 4,
        scratch_shapes=[pltpu.VMEM((rows, model), bf16), pltpu.VMEM((rows, count), f32)],
        compiler_params=params(), cost_estimate=cost(2 * rows * count * model, 2 * (rows + count) * model),
        name="last_scores",
    )(me, *hid, *words, stats)


def close_kernel(*refs, flips, nw):
    nl = len(flips)
    lines, words, rest = refs[:4], refs[4:4 + nw], refs[4 + nw:]
    prob, hot, one, before, stats, facts = rest[:6]
    parts, loss = rest[6:10], rest[10]
    size = lines[0].shape[0] * 4 // nl
    count, model = one.shape
    per = count // LANES
    quarter = count // 4

    def line(j, i, kind):
        over, halves = flips[j]
        at = j % (nl // 4) * size + kind * per + (i ^ over)
        v = lines[j // (nl // 4)][at:at + 1, :]
        return pltpu.roll(v, LANES // 2, axis=1) if halves else v

    scales = []
    for i in range(per):
        each = [line(j, i, 0) for j in range(nl)]
        top = functools.reduce(jnp.maximum, each)
        whole = top + jnp.log(sum(jnp.exp(v - top) for v in each))
        if i == 0:
            loss[...] = whole - sum(line(j, i, 1) for j in range(nl))
        weight = jnp.broadcast_to(jnp.exp(each[0] - whole), (LANES, LANES)).T
        whole = jnp.broadcast_to(whole, (LANES, LANES)).T
        part = slice(i * LANES, (i + 1) * LANES)
        scales.append((jnp.exp(stats[part, 0:1] - whole[:, 0:1]), jnp.exp(facts[part, 0:1] - whole[:, 0:1]),
                       facts[part, 1:2] - weight[:, 0:1]))
    c1, c2, c3 = (jnp.concatenate(c, axis=0) for c in zip(*scales))
    for n in range(0, model, 256):
        cols = slice(n, n + 256)
        mu = jnp.concatenate([
            sum(ref[at + 2 * per + m // LANES:at + 2 * per + m // LANES + 1, :]
                for ref in lines for at in range(0, ref.shape[0], size)) * (1.0 / nl)
            for m in range(n, n + 256, LANES)], axis=1)
        goal = product(hot, words, n, 256) + before[:, cols].astype(f32)
        mix = (c1 * one[:, cols] + c2 * product(prob, words, n, 256) + (c3 * mu - goal)).astype(bf16)
        for q in range(4):
            parts[q][:, cols] = mix[q * quarter:(q + 1) * quarter]


def close(lines, flips, words, prob, hot, one, before, stats, facts):
    rows, model = one.shape
    side = jax.ShapeDtypeStruct((rows // 4, model), bf16)
    return pl.pallas_call(
        functools.partial(close_kernel, flips=flips, nw=len(words)),
        out_shape=[side] * 4 + [jax.ShapeDtypeStruct((1, LANES), f32)],
        in_specs=[VM] * (len(lines) + len(words) + 6), out_specs=[VM] * 5, compiler_params=params(),
        cost_estimate=cost(4 * rows * prob.shape[1] * model, 8 * rows * model), name="close",
    )(*lines, *words, prob, hot, one, before, stats, facts)


def plus(a, b):
    return (a.astype(f32) + b.astype(f32)).astype(bf16)


def add_kernel(*refs):
    n = len(refs) // 4
    for i in range(n):
        keep, got = refs[2 * i:2 * i + 2]
        first, second = refs[2 * n + 2 * i:2 * n + 2 * i + 2]
        rows = first.shape[0]
        first[...] = plus(keep[0:rows, :], got[0:rows, :])
        second[...] = plus(keep[rows:2 * rows, :], got[rows:2 * rows, :])


def add_halves(*pairs):
    outs = [jax.ShapeDtypeStruct((p.shape[0] // 2, p.shape[1]), bf16) for p in pairs]
    return pl.pallas_call(
        add_kernel, out_shape=outs, in_specs=[VM] * len(pairs), out_specs=[VM] * len(pairs),
        compiler_params=params(), cost_estimate=cost(pairs[0].size, 8 * pairs[0].size), name="add_halves",
    )(*pairs)


def add_four_kernel(*refs):
    parts, halves = refs[:4], refs[4:]
    rows = halves[0].shape[0]
    for i, out in enumerate(halves):
        part = slice(i * rows, (i + 1) * rows)
        out[...] = sum(ref[part, :].astype(f32) for ref in parts).astype(bf16)


def add_four(*parts):
    rows, model = parts[0].shape
    return pl.pallas_call(
        add_four_kernel, out_shape=[jax.ShapeDtypeStruct((rows // 2, model), bf16)] * 2,
        in_specs=[VM] * 4, out_specs=[VM] * 2,
        compiler_params=params(), cost_estimate=cost(4 * rows * model, 10 * rows * model), name="add_four",
    )(*parts)


def per_device(char_ids, char_table, conv_weight, proj_weight, gate_weight, trans_weight, gate_bias, hidden, targets,
               *, vocab, blk):
    devices = vocab * blk
    axes = ("vocab", "blk")

    def swap(x, bits):
        return lax.ppermute(x, axes, [(i, i ^ bits) for i in range(devices)])

    core, near = blk, 1
    bit_a, bit_b = 2 * blk, 4 * blk
    rest = [1 << i for i in range(1, blk.bit_length() - 1)] + [
        blk << i for i in range(3, vocab.bit_length() - 1)]
    me = lax.axis_index("vocab") * blk + lax.axis_index("blk")
    local, length = char_ids.shape
    mine = hidden.shape[0]

    rows, goal = hidden, targets.reshape(1, mine)
    for bit in rest:
        rows = jnp.concatenate([rows, swap(rows, bit)], axis=0)
        goal = jnp.concatenate([goal, swap(goal, bit)], axis=1)
    weights = (char_table.T, conv_weight, proj_weight, gate_weight, trans_weight, gate_bias)
    many = 4 * (mine << len(rest)) > local
    size = local // 2
    marks = (0, size)
    ids = char_ids.T
    e0 = embed(ids, length, 0, size, *weights)
    e0, rows, goal = lax.optimization_barrier((e0, rows, goal))
    goal = goal.reshape(-1, 1)
    code = jnp.concatenate([goal // 256, goal % 256], axis=1).astype(bf16)
    rows = jnp.concatenate([rows, jnp.pad(code, ((0, 0), (0, LANES - 2)))], axis=1)
    hid = [rows] + [swap(rows, b) for b in (bit_b, bit_a, bit_a | bit_b)]
    e1 = embed(ids, length, size, local - size, *weights)
    held, *hid = lax.optimization_barrier((e1, *hid))
    pieces = [e0, held]
    cores = [swap(e, core) for e in pieces]
    nears = [swap(e, near) for e in pieces]
    held, nears[0] = lax.optimization_barrier((held, nears[0]))
    far = swap(nears[0], core)

    me = me.astype(jnp.int32).reshape(1)
    meta = [tuple((bits, m) for m in marks) for bits in (0, core, near, core | near)]
    early = [(nears[0], meta[2][0]), (far, meta[3][0])]
    late = []
    if many:
        early, late = [], early
    words = pieces + cores + [w for w, _ in early]
    one, target, stats = first_fold(me, hid, words, meta[0] + meta[1] + tuple(m for _, m in early), local)
    held, stats = lax.optimization_barrier((nears[1], stats))
    late += [(held, meta[2][1]), (swap(held, core), meta[3][1])]
    words, metas = [w for w, _ in late], tuple(m for _, m in late)
    prob, hot, facts, line = last_scores(
        me, hid, words, metas, (0, core, near, core | near), local, stats)
    lines, others = line, [0]
    for bit in rest:
        lines = jnp.concatenate([lines, swap(lines, bit)], axis=0)
        others += [o | bit for o in others]
    plane = (bit_b, bit_a, bit_a | bit_b)
    lines = [lines] + [swap(lines, o) for o in plane]
    others = [o | p for p in (0,) + plane for o in others]
    order = rest + [bit_b, bit_a]
    flips = tuple((sum(1 << (j - 1) for j, b in enumerate(order) if j and o & b), bool(o & rest[0])) for o in others)
    *parts, loss = close(lines, flips, words, prob, hot, one, target, stats, facts)
    far_part = swap(parts[3], bit_a | bit_b)
    keep, send = add_four(parts[0], swap(parts[1], bit_b), swap(parts[2], bit_a), far_part)
    for bit in rest[:0:-1]:
        keep, send = add_halves(keep, swap(send, bit))
    grad = plus(keep, swap(send, rest[0]))
    return loss[0, :mine], grad


def solution(mesh):
    words = P(("vocab", "blk"))
    return jax.shard_map(
        functools.partial(per_device, vocab=mesh.shape["vocab"], blk=mesh.shape["blk"]),
        mesh=mesh,
        in_specs=(P(("vocab", "blk"), None), P(), P(), P(), P(), P(), P(), P(("vocab", "blk"), None), words),
        out_specs=(words, P(("vocab", "blk"), None)),
        check_vma=False,
    )
```

```python
import functools
import jax
import jax.numpy as jnp
from jax import lax
from jax.experimental import pallas as pl
from jax.experimental.pallas import tpu as pltpu
from jax.sharding import PartitionSpec as P

bf16=jnp.bfloat16; f32=jnp.float32
LANES = 128
SPAN = 8


def prep_toeplitz(conv_ref, toep, ce, k, filters):
    depth = toep.shape[0]
    rows = (k + 1) * ce
    piece = conv_ref[0:rows, k * filters:(k + 1) * filters]
    for o in range(SPAN):
        cols = slice((k * SPAN + o) * filters, (k * SPAN + o + 1) * filters)
        if o:
            toep[0:o * ce, cols] = jnp.zeros((o * ce, filters), bf16)
        toep[o * ce:o * ce + rows, cols] = piece
        rest = depth - o * ce - rows
        if rest:
            toep[o * ce + rows:depth, cols] = jnp.zeros((rest, filters), bf16)


def lookup(ids_ref, start, words, tab_ref, vec, length, ce, g):
    per = LANES // ce
    low_tab = tab_ref[:, 0:LANES].astype(f32)
    top_tab = tab_ref[:, LANES:2 * LANES].astype(f32)
    first = start // LANES * LANES
    for tile in range(first, start + words, LANES):
        low_word, high_word = max(tile, start), min(tile + LANES, start + words)
        parts = []
        for p in range(g * per, (g + 1) * per):
            if p >= length:
                parts.append(jnp.zeros((ce, LANES), f32))
                continue
            idx = jnp.broadcast_to(ids_ref[p:p + 1, tile:tile + LANES], (8, LANES))
            low = jnp.bitwise_and(idx, LANES - 1)
            top = idx >= LANES
            for h in range(0, ce, 8):
                one = jnp.take_along_axis(low_tab[h:h + 8], low, axis=1)
                two = jnp.take_along_axis(top_tab[h:h + 8], low, axis=1)
                parts.append(jnp.where(top, two, one))
        block = jnp.concatenate(parts, axis=0).T.astype(bf16)
        vec[low_word - start:high_word - start, g * LANES:(g + 1) * LANES] = block[low_word - tile:high_word - tile]


def conv_pool(vec, toep, acc, length, widths, filters, look, build):
    ce = toep.shape[0] // (2 * SPAN)

    def tile(k, o, lhs):
        cols = slice((k * SPAN + o) * filters, (k * SPAN + o + 2) * filters)
        depth = LANES if (o + k + 2) * ce <= LANES else 2 * LANES
        return jnp.dot(lhs[:, 0:depth], toep[0:depth, cols], preferred_element_type=f32)
    acc[...] = jnp.full(acc.shape, -jnp.inf, f32)
    look(0)
    for b in range(-(-length // SPAN)):
        look(b + 1)
        lhs = vec[:, b * LANES:(b + 2) * LANES]
        for k in range(widths):
            usable = min(SPAN, length - k - b * SPAN)
            if usable <= 0:
                continue
            if b == 0:
                build(k)
            best = acc[:, k * filters:(k + 1) * filters]
            for o in range(0, usable, 2):
                r = tile(k, o, lhs)
                best = jnp.maximum(best, r[:, :filters])
                if o + 1 < usable:
                    best = jnp.maximum(best, r[:, filters:])
            acc[:, k * filters:(k + 1) * filters] = best


def cnn_kernel(ids_ref, tab_ref, conv_ref, bias_ref, proj_hbm, gate_hbm, trans_hbm, *rest,
               widths, filters, ce, length, layers, nt, start):
    out_ref, vec, toep, acc, feat, proj, gate, trans, state, last, sems = rest
    copies = [pltpu.make_async_copy(s, d, sems.at[i]) for i, (s, d) in enumerate(
        ((proj_hbm, proj), (gate_hbm, gate), (trans_hbm, trans)))]
    for c in copies:
        c.start()
    words = out_ref.shape[0]
    conv_pool(
        vec, toep, acc, length, widths, filters,
        lambda g: lookup(ids_ref, start, words, tab_ref, vec, length, ce, g),
        lambda k: prep_toeplitz(conv_ref, toep, ce, k, filters))
    for c in copies:
        c.wait()
    feat[...] = jnp.tanh(acc[...]).astype(bf16)
    model = last.shape[1]
    for n in range(0, model, nt):
        state[:, n:n + nt] = jnp.dot(feat[...], proj[:, n:n + nt], preferred_element_type=f32).astype(bf16)
    for l in range(layers):
        for n in range(0, model, nt):
            cur = state[...]
            g = jnp.dot(cur, gate[l, :, n:n + nt], preferred_element_type=f32) + bias_ref[l:l + 1, n:n + nt]
            t = jnp.dot(cur, trans[l, :, n:n + nt], preferred_element_type=f32)
            opened = jax.nn.sigmoid(g)
            carried = jnp.maximum(t, 0.0)
            new = (opened * carried + (1.0 - opened) * state[:, n:n + nt].astype(f32)).astype(bf16)
            if l + 1 < layers:
                last[:, n:n + nt] = new
            else:
                out_ref[:, n:n + nt] = new
        if l + 1 < layers:
            state[...] = last[...]


ANY = pl.BlockSpec(memory_space=pl.ANY)
VM = pl.BlockSpec(memory_space=pltpu.VMEM)


def params(limit_mib=56):
    return pltpu.CompilerParams(vmem_limit_bytes=limit_mib << 20)


def embed(ids, length, start, words, tab_t, conv_weight, proj_weight, gate_weight, trans_weight, gate_bias, nt=256):
    ce = tab_t.shape[0]
    widths = conv_weight.shape[0] // ce
    filters = conv_weight.shape[1] // widths
    layers, model, _ = gate_weight.shape
    flops = 2 * words * (length * 256 * widths * filters + widths * filters * model + 2 * layers * model * model)
    return pl.pallas_call(
        functools.partial(cnn_kernel, widths=widths, filters=filters, ce=ce, length=length, layers=layers, nt=nt,
                          start=start),
        out_shape=jax.ShapeDtypeStruct((words, model), bf16),
        in_specs=[VM, VM, VM, VM, ANY, ANY, ANY],
        out_specs=VM,
        scratch_shapes=[
            pltpu.VMEM((words, (-(-length // SPAN) + 1) * LANES), bf16),
            pltpu.VMEM((2 * LANES, widths * SPAN * filters), bf16),
            pltpu.VMEM((words, widths * filters), f32),
            pltpu.VMEM((words, widths * filters), bf16),
            pltpu.VMEM(proj_weight.shape, bf16),
            pltpu.VMEM(gate_weight.shape, bf16),
            pltpu.VMEM(trans_weight.shape, bf16),
            pltpu.VMEM((words, model), bf16),
            pltpu.VMEM((words, model), bf16),
            pltpu.SemaphoreType.DMA((3,)),
        ],
        compiler_params=params(),
        cost_estimate=pl.CostEstimate(flops=flops, bytes_accessed=12 << 20, transcendentals=words * 4096),
        name="embed",
    )(ids, tab_t, conv_weight, gate_bias, proj_weight, gate_weight, trans_weight)


def as_line(column):
    return jnp.broadcast_to(column, (LANES, LANES)).T[0:1, :]


def to_lines(column, out, at):
    for i in range(column.shape[0] // LANES):
        out[at + i:at + i + 1, :] = as_line(column[i * LANES:(i + 1) * LANES, :])


def aims(me_ref, hid, local):
    model = hid[0].shape[1] - LANES
    apart, place = [], []
    for h in hid:
        code = h[:, model:model + LANES].astype(f32).astype(jnp.int32)
        goal = code[:, 0:1] * 256 + code[:, 1:2]
        owner = lax.div(goal, local)
        apart.append(jnp.bitwise_xor(owner, me_ref[0]))
        place.append(goal - owner * local)
    return jnp.concatenate(apart, axis=0), jnp.concatenate(place, axis=0)


def spots(apart, place, meta):
    bits, start = meta
    return jnp.where(apart == bits, place - start, -1)


def scores_of(rows, words, metas, apart, place, score, prob, hot):
    at, top, aim = 0, None, None
    for ref, meta in zip(words, metas):
        n = ref.shape[0]
        piece = lax.dot_general(rows[...], ref[...], (((1,), (1,)), ((), ())), preferred_element_type=f32)
        score[:, at:at + n] = piece
        hit = lax.broadcasted_iota(jnp.int32, piece.shape, 1) == spots(apart, place, meta)
        hot[:, at:at + n] = jnp.where(hit, 1.0, 0.0).astype(bf16)
        part = jnp.sum(jnp.where(hit, piece, 0.0), axis=1, keepdims=True)
        best = jnp.max(piece, axis=1, keepdims=True)
        top = best if top is None else jnp.maximum(top, best)
        aim = part if aim is None else aim + part
        at += n
    at, total = 0, None
    for ref in words:
        n = ref.shape[0]
        w = jnp.exp(score[:, at:at + n] - top).astype(bf16)
        prob[:, at:at + n] = w
        part = jnp.sum(w.astype(f32), axis=1, keepdims=True)
        total = part if total is None else total + part
        at += n
    return top, total, aim


def product(left, words, n, size):
    at, res = 0, None
    for ref in words:
        count = ref.shape[0]
        d = jnp.dot(left[:, at:at + count], ref[:, n:n + size], preferred_element_type=f32)
        res = d if res is None else res + d
        at += count
    return res


def pack(columns, out):
    lane = lax.broadcasted_iota(jnp.int32, out.shape, 1)
    res = jnp.zeros(out.shape, f32)
    for i, column in enumerate(columns):
        res = jnp.where(lane == i, column, res)
    out[...] = res


def load_rows(hid, rows):
    at = 0
    for h in hid:
        rows[at:at + h.shape[0], :] = h[:, 0:rows.shape[1]]
        at += h.shape[0]


def first_kernel(me_ref, *refs, nh, metas, local):
    hid, words = refs[:nh], refs[nh:nh + len(metas)]
    out, target, stats, rows, score, prob, hot = refs[nh + len(metas):]
    load_rows(hid, rows)
    each = scores_of(rows, words, metas, *aims(me_ref, hid, local), score, prob, hot)
    pack(each, stats)
    for n in range(0, out.shape[1], 256):
        out[:, n:n + 256] = product(prob, words, n, 256)
        target[:, n:n + 256] = product(hot, words, n, 256).astype(bf16)


def cost(flops, size, trans=0):
    return pl.CostEstimate(flops=flops, bytes_accessed=size, transcendentals=trans)


SM = pl.BlockSpec(memory_space=pltpu.SMEM)


def first_fold(me, hid, words, metas, local):
    model = words[0].shape[1]
    rows = sum(h.shape[0] for h in hid)
    count = sum(w.shape[0] for w in words)
    return pl.pallas_call(
        functools.partial(first_kernel, nh=len(hid), metas=metas, local=local),
        out_shape=[jax.ShapeDtypeStruct((rows, model), f32), jax.ShapeDtypeStruct((rows, model), bf16),
                   jax.ShapeDtypeStruct((rows, LANES), f32)],
        in_specs=[SM] + [VM] * (len(hid) + len(words)), out_specs=[VM] * 3,
        scratch_shapes=[pltpu.VMEM((rows, model), bf16), pltpu.VMEM((rows, count), f32),
                        pltpu.VMEM((rows, count), bf16), pltpu.VMEM((rows, count), bf16)],
        compiler_params=params(), cost_estimate=cost(6 * rows * count * model, 2 * (rows + count) * model),
        name="first_fold",
    )(me, *hid, *words)


def last_kernel(me_ref, *refs, nh, metas, group, local):
    hid, words = refs[:nh], refs[nh:nh + len(metas)]
    stats, prob, hot, facts, lines, rows, score = refs[nh + len(metas):]
    load_rows(hid, rows)
    count, model = rows.shape
    apart, place = aims(me_ref, hid, local)
    top2, total2, aim2 = scores_of(rows, words, metas, apart, place, score, prob, hot)
    top1, total1, aim1 = (stats[:, i:i + 1] for i in range(3))
    top = jnp.maximum(top1, top2)
    total = jnp.exp(top1 - top) * total1 + jnp.exp(top2 - top) * total2
    inside = sum(jnp.where(apart == bits, 1.0, 0.0) for bits in group)
    pack((top2, inside), facts)
    per = count // LANES
    to_lines(top + jnp.log(total), lines, 0)
    to_lines(aim1 + aim2, lines, per)
    centre = jnp.sum(words[0][0:LANES, :].astype(f32), axis=0, keepdims=True) * (1.0 / LANES)
    for n in range(model // LANES):
        lines[2 * per + n:2 * per + n + 1, :] = centre[:, n * LANES:(n + 1) * LANES]


def last_scores(me, hid, words, metas, group, local, stats):
    model = words[0].shape[1]
    rows = stats.shape[0]
    count = sum(w.shape[0] for w in words)
    return pl.pallas_call(
        functools.partial(last_kernel, nh=len(hid), metas=metas, group=group, local=local),
        out_shape=[jax.ShapeDtypeStruct((rows, count), bf16)] * 2 + [
            jax.ShapeDtypeStruct((rows, LANES), f32),
            jax.ShapeDtypeStruct((2 * rows // LANES + model // LANES, LANES), f32)],
        in_specs=[SM] + [VM] * (len(hid) + len(words) + 1), out_specs=[VM] * 4,
        scratch_shapes=[pltpu.VMEM((rows, model), bf16), pltpu.VMEM((rows, count), f32)],
        compiler_params=params(), cost_estimate=cost(2 * rows * count * model, 2 * (rows + count) * model),
        name="last_scores",
    )(me, *hid, *words, stats)


def close_kernel(*refs, flips, nw):
    nl = len(flips)
    lines, words, rest = refs[:4], refs[4:4 + nw], refs[4 + nw:]
    prob, hot, one, before, stats, facts = rest[:6]
    parts, loss = rest[6:10], rest[10]
    size = lines[0].shape[0] * 4 // nl
    count, model = one.shape
    per = count // LANES
    quarter = count // 4

    def line(j, i, kind):
        over, halves = flips[j]
        at = j % (nl // 4) * size + kind * per + (i ^ over)
        v = lines[j // (nl // 4)][at:at + 1, :]
        return pltpu.roll(v, LANES // 2, axis=1) if halves else v

    scales = []
    for i in range(per):
        each = [line(j, i, 0) for j in range(nl)]
        top = functools.reduce(jnp.maximum, each)
        whole = top + jnp.log(sum(jnp.exp(v - top) for v in each))
        if i == 0:
            loss[...] = whole - sum(line(j, i, 1) for j in range(nl))
        weight = jnp.broadcast_to(jnp.exp(each[0] - whole), (LANES, LANES)).T
        whole = jnp.broadcast_to(whole, (LANES, LANES)).T
        part = slice(i * LANES, (i + 1) * LANES)
        scales.append((jnp.exp(stats[part, 0:1] - whole[:, 0:1]), jnp.exp(facts[part, 0:1] - whole[:, 0:1]),
                       facts[part, 1:2] - weight[:, 0:1]))
    c1, c2, c3 = (jnp.concatenate(c, axis=0) for c in zip(*scales))
    for n in range(0, model, 256):
        cols = slice(n, n + 256)
        mu = jnp.concatenate([
            sum(ref[at + 2 * per + m // LANES:at + 2 * per + m // LANES + 1, :]
                for ref in lines for at in range(0, ref.shape[0], size)) * (1.0 / nl)
            for m in range(n, n + 256, LANES)], axis=1)
        goal = product(hot, words, n, 256) + before[:, cols].astype(f32)
        mix = (c1 * one[:, cols] + c2 * product(prob, words, n, 256) + (c3 * mu - goal)).astype(bf16)
        for q in range(4):
            parts[q][:, cols] = mix[q * quarter:(q + 1) * quarter]


def close(lines, flips, words, prob, hot, one, before, stats, facts):
    rows, model = one.shape
    side = jax.ShapeDtypeStruct((rows // 4, model), bf16)
    return pl.pallas_call(
        functools.partial(close_kernel, flips=flips, nw=len(words)),
        out_shape=[side] * 4 + [jax.ShapeDtypeStruct((1, LANES), f32)],
        in_specs=[VM] * (len(lines) + len(words) + 6), out_specs=[VM] * 5, compiler_params=params(),
        cost_estimate=cost(4 * rows * prob.shape[1] * model, 8 * rows * model), name="close",
    )(*lines, *words, prob, hot, one, before, stats, facts)


def plus(a, b):
    return (a.astype(f32) + b.astype(f32)).astype(bf16)


def add_kernel(*refs):
    n = len(refs) // 4
    for i in range(n):
        keep, got = refs[2 * i:2 * i + 2]
        first, second = refs[2 * n + 2 * i:2 * n + 2 * i + 2]
        rows = first.shape[0]
        first[...] = plus(keep[0:rows, :], got[0:rows, :])
        second[...] = plus(keep[rows:2 * rows, :], got[rows:2 * rows, :])


def add_halves(*pairs):
    outs = [jax.ShapeDtypeStruct((p.shape[0] // 2, p.shape[1]), bf16) for p in pairs]
    return pl.pallas_call(
        add_kernel, out_shape=outs, in_specs=[VM] * len(pairs), out_specs=[VM] * len(pairs),
        compiler_params=params(), cost_estimate=cost(pairs[0].size, 8 * pairs[0].size), name="add_halves",
    )(*pairs)


def add_four_kernel(*refs):
    parts, halves = refs[:4], refs[4:]
    rows = halves[0].shape[0]
    for i, out in enumerate(halves):
        part = slice(i * rows, (i + 1) * rows)
        out[...] = sum(ref[part, :].astype(f32) for ref in parts).astype(bf16)


def add_four(*parts):
    rows, model = parts[0].shape
    return pl.pallas_call(
        add_four_kernel, out_shape=[jax.ShapeDtypeStruct((rows // 2, model), bf16)] * 2,
        in_specs=[VM] * 4, out_specs=[VM] * 2,
        compiler_params=params(), cost_estimate=cost(4 * rows * model, 10 * rows * model), name="add_four",
    )(*parts)


def per_device(char_ids, char_table, conv_weight, proj_weight, gate_weight, trans_weight, gate_bias, hidden, targets,
               *, vocab, blk):
    devices = vocab * blk
    axes = ("vocab", "blk")

    def swap(x, bits):
        return lax.ppermute(x, axes, [(i, i ^ bits) for i in range(devices)])

    core, near = blk, 1
    bit_a, bit_b = 2 * blk, 4 * blk
    rest = [1 << i for i in range(1, blk.bit_length() - 1)] + [
        blk << i for i in range(3, vocab.bit_length() - 1)]
    me = lax.axis_index("vocab") * blk + lax.axis_index("blk")
    local, length = char_ids.shape
    mine = hidden.shape[0]

    rows, goal = hidden, targets.reshape(1, mine)
    for bit in rest:
        rows = jnp.concatenate([rows, swap(rows, bit)], axis=0)
        goal = jnp.concatenate([goal, swap(goal, bit)], axis=1)
    weights = (char_table.T, conv_weight, proj_weight, gate_weight, trans_weight, gate_bias)
    many = 4 * (mine << len(rest)) > local
    size = local // 2
    marks = (0, size)
    ids = char_ids.T
    e0 = embed(ids, length, 0, size, *weights)
    e0, rows, goal = lax.optimization_barrier((e0, rows, goal))
    goal = goal.reshape(-1, 1)
    code = jnp.concatenate([goal // 256, goal % 256], axis=1).astype(bf16)
    rows = jnp.concatenate([rows, jnp.pad(code, ((0, 0), (0, LANES - 2)))], axis=1)
    hid = [rows] + [swap(rows, b) for b in (bit_b, bit_a, bit_a | bit_b)]
    e1 = embed(ids, length, size, local - size, *weights)
    held, *hid = lax.optimization_barrier((e1, *hid))
    pieces = [e0, held]
    cores = [swap(e, core) for e in pieces]
    nears = [swap(e, near) for e in pieces]
    held, nears[0] = lax.optimization_barrier((held, nears[0]))
    far = swap(nears[0], core)

    me = me.astype(jnp.int32).reshape(1)
    meta = [tuple((bits, m) for m in marks) for bits in (0, core, near, core | near)]
    early = [(nears[0], meta[2][0]), (far, meta[3][0])]
    late = []
    if many:
        early, late = [], early
    words = pieces + cores + [w for w, _ in early]
    one, target, stats = first_fold(me, hid, words, meta[0] + meta[1] + tuple(m for _, m in early), local)
    held, stats = lax.optimization_barrier((nears[1], stats))
    late += [(held, meta[2][1]), (swap(held, core), meta[3][1])]
    words, metas = [w for w, _ in late], tuple(m for _, m in late)
    prob, hot, facts, line = last_scores(
        me, hid, words, metas, (0, core, near, core | near), local, stats)
    lines, others = line, [0]
    for bit in rest:
        lines = jnp.concatenate([lines, swap(lines, bit)], axis=0)
        others += [o | bit for o in others]
    plane = (bit_b, bit_a, bit_a | bit_b)
    lines = [lines] + [swap(lines, o) for o in plane]
    others = [o | p for p in (0,) + plane for o in others]
    order = rest + [bit_b, bit_a]
    flips = tuple((sum(1 << (j - 1) for j, b in enumerate(order) if j and o & b), bool(o & rest[0])) for o in others)
    *parts, loss = close(lines, flips, words, prob, hot, one, target, stats, facts)
    far_part = swap(parts[3], bit_a | bit_b)
    keep, send = add_four(parts[0], swap(parts[1], bit_b), swap(parts[2], bit_a), far_part)
    for bit in rest[:0:-1]:
        keep, send = add_halves(keep, swap(send, bit))
    grad = plus(keep, swap(send, rest[0]))
    return loss[0, :mine], grad


def solution(mesh):
    words = P(("vocab", "blk"))
    return jax.shard_map(
        functools.partial(per_device, vocab=mesh.shape["vocab"], blk=mesh.shape["blk"]),
        mesh=mesh,
        in_specs=(P(("vocab", "blk"), None), P(), P(), P(), P(), P(), P(), P(("vocab", "blk"), None), words),
        out_specs=(words, P(("vocab", "blk"), None)),
        check_vma=False,
    )
```

```python
import functools
import jax
import jax.numpy as jnp
from jax import lax
from jax.experimental import pallas as pl
from jax.experimental.pallas import tpu as pltpu
from jax.sharding import PartitionSpec as P

bf16=jnp.bfloat16; f32=jnp.float32
LANES = 128
SPAN = 8


def prep_toeplitz(conv_ref, toep, ce, k, filters):
    depth = toep.shape[0]
    rows = (k + 1) * ce
    piece = conv_ref[0:rows, k * filters:(k + 1) * filters]
    for o in range(SPAN):
        cols = slice((k * SPAN + o) * filters, (k * SPAN + o + 1) * filters)
        if o:
            toep[0:o * ce, cols] = jnp.zeros((o * ce, filters), bf16)
        toep[o * ce:o * ce + rows, cols] = piece
        rest = depth - o * ce - rows
        if rest:
            toep[o * ce + rows:depth, cols] = jnp.zeros((rest, filters), bf16)


def lookup(ids_ref, start, words, tab_ref, vec, length, ce, g):
    per = LANES // ce
    low_tab = tab_ref[:, 0:LANES].astype(f32)
    top_tab = tab_ref[:, LANES:2 * LANES].astype(f32)
    first = start // LANES * LANES
    for tile in range(first, start + words, LANES):
        low_word, high_word = max(tile, start), min(tile + LANES, start + words)
        parts = []
        for p in range(g * per, (g + 1) * per):
            if p >= length:
                parts.append(jnp.zeros((ce, LANES), f32))
                continue
            idx = jnp.broadcast_to(ids_ref[p:p + 1, tile:tile + LANES], (8, LANES))
            low = jnp.bitwise_and(idx, LANES - 1)
            top = idx >= LANES
            for h in range(0, ce, 8):
                one = jnp.take_along_axis(low_tab[h:h + 8], low, axis=1)
                two = jnp.take_along_axis(top_tab[h:h + 8], low, axis=1)
                parts.append(jnp.where(top, two, one))
        block = jnp.concatenate(parts, axis=0).T.astype(bf16)
        vec[low_word - start:high_word - start, g * LANES:(g + 1) * LANES] = block[low_word - tile:high_word - tile]


def conv_pool(vec, toep, acc, length, widths, filters, look, build):
    ce = toep.shape[0] // (2 * SPAN)

    def tile(k, o, lhs):
        cols = slice((k * SPAN + o) * filters, (k * SPAN + o + 2) * filters)
        depth = LANES if (o + k + 2) * ce <= LANES else 2 * LANES
        return jnp.dot(lhs[:, 0:depth], toep[0:depth, cols], preferred_element_type=f32)
    acc[...] = jnp.full(acc.shape, -jnp.inf, f32)
    look(0)
    for b in range(-(-length // SPAN)):
        look(b + 1)
        lhs = vec[:, b * LANES:(b + 2) * LANES]
        for k in range(widths):
            usable = min(SPAN, length - k - b * SPAN)
            if usable <= 0:
                continue
            if b == 0:
                build(k)
            best = acc[:, k * filters:(k + 1) * filters]
            for o in range(0, usable, 2):
                r = tile(k, o, lhs)
                best = jnp.maximum(best, r[:, :filters])
                if o + 1 < usable:
                    best = jnp.maximum(best, r[:, filters:])
            acc[:, k * filters:(k + 1) * filters] = best


def cnn_kernel(ids_ref, tab_ref, conv_ref, bias_ref, proj_hbm, gate_hbm, trans_hbm, *rest,
               widths, filters, ce, length, layers, nt, start):
    out_ref, vec, toep, acc, feat, proj, gate, trans, state, last, sems = rest
    copies = [pltpu.make_async_copy(s, d, sems.at[i]) for i, (s, d) in enumerate(
        ((proj_hbm, proj), (gate_hbm, gate), (trans_hbm, trans)))]
    for c in copies:
        c.start()
    words = out_ref.shape[0]
    conv_pool(
        vec, toep, acc, length, widths, filters,
        lambda g: lookup(ids_ref, start, words, tab_ref, vec, length, ce, g),
        lambda k: prep_toeplitz(conv_ref, toep, ce, k, filters))
    for c in copies:
        c.wait()
    feat[...] = jnp.tanh(acc[...]).astype(bf16)
    model = last.shape[1]
    for n in range(0, model, nt):
        state[:, n:n + nt] = jnp.dot(feat[...], proj[:, n:n + nt], preferred_element_type=f32).astype(bf16)
    for l in range(layers):
        for n in range(0, model, nt):
            cur = state[...]
            g = jnp.dot(cur, gate[l, :, n:n + nt], preferred_element_type=f32) + bias_ref[l:l + 1, n:n + nt]
            t = jnp.dot(cur, trans[l, :, n:n + nt], preferred_element_type=f32)
            opened = jax.nn.sigmoid(g)
            carried = jnp.maximum(t, 0.0)
            new = (opened * carried + (1.0 - opened) * state[:, n:n + nt].astype(f32)).astype(bf16)
            if l + 1 < layers:
                last[:, n:n + nt] = new
            else:
                out_ref[:, n:n + nt] = new
        if l + 1 < layers:
            state[...] = last[...]


ANY = pl.BlockSpec(memory_space=pl.ANY)
VM = pl.BlockSpec(memory_space=pltpu.VMEM)


def params(limit_mib=56):
    return pltpu.CompilerParams(vmem_limit_bytes=limit_mib << 20)


def embed(ids, length, start, words, tab_t, conv_weight, proj_weight, gate_weight, trans_weight, gate_bias, nt=256):
    ce = tab_t.shape[0]
    widths = conv_weight.shape[0] // ce
    filters = conv_weight.shape[1] // widths
    layers, model, _ = gate_weight.shape
    flops = 2 * words * (length * 256 * widths * filters + widths * filters * model + 2 * layers * model * model)
    return pl.pallas_call(
        functools.partial(cnn_kernel, widths=widths, filters=filters, ce=ce, length=length, layers=layers, nt=nt,
                          start=start),
        out_shape=jax.ShapeDtypeStruct((words, model), bf16),
        in_specs=[VM, VM, VM, VM, ANY, ANY, ANY],
        out_specs=VM,
        scratch_shapes=[
            pltpu.VMEM((words, (-(-length // SPAN) + 1) * LANES), bf16),
            pltpu.VMEM((2 * LANES, widths * SPAN * filters), bf16),
            pltpu.VMEM((words, widths * filters), f32),
            pltpu.VMEM((words, widths * filters), bf16),
            pltpu.VMEM(proj_weight.shape, bf16),
            pltpu.VMEM(gate_weight.shape, bf16),
            pltpu.VMEM(trans_weight.shape, bf16),
            pltpu.VMEM((words, model), bf16),
            pltpu.VMEM((words, model), bf16),
            pltpu.SemaphoreType.DMA((3,)),
        ],
        compiler_params=params(),
        cost_estimate=pl.CostEstimate(flops=flops, bytes_accessed=12 << 20, transcendentals=words * 4096),
        name="embed",
    )(ids, tab_t, conv_weight, gate_bias, proj_weight, gate_weight, trans_weight)


def as_line(column):
    return jnp.broadcast_to(column, (LANES, LANES)).T[0:1, :]


def to_lines(column, out, at):
    for i in range(column.shape[0] // LANES):
        out[at + i:at + i + 1, :] = as_line(column[i * LANES:(i + 1) * LANES, :])


def aims(me_ref, hid, local):
    model = hid[0].shape[1] - LANES
    apart, place = [], []
    for h in hid:
        code = h[:, model:model + LANES].astype(f32).astype(jnp.int32)
        goal = code[:, 0:1] * 256 + code[:, 1:2]
        owner = lax.div(goal, local)
        apart.append(jnp.bitwise_xor(owner, me_ref[0]))
        place.append(goal - owner * local)
    return jnp.concatenate(apart, axis=0), jnp.concatenate(place, axis=0)


def spots(apart, place, meta):
    bits, start = meta
    return jnp.where(apart == bits, place - start, -1)


def scores_of(rows, words, metas, apart, place, score, prob, hot):
    at, top, aim = 0, None, None
    for ref, meta in zip(words, metas):
        n = ref.shape[0]
        piece = lax.dot_general(rows[...], ref[...], (((1,), (1,)), ((), ())), preferred_element_type=f32)
        score[:, at:at + n] = piece
        hit = lax.broadcasted_iota(jnp.int32, piece.shape, 1) == spots(apart, place, meta)
        hot[:, at:at + n] = jnp.where(hit, 1.0, 0.0).astype(bf16)
        part = jnp.sum(jnp.where(hit, piece, 0.0), axis=1, keepdims=True)
        best = jnp.max(piece, axis=1, keepdims=True)
        top = best if top is None else jnp.maximum(top, best)
        aim = part if aim is None else aim + part
        at += n
    at, total = 0, None
    for ref in words:
        n = ref.shape[0]
        w = jnp.exp(score[:, at:at + n] - top).astype(bf16)
        prob[:, at:at + n] = w
        part = jnp.sum(w.astype(f32), axis=1, keepdims=True)
        total = part if total is None else total + part
        at += n
    return top, total, aim


def product(left, words, n, size):
    at, res = 0, None
    for ref in words:
        count = ref.shape[0]
        d = jnp.dot(left[:, at:at + count], ref[:, n:n + size], preferred_element_type=f32)
        res = d if res is None else res + d
        at += count
    return res


def pack(columns, out):
    lane = lax.broadcasted_iota(jnp.int32, out.shape, 1)
    res = jnp.zeros(out.shape, f32)
    for i, column in enumerate(columns):
        res = jnp.where(lane == i, column, res)
    out[...] = res


def load_rows(hid, rows):
    at = 0
    for h in hid:
        rows[at:at + h.shape[0], :] = h[:, 0:rows.shape[1]]
        at += h.shape[0]


def first_kernel(me_ref, *refs, nh, metas, local):
    hid, words = refs[:nh], refs[nh:nh + len(metas)]
    out, target, stats, rows, score, prob, hot = refs[nh + len(metas):]
    load_rows(hid, rows)
    each = scores_of(rows, words, metas, *aims(me_ref, hid, local), score, prob, hot)
    pack(each, stats)
    for n in range(0, out.shape[1], 256):
        out[:, n:n + 256] = product(prob, words, n, 256)
        target[:, n:n + 256] = product(hot, words, n, 256).astype(bf16)


def cost(flops, size, trans=0):
    return pl.CostEstimate(flops=flops, bytes_accessed=size, transcendentals=trans)


SM = pl.BlockSpec(memory_space=pltpu.SMEM)


def first_fold(me, hid, words, metas, local):
    model = words[0].shape[1]
    rows = sum(h.shape[0] for h in hid)
    count = sum(w.shape[0] for w in words)
    return pl.pallas_call(
        functools.partial(first_kernel, nh=len(hid), metas=metas, local=local),
        out_shape=[jax.ShapeDtypeStruct((rows, model), f32), jax.ShapeDtypeStruct((rows, model), bf16),
                   jax.ShapeDtypeStruct((rows, LANES), f32)],
        in_specs=[SM] + [VM] * (len(hid) + len(words)), out_specs=[VM] * 3,
        scratch_shapes=[pltpu.VMEM((rows, model), bf16), pltpu.VMEM((rows, count), f32),
                        pltpu.VMEM((rows, count), bf16), pltpu.VMEM((rows, count), bf16)],
        compiler_params=params(), cost_estimate=cost(6 * rows * count * model, 2 * (rows + count) * model),
        name="first_fold",
    )(me, *hid, *words)


def last_kernel(me_ref, *refs, nh, metas, group, local):
    hid, words = refs[:nh], refs[nh:nh + len(metas)]
    stats, prob, hot, facts, lines, rows, score = refs[nh + len(metas):]
    load_rows(hid, rows)
    count, model = rows.shape
    apart, place = aims(me_ref, hid, local)
    top2, total2, aim2 = scores_of(rows, words, metas, apart, place, score, prob, hot)
    top1, total1, aim1 = (stats[:, i:i + 1] for i in range(3))
    top = jnp.maximum(top1, top2)
    total = jnp.exp(top1 - top) * total1 + jnp.exp(top2 - top) * total2
    inside = sum(jnp.where(apart == bits, 1.0, 0.0) for bits in group)
    pack((top2, inside), facts)
    per = count // LANES
    to_lines(top + jnp.log(total), lines, 0)
    to_lines(aim1 + aim2, lines, per)
    centre = jnp.sum(words[0][0:LANES, :].astype(f32), axis=0, keepdims=True) * (1.0 / LANES)
    for n in range(model // LANES):
        lines[2 * per + n:2 * per + n + 1, :] = centre[:, n * LANES:(n + 1) * LANES]


def last_scores(me, hid, words, metas, group, local, stats):
    model = words[0].shape[1]
    rows = stats.shape[0]
    count = sum(w.shape[0] for w in words)
    return pl.pallas_call(
        functools.partial(last_kernel, nh=len(hid), metas=metas, group=group, local=local),
        out_shape=[jax.ShapeDtypeStruct((rows, count), bf16)] * 2 + [
            jax.ShapeDtypeStruct((rows, LANES), f32),
            jax.ShapeDtypeStruct((2 * rows // LANES + model // LANES, LANES), f32)],
        in_specs=[SM] + [VM] * (len(hid) + len(words) + 1), out_specs=[VM] * 4,
        scratch_shapes=[pltpu.VMEM((rows, model), bf16), pltpu.VMEM((rows, count), f32)],
        compiler_params=params(), cost_estimate=cost(2 * rows * count * model, 2 * (rows + count) * model),
        name="last_scores",
    )(me, *hid, *words, stats)


def close_kernel(*refs, flips, nw):
    nl = len(flips)
    lines, words, rest = refs[:nl], refs[nl:nl + nw], refs[nl + nw:]
    prob, hot, one, before, stats, facts = rest[:6]
    parts, loss = rest[6:10], rest[10]
    count, model = one.shape
    per = count // LANES
    quarter = count // 4

    def line(j, i, kind):
        over, halves = flips[j]
        at = kind * per + (i ^ over)
        v = lines[j][at:at + 1, :]
        return pltpu.roll(v, LANES // 2, axis=1) if halves else v

    scales = []
    for i in range(per):
        each = [line(j, i, 0) for j in range(nl)]
        top = functools.reduce(jnp.maximum, each)
        whole = top + jnp.log(sum(jnp.exp(v - top) for v in each))
        if i == 0:
            loss[...] = whole - sum(line(j, i, 1) for j in range(nl))
        weight = jnp.broadcast_to(jnp.exp(each[0] - whole), (LANES, LANES)).T
        whole = jnp.broadcast_to(whole, (LANES, LANES)).T
        part = slice(i * LANES, (i + 1) * LANES)
        scales.append((jnp.exp(stats[part, 0:1] - whole[:, 0:1]), jnp.exp(facts[part, 0:1] - whole[:, 0:1]),
                       facts[part, 1:2] - weight[:, 0:1]))
    c1, c2, c3 = (jnp.concatenate(c, axis=0) for c in zip(*scales))
    for n in range(0, model, 256):
        cols = slice(n, n + 256)
        mu = jnp.concatenate([
            sum(ref[2 * per + m // LANES:2 * per + m // LANES + 1, :] for ref in lines) * (1.0 / nl)
            for m in range(n, n + 256, LANES)], axis=1)
        goal = product(hot, words, n, 256) + before[:, cols].astype(f32)
        mix = (c1 * one[:, cols] + c2 * product(prob, words, n, 256) + (c3 * mu - goal)).astype(bf16)
        for q in range(4):
            parts[q][:, cols] = mix[q * quarter:(q + 1) * quarter]


def close(lines, flips, words, prob, hot, one, before, stats, facts):
    rows, model = one.shape
    side = jax.ShapeDtypeStruct((rows // 4, model), bf16)
    return pl.pallas_call(
        functools.partial(close_kernel, flips=flips, nw=len(words)),
        out_shape=[side] * 4 + [jax.ShapeDtypeStruct((1, LANES), f32)],
        in_specs=[VM] * (len(lines) + len(words) + 6), out_specs=[VM] * 5, compiler_params=params(),
        cost_estimate=cost(4 * rows * prob.shape[1] * model, 8 * rows * model), name="close",
    )(*lines, *words, prob, hot, one, before, stats, facts)


def plus(a, b):
    return (a.astype(f32) + b.astype(f32)).astype(bf16)


def add_kernel(*refs):
    n = len(refs) // 4
    for i in range(n):
        keep, got = refs[2 * i:2 * i + 2]
        first, second = refs[2 * n + 2 * i:2 * n + 2 * i + 2]
        rows = first.shape[0]
        first[...] = plus(keep[0:rows, :], got[0:rows, :])
        second[...] = plus(keep[rows:2 * rows, :], got[rows:2 * rows, :])


def add_halves(*pairs):
    outs = [jax.ShapeDtypeStruct((p.shape[0] // 2, p.shape[1]), bf16) for p in pairs]
    return pl.pallas_call(
        add_kernel, out_shape=outs, in_specs=[VM] * len(pairs), out_specs=[VM] * len(pairs),
        compiler_params=params(), cost_estimate=cost(pairs[0].size, 8 * pairs[0].size), name="add_halves",
    )(*pairs)


def add_four_kernel(*refs):
    parts, halves = refs[:4], refs[4:]
    rows = halves[0].shape[0]
    for i, out in enumerate(halves):
        part = slice(i * rows, (i + 1) * rows)
        out[...] = sum(ref[part, :].astype(f32) for ref in parts).astype(bf16)


def add_four(*parts):
    rows, model = parts[0].shape
    return pl.pallas_call(
        add_four_kernel, out_shape=[jax.ShapeDtypeStruct((rows // 2, model), bf16)] * 2,
        in_specs=[VM] * 4, out_specs=[VM] * 2,
        compiler_params=params(), cost_estimate=cost(4 * rows * model, 10 * rows * model), name="add_four",
    )(*parts)


def per_device(char_ids, char_table, conv_weight, proj_weight, gate_weight, trans_weight, gate_bias, hidden, targets,
               *, vocab, blk):
    devices = vocab * blk
    axes = ("vocab", "blk")

    def swap(x, bits):
        return lax.ppermute(x, axes, [(i, i ^ bits) for i in range(devices)])

    core, near = blk, 1
    bit_a, bit_b = 2 * blk, 4 * blk
    rest = [1 << i for i in range(1, blk.bit_length() - 1)] + [
        blk << i for i in range(3, vocab.bit_length() - 1)]
    me = lax.axis_index("vocab") * blk + lax.axis_index("blk")
    local, length = char_ids.shape
    mine = hidden.shape[0]

    rows, goal = hidden, targets.reshape(1, mine)
    for bit in rest:
        rows = jnp.concatenate([rows, swap(rows, bit)], axis=0)
        goal = jnp.concatenate([goal, swap(goal, bit)], axis=1)
    weights = (char_table.T, conv_weight, proj_weight, gate_weight, trans_weight, gate_bias)
    many = 4 * (mine << len(rest)) > local
    size = local // 2
    marks = (0, size)
    ids = char_ids.T
    e0 = embed(ids, length, 0, size, *weights)
    e0, rows, goal = lax.optimization_barrier((e0, rows, goal))
    goal = goal.reshape(-1, 1)
    code = jnp.concatenate([goal // 256, goal % 256], axis=1).astype(bf16)
    rows = jnp.concatenate([rows, jnp.pad(code, ((0, 0), (0, LANES - 2)))], axis=1)
    hid = [rows] + [swap(rows, b) for b in (bit_b, bit_a, bit_a | bit_b)]
    e1 = embed(ids, length, size, local - size, *weights)
    held, *hid = lax.optimization_barrier((e1, *hid))
    pieces = [e0, held]
    cores = [swap(e, core) for e in pieces]
    nears = [swap(e, near) for e in pieces]
    held, nears[0] = lax.optimization_barrier((held, nears[0]))
    far = swap(nears[0], core)

    me = me.astype(jnp.int32).reshape(1)
    meta = [tuple((bits, m) for m in marks) for bits in (0, core, near, core | near)]
    early = [(nears[0], meta[2][0]), (far, meta[3][0])]
    late = []
    if many:
        early, late = [], early
    words = pieces + cores + [w for w, _ in early]
    one, target, stats = first_fold(me, hid, words, meta[0] + meta[1] + tuple(m for _, m in early), local)
    held, stats = lax.optimization_barrier((nears[1], stats))
    late += [(held, meta[2][1]), (swap(held, core), meta[3][1])]
    words, metas = [w for w, _ in late], tuple(m for _, m in late)
    prob, hot, facts, line = last_scores(
        me, hid, words, metas, (0, core, near, core | near), local, stats)
    lines, others = [line], [0]
    for bit in rest:
        lines += [swap(v, bit) for v in lines]
        others += [o | bit for o in others]
    plane = (bit_b, bit_a, bit_a | bit_b)
    lines += [swap(v, o) for o in plane for v in lines]
    others = [o | p for p in (0,) + plane for o in others]
    order = rest + [bit_b, bit_a]
    flips = tuple((sum(1 << (j - 1) for j, b in enumerate(order) if j and o & b), bool(o & rest[0])) for o in others)
    *parts, loss = close(lines, flips, words, prob, hot, one, target, stats, facts)
    far_part = swap(parts[3], bit_a | bit_b)
    keep, send = add_four(parts[0], swap(parts[1], bit_b), swap(parts[2], bit_a), far_part)
    for bit in rest[:0:-1]:
        keep, send = add_halves(keep, swap(send, bit))
    grad = plus(keep, swap(send, rest[0]))
    return loss[0, :mine], grad


def solution(mesh):
    words = P(("vocab", "blk"))
    return jax.shard_map(
        functools.partial(per_device, vocab=mesh.shape["vocab"], blk=mesh.shape["blk"]),
        mesh=mesh,
        in_specs=(P(("vocab", "blk"), None), P(), P(), P(), P(), P(), P(), P(("vocab", "blk"), None), words),
        out_specs=(words, P(("vocab", "blk"), None)),
        check_vma=False,
    )
```
